256 devices in a mesh: gx: 4 (over y), gy: 8 (over x, core), gz: 8 (over z).
Axes of the slice: x: 4, y: 4, z: 8, core: 2. Of those that a mesh axis runs over, the one named last changes fastest.
Arguments:
- right_side: float32 [32, 256, 1024], P('gx', 'gy', 'gz'), may hold values from -8 to 8
- alpha_coef: float32 [32, 256, 1024], P('gx', 'gy', 'gz'), may hold values from 0.25 to 4
- beta_coef: float32 [32, 256, 1024], P('gx', 'gy', 'gz'), may hold values from 0.25 to 4
Outputs:
- solution_field: float32 [32, 256, 1024], P('gx', 'gy', 'gz')
- residual_field: float32 [32, 256, 1024], P('gx', 'gy', 'gz')
The draws below stay inside these ranges and needn't reach their ends.
All inputs are finite; a program needn't handle non-finite values.
Results may differ from the reference program's by a relative error of at most 0.0003.
Values sent between devices are 32-bit elements; how exact they have to be, the bound alone decides.
A program may use at most 64 MiB of HBM per device.

```python
import math
import jax
import jax.numpy as jnp

LEVELS = 3
SWEEPS = 4
BOTTOM = 12
NX = 32
NY = 256
NZ = 1024


def levels(stream_key, shape, split, least, top_value):
    def one(position, blocks):
        draws = jax.random.uniform(jax.random.fold_in(jax.random.fold_in(stream_key, 6), position), (blocks,), jnp.float32, least / len(split), top_value / len(split))
        return jnp.repeat(jnp.exp(draws), shape[position] // blocks).reshape((-1,) + (1,) * (len(shape) - position - 1))

    loudness = one(*split[0])
    for cut in split[1:]:
        loudness = loudness * one(*cut)
    return loudness


def scatter_about(own_key, dims, deviation, bound, split=(), dtype=jnp.bfloat16):
    result = jax.random.normal(own_key, dims, jnp.float32) * deviation
    if len(split) > 0:
        result = levels(own_key, dims, split, -0.22, 0.18) * result
    return jnp.clip(result, min=-bound, max=bound).astype(dtype)


def setup_inputs(seed: int = 0) -> dict:
    seeds = jax.random.split(jax.random.key(seed), 4)
    right_side = scatter_about(seeds[0], (NX, NY, NZ), 1.0, 8.0, ((0, 4), (1, 8), (2, 8)), jnp.float32)
    alpha_coef = jnp.clip(jnp.exp(math.log(4.0) - 2.7725887 * jax.random.uniform(seeds[1], (NX, NY, NZ), jnp.float32) ** levels(seeds[1], (NX, NY, NZ), ((0, 4), (1, 8), (2, 8)), -0.2, 0.2)), 0.25, 4.0)
    beta_coef = jnp.clip(jnp.exp(math.log(4.0) - 2.7725887 * jax.random.uniform(seeds[2], (NX, NY, NZ), jnp.float32) ** levels(seeds[2], (NX, NY, NZ), ((0, 4), (1, 8), (2, 8)), -0.2, 0.2)), 0.25, 4.0)
    return dict(right_side=right_side, alpha_coef=alpha_coef, beta_coef=beta_coef)


SHIFT_BASE = 0.01
UPPER_EIG = 2.0
SMOOTH_LOWER = 0.25
BOTTOM_LOWER = 0.02


def split_padded(padded):
    return (padded[:-2, 1:-1, 1:-1], padded[2:, 1:-1, 1:-1],
            padded[1:-1, :-2, 1:-1], padded[1:-1, 2:, 1:-1],
            padded[1:-1, 1:-1, :-2], padded[1:-1, 1:-1, 2:])


def zero_pad(field):
    return jnp.pad(field, 1)


def level_operator(beta_level, alpha_level, padded_beta, shift):
    coeffs = tuple(0.5 * (beta_level + other) for other in split_padded(padded_beta))
    diagonal = shift * alpha_level
    for coeff in coeffs:
        diagonal = diagonal + coeff
    return coeffs, diagonal


def apply_operator(field, operator, pad_field):
    coeffs, diagonal = operator
    others = split_padded(pad_field(field))
    total = coeffs[0] * others[0]
    for index in range(1, 6):
        total = total + coeffs[index] * others[index]
    return diagonal * field - total


def chebyshev(iterate, rhs_level, operator, count, lower, zero_start, pad_field):
    diagonal = operator[1]
    center = (UPPER_EIG + lower) / 2.0
    half_width = (UPPER_EIG - lower) / 2.0
    sigma_ratio = center / half_width
    rho_old = 1.0 / sigma_ratio
    if zero_start:
        remain = rhs_level
    else:
        remain = rhs_level - apply_operator(iterate, operator, pad_field)
    update = remain / diagonal / center
    iterate = iterate + update
    for sweep_index in range(count - 1):
        remain = rhs_level - apply_operator(iterate, operator, pad_field)
        rho_new = 1.0 / (2.0 * sigma_ratio - rho_old)
        update = (rho_new * rho_old) * update + (2.0 * rho_new / half_width) * (remain / diagonal)
        iterate = iterate + update
        rho_old = rho_new
    return iterate


def restrict_mean(field):
    first, second, third = field.shape
    blocks = field.reshape(first // 2, 2, second // 2, 2, third // 2, 2)
    return jnp.sum(blocks, axis=(1, 3, 5)) * 0.125


def prolong_copy(field):
    return jnp.repeat(jnp.repeat(jnp.repeat(field, 2, axis=0), 2, axis=1), 2, axis=2)


def reference(right_side, alpha_coef, beta_coef):
    betas = [beta_coef]
    alphas = [alpha_coef]
    for level in range(LEVELS):
        betas.append(restrict_mean(betas[-1]))
        alphas.append(restrict_mean(alphas[-1]))
    operators = [level_operator(betas[level], alphas[level], zero_pad(betas[level]), SHIFT_BASE * 4.0 ** level)
                 for level in range(LEVELS + 1)]
    rhs_levels = [right_side]
    smoothed = []
    for level in range(LEVELS):
        iterate = chebyshev(jnp.zeros_like(rhs_levels[level]), rhs_levels[level], operators[level],
                            SWEEPS, SMOOTH_LOWER, True, zero_pad)
        remain = rhs_levels[level] - apply_operator(iterate, operators[level], zero_pad)
        smoothed.append(iterate)
        rhs_levels.append(4.0 * restrict_mean(remain))
    correction = chebyshev(jnp.zeros_like(rhs_levels[LEVELS]), rhs_levels[LEVELS], operators[LEVELS],
                           BOTTOM, BOTTOM_LOWER, True, zero_pad)
    for level in range(LEVELS - 1, -1, -1):
        start_field = smoothed[level] + prolong_copy(correction)
        correction = chebyshev(start_field, rhs_levels[level], operators[level],
                               SWEEPS, SMOOTH_LOWER, False, zero_pad)
    residual_field = right_side - apply_operator(correction, operators[0], zero_pad)
    return correction, residual_field
```

```python
import functools

import jax
import jax.numpy as jnp
from jax import lax
from jax.experimental import pallas as pl
from jax.experimental.pallas import tpu as pltpu
from jax.sharding import PartitionSpec as P

MESH = pl.DeviceIdType.MESH
AXES = ("gx", "gy", "gz")

LEVELS = 3
SWEEPS = 4
BOTTOM = 12


SHIFT_BASE = 0.01
UPPER_EIG = 2.0
SMOOTH_LOWER = 0.25
BOTTOM_LOWER = 0.02


def halo_kernel(sizes, *refs):
    sends, halos = refs[0:6], refs[6:12]
    send_sem, recv_sem = refs[12], refs[13]
    index = [lax.axis_index(axis) for axis in AXES]
    targets = []
    for k in range(6):
        axis = k // 2
        if k % 2 == 0:
            exists = index[axis] > 0
            other = index[axis] - 1
        else:
            exists = index[axis] < sizes[axis] - 1
            other = index[axis] + 1
        device = tuple(other if a == axis else index[a] for a in range(3))
        targets.append((exists, device))
    barrier = pltpu.get_barrier_semaphore()
    count = jnp.int32(0)
    for exists, device in targets:

        @pl.when(exists)
        def _():
            pl.semaphore_signal(barrier, inc=1, device_id=device, device_id_type=MESH)

        count = count + exists.astype(jnp.int32)
    pl.semaphore_wait(barrier, count)
    copies = []
    for k, (exists, device) in enumerate(targets):
        copy = pltpu.make_async_remote_copy(
            src_ref=sends[k],
            dst_ref=halos[k ^ 1],
            send_sem=send_sem.at[k],
            recv_sem=recv_sem.at[k ^ 1],
            device_id=device,
            device_id_type=MESH,
        )
        copies.append(copy)
        pl.when(exists)(copy.start)
    for k, (exists, device) in enumerate(targets):

        @pl.when(jnp.logical_not(exists))
        def _():
            halos[k][...] = jnp.zeros(halos[k].shape, halos[k].dtype)

    for k, (exists, device) in enumerate(targets):
        incoming = pltpu.make_async_remote_copy(
            src_ref=sends[k ^ 1],
            dst_ref=halos[k],
            send_sem=send_sem.at[k ^ 1],
            recv_sem=recv_sem.at[k],
            device_id=device,
            device_id_type=MESH,
        )
        pl.when(exists)(copies[k].wait_send)
        pl.when(exists)(incoming.wait_recv)


SIZES = {}


def exchange(faces):
    shape = faces[0].shape + faces[2].shape + faces[4].shape
    ident = SIZES.setdefault(shape, len(SIZES))
    sizes = tuple(lax.axis_size(axis) for axis in AXES)
    vmem = pl.BlockSpec(memory_space=pltpu.VMEM)
    return pl.pallas_call(
        functools.partial(halo_kernel, sizes),
        out_shape=tuple(jax.ShapeDtypeStruct(f.shape, f.dtype) for f in faces),
        in_specs=[vmem] * 6,
        out_specs=tuple([vmem] * 6),
        scratch_shapes=[pltpu.SemaphoreType.DMA((6,)), pltpu.SemaphoreType.DMA((6,))],
        compiler_params=pltpu.CompilerParams(collective_id=ident, has_side_effects=True),
    )(*faces)


def neighbours(field):
    last = [n - 1 for n in field.shape]
    faces = (
        field[0], field[last[0]],
        field[:, 0], field[:, last[1]],
        field[:, :, 0], field[:, :, last[2]],
    )
    halos = exchange(faces)
    return (
        jnp.concatenate([halos[0][None], field[:-1]], axis=0),
        jnp.concatenate([field[1:], halos[1][None]], axis=0),
        jnp.concatenate([halos[2][:, None], field[:, :-1]], axis=1),
        jnp.concatenate([field[:, 1:], halos[3][:, None]], axis=1),
        jnp.concatenate([halos[4][:, :, None], field[:, :, :-1]], axis=2),
        jnp.concatenate([field[:, :, 1:], halos[5][:, :, None]], axis=2),
    )


def split_padded(padded):
    return (
        padded[:-2, 1:-1, 1:-1],
        padded[2:, 1:-1, 1:-1],
        padded[1:-1, :-2, 1:-1],
        padded[1:-1, 2:, 1:-1],
        padded[1:-1, 1:-1, :-2],
        padded[1:-1, 1:-1, 2:],
    )


def zero_pad(field):
    return split_padded(jnp.pad(field, 1))


rim_iterate = neighbours
rim_coefficient = neighbours


def level_operator(beta_level, alpha_level, beta_sides, shift):
    coeffs = tuple((0.5 * (beta_level + other) for other in beta_sides))
    diagonal = shift * alpha_level
    for coeff in coeffs:
        diagonal = diagonal + coeff
    return (coeffs, diagonal)


def apply_operator(field, operator, pad_field):
    coeffs, diagonal = operator
    others = pad_field(field)
    total = coeffs[0] * others[0]
    for index in range(1, 6):
        total = total + coeffs[index] * others[index]
    return diagonal * field - total


def chebyshev(iterate, rhs_level, operator, count, lower, zero_start, pad_field):
    diagonal = operator[1]
    center = (UPPER_EIG + lower) / 2.0
    half_width = (UPPER_EIG - lower) / 2.0
    sigma_ratio = center / half_width
    rho_old = 1.0 / sigma_ratio
    if zero_start:
        remain = rhs_level
    else:
        remain = rhs_level - apply_operator(iterate, operator, pad_field)
    update = remain / diagonal / center
    iterate = iterate + update
    for sweep_index in range(count - 1):
        remain = rhs_level - apply_operator(iterate, operator, pad_field)
        rho_new = 1.0 / (2.0 * sigma_ratio - rho_old)
        update = rho_new * rho_old * update + 2.0 * rho_new / half_width * (remain / diagonal)
        iterate = iterate + update
        rho_old = rho_new
    return iterate


def restrict_mean(field):
    first, second, third = field.shape
    blocks = field.reshape(first // 2, 2, second // 2, 2, third // 2, 2)
    return jnp.sum(blocks, axis=(1, 3, 5)) * 0.125


def prolong_copy(field):
    return jnp.repeat(jnp.repeat(jnp.repeat(field, 2, axis=0), 2, axis=1), 2, axis=2)


def shards(right_side, alpha_coef, beta_coef):
    betas = [beta_coef]
    alphas = [alpha_coef]
    for level in range(LEVELS):
        betas.append(restrict_mean(betas[-1]))
        alphas.append(restrict_mean(alphas[-1]))
    operators = []
    for level in range(LEVELS):
        padded_beta = rim_coefficient(betas[level])
        operators.append(
            level_operator(betas[level], alphas[level], padded_beta, SHIFT_BASE * 4.0**level)
        )
    rhs_levels = [right_side]
    smoothed = []
    for level in range(LEVELS):
        iterate = chebyshev(
            jnp.zeros_like(rhs_levels[level]),
            rhs_levels[level],
            operators[level],
            SWEEPS,
            SMOOTH_LOWER,
            True,
            rim_iterate,
        )
        remain = rhs_levels[level] - apply_operator(iterate, operators[level], rim_iterate)
        smoothed.append(iterate)
        rhs_levels.append(4.0 * restrict_mean(remain))
    coarse_rhs = rhs_levels[LEVELS]
    local_shape = coarse_rhs.shape
    packed = jnp.stack([coarse_rhs, betas[LEVELS], alphas[LEVELS]])
    index_x = lax.axis_index("gx")
    index_y = lax.axis_index("gy")
    index_z = lax.axis_index("gz")
    packed = lax.all_gather(packed, "gx", axis=1, tiled=True)
    packed = lax.all_gather(packed, "gy", axis=2, tiled=True)
    packed = lax.all_gather(packed, "gz", axis=3, tiled=True)
    whole_rhs = packed[0]
    whole_beta = packed[1]
    whole_alpha = packed[2]
    bottom_operator = level_operator(
        whole_beta, whole_alpha, zero_pad(whole_beta), SHIFT_BASE * 4.0**LEVELS
    )
    whole_correction = chebyshev(
        jnp.zeros_like(whole_rhs), whole_rhs, bottom_operator, BOTTOM, BOTTOM_LOWER, True, zero_pad
    )
    starts = (index_x * local_shape[0], index_y * local_shape[1], index_z * local_shape[2])
    correction = lax.dynamic_slice(whole_correction, starts, local_shape)
    for level in range(LEVELS - 1, -1, -1):
        start_field = smoothed[level] + prolong_copy(correction)
        correction = chebyshev(
            start_field,
            rhs_levels[level],
            operators[level],
            SWEEPS,
            SMOOTH_LOWER,
            False,
            rim_iterate,
        )
    residual_field = right_side - apply_operator(correction, operators[0], rim_iterate)
    return (correction, residual_field)


def solution(mesh):
    in_specs = (P("gx", "gy", "gz"), P("gx", "gy", "gz"), P("gx", "gy", "gz"))
    out_specs = (P("gx", "gy", "gz"), P("gx", "gy", "gz"))
    return jax.shard_map(shards, mesh=mesh, in_specs=in_specs, out_specs=out_specs, check_vma=False)
```

```python
import functools

import jax
import jax.numpy as jnp
from jax import lax
from jax.experimental import pallas as pl
from jax.experimental.pallas import tpu as pltpu
from jax.sharding import PartitionSpec as P

MESH = pl.DeviceIdType.MESH
AXES = ("gx", "gy", "gz")

LEVELS = 3
SWEEPS = 4
BOTTOM = 12


SHIFT_BASE = 0.01
UPPER_EIG = 2.0
SMOOTH_LOWER = 0.25
BOTTOM_LOWER = 0.02


def level_kernel(cfg, *refs):
    sizes, shift, count, lower, zero_start, residual = cfg
    n_in = 3 if zero_start else 4
    b_ref, beta_ref, alpha_ref = refs[0:3]
    v0_ref = None if zero_start else refs[3]
    outs = refs[n_in : n_in + (2 if residual else 1)]
    fld, xh, yzh, coef, dbuf, send_sem, recv_sem = refs[n_in + len(outs) :]
    A, B, C = b_ref.shape
    index = [lax.axis_index(axis) for axis in AXES]
    targets = []
    for k in range(6):
        axis = k // 2
        if k % 2 == 0:
            exists = index[axis] > 0
            other = index[axis] - 1
        else:
            exists = index[axis] < sizes[axis] - 1
            other = index[axis] + 1
        device = tuple(other if a == axis else index[a] for a in range(3))
        targets.append((exists, device))

    def halo(h, slot):
        return xh.at[h, slot] if h < 2 else yzh.at[h - 2, slot]

    barrier = pltpu.get_barrier_semaphore()
    total = jnp.int32(0)
    for exists, device in targets:

        @pl.when(exists)
        def _():
            pl.semaphore_signal(barrier, inc=1, device_id=device, device_id_type=MESH)

        total = total + exists.astype(jnp.int32)
    for h, (exists, device) in enumerate(targets):

        @pl.when(jnp.logical_not(exists))
        def _():
            for slot in range(2):
                buf = halo(h, slot)
                buf[...] = jnp.zeros(buf.shape, buf.dtype)

    pl.semaphore_wait(barrier, total)

    def exchange(src, slot):
        sources = (src.at[0], src.at[A - 1], src, src, src, src)
        copies = []
        for k, (exists, device) in enumerate(targets):
            copy = pltpu.make_async_remote_copy(
                src_ref=sources[k],
                dst_ref=halo(k ^ 1, slot),
                send_sem=send_sem.at[k],
                recv_sem=recv_sem.at[slot, k ^ 1],
                device_id=device,
                device_id_type=MESH,
            )
            copies.append(copy)
            pl.when(exists)(copy.start)
        for k, (exists, device) in enumerate(targets):
            incoming = pltpu.make_async_remote_copy(
                src_ref=sources[k ^ 1],
                dst_ref=halo(k, slot),
                send_sem=send_sem.at[k ^ 1],
                recv_sem=recv_sem.at[slot, k],
                device_id=device,
                device_id_type=MESH,
            )
            pl.when(exists)(copies[k].wait_send)
            pl.when(exists)(incoming.wait_recv)

    rows = lax.broadcasted_iota(jnp.int32, (B, C), 0)
    cols = lax.broadcasted_iota(jnp.int32, (B, C), 1)

    def sides(src, i, slot):
        here = src[i]
        lower_x = src[i - 1] if i > 0 else xh[0, slot]
        upper_x = src[i + 1] if i < A - 1 else xh[1, slot]
        lower_y = jnp.where(rows == 0, pltpu.roll(yzh[0, slot, i], 1, 0), pltpu.roll(here, 1, 0))
        upper_y = jnp.where(
            rows == B - 1, pltpu.roll(yzh[1, slot, i], B - 1, 0), pltpu.roll(here, B - 1, 0)
        )
        lower_z = jnp.where(cols == 0, pltpu.roll(yzh[2, slot, i], 1, 1), pltpu.roll(here, 1, 1))
        upper_z = jnp.where(
            cols == C - 1, pltpu.roll(yzh[3, slot, i], C - 1, 1), pltpu.roll(here, C - 1, 1)
        )
        return here, (lower_x, upper_x, lower_y, upper_y, lower_z, upper_z)

    exchanges = [0]

    def next_slot():
        slot = exchanges[0] % 2
        exchanges[0] += 1
        return slot

    slot = next_slot()
    exchange(beta_ref, slot)
    for i in range(A):
        here, others = sides(beta_ref, i, slot)
        diagonal = shift * alpha_ref[i]
        for k in range(6):
            face = 0.5 * (here + others[k])
            coef[k, i] = face
            diagonal = diagonal + face
        coef[6, i] = diagonal

    def apply_rows(src, slot, i):
        here, others = sides(src, i, slot)
        acc = coef[0, i] * others[0]
        for k in range(1, 6):
            acc = acc + coef[k, i] * others[k]
        return b_ref[i] - (coef[6, i] * here - acc)

    center = (UPPER_EIG + lower) / 2.0
    half_width = (UPPER_EIG - lower) / 2.0
    sigma_ratio = center / half_width
    rho_old = 1.0 / sigma_ratio
    current = 0
    if zero_start:
        for i in range(A):
            update = b_ref[i] / coef[6, i] / center
            dbuf[i] = update
            fld[current, i] = update
    else:
        slot = next_slot()
        exchange(v0_ref, slot)
        for i in range(A):
            remain = apply_rows(v0_ref, slot, i)
            update = remain / coef[6, i] / center
            dbuf[i] = update
            fld[current, i] = v0_ref[i] + update
    for sweep in range(count - 1):
        rho_new = 1.0 / (2.0 * sigma_ratio - rho_old)
        slot = next_slot()
        src = fld.at[current]
        exchange(src, slot)
        last = sweep == count - 2
        dst = outs[0] if last else fld.at[1 - current]
        for i in range(A):
            remain = apply_rows(src, slot, i)
            update = (rho_new * rho_old) * dbuf[i] + (2.0 * rho_new / half_width) * (
                remain / coef[6, i]
            )
            dbuf[i] = update
            dst[i] = src[i] + update
        rho_old = rho_new
        current = 1 - current
    if residual:
        slot = next_slot()
        exchange(outs[0], slot)
        for i in range(A):
            outs[1][i] = apply_rows(outs[0], slot, i)


KERNELS = {}


def smooth(level_args, shift, count, lower, zero_start, residual):
    A, B, C = level_args[0].shape
    sizes = tuple(lax.axis_size(axis) for axis in AXES)
    cfg = (sizes, shift, count, lower, zero_start, residual)
    ident = KERNELS.setdefault((A, B, C) + cfg[1:], len(KERNELS))
    vmem = pl.BlockSpec(memory_space=pltpu.VMEM)
    block = jax.ShapeDtypeStruct((A, B, C), jnp.float32)
    n_out = 2 if residual else 1
    return pl.pallas_call(
        functools.partial(level_kernel, cfg),
        out_shape=tuple([block] * n_out),
        in_specs=[vmem] * len(level_args),
        out_specs=tuple([vmem] * n_out),
        scratch_shapes=[
            pltpu.VMEM((2, A, B, C), jnp.float32),
            pltpu.VMEM((2, 2, B, C), jnp.float32),
            pltpu.VMEM((4, 2, A, B, C), jnp.float32),
            pltpu.VMEM((7, A, B, C), jnp.float32),
            pltpu.VMEM((A, B, C), jnp.float32),
            pltpu.SemaphoreType.DMA((6,)),
            pltpu.SemaphoreType.DMA((2, 6)),
        ],
        compiler_params=pltpu.CompilerParams(collective_id=ident, has_side_effects=True),
    )(*level_args)


def split_padded(padded):
    return (
        padded[:-2, 1:-1, 1:-1],
        padded[2:, 1:-1, 1:-1],
        padded[1:-1, :-2, 1:-1],
        padded[1:-1, 2:, 1:-1],
        padded[1:-1, 1:-1, :-2],
        padded[1:-1, 1:-1, 2:],
    )


def zero_pad(field):
    return split_padded(jnp.pad(field, 1))


def level_operator(beta_level, alpha_level, beta_sides, shift):
    coeffs = tuple((0.5 * (beta_level + other) for other in beta_sides))
    diagonal = shift * alpha_level
    for coeff in coeffs:
        diagonal = diagonal + coeff
    return (coeffs, diagonal)


def apply_operator(field, operator, pad_field):
    coeffs, diagonal = operator
    others = pad_field(field)
    total = coeffs[0] * others[0]
    for index in range(1, 6):
        total = total + coeffs[index] * others[index]
    return diagonal * field - total


def chebyshev(iterate, rhs_level, operator, count, lower, zero_start, pad_field):
    diagonal = operator[1]
    center = (UPPER_EIG + lower) / 2.0
    half_width = (UPPER_EIG - lower) / 2.0
    sigma_ratio = center / half_width
    rho_old = 1.0 / sigma_ratio
    if zero_start:
        remain = rhs_level
    else:
        remain = rhs_level - apply_operator(iterate, operator, pad_field)
    update = remain / diagonal / center
    iterate = iterate + update
    for sweep_index in range(count - 1):
        remain = rhs_level - apply_operator(iterate, operator, pad_field)
        rho_new = 1.0 / (2.0 * sigma_ratio - rho_old)
        update = rho_new * rho_old * update + 2.0 * rho_new / half_width * (remain / diagonal)
        iterate = iterate + update
        rho_old = rho_new
    return iterate


def restrict_mean(field):
    first, second, third = field.shape
    blocks = field.reshape(first // 2, 2, second // 2, 2, third // 2, 2)
    return jnp.sum(blocks, axis=(1, 3, 5)) * 0.125


def prolong_copy(field):
    return jnp.repeat(jnp.repeat(jnp.repeat(field, 2, axis=0), 2, axis=1), 2, axis=2)


def shards(right_side, alpha_coef, beta_coef):
    betas = [beta_coef]
    alphas = [alpha_coef]
    for level in range(LEVELS):
        betas.append(restrict_mean(betas[-1]))
        alphas.append(restrict_mean(alphas[-1]))
    rhs_levels = [right_side]
    smoothed = []
    for level in range(LEVELS):
        iterate, remain = smooth(
            (rhs_levels[level], betas[level], alphas[level]),
            SHIFT_BASE * 4.0**level,
            SWEEPS,
            SMOOTH_LOWER,
            True,
            True,
        )
        smoothed.append(iterate)
        rhs_levels.append(4.0 * restrict_mean(remain))
    coarse_rhs = rhs_levels[LEVELS]
    local_shape = coarse_rhs.shape
    packed = jnp.stack([coarse_rhs, betas[LEVELS], alphas[LEVELS]])
    index_x = lax.axis_index("gx")
    index_y = lax.axis_index("gy")
    index_z = lax.axis_index("gz")
    packed = lax.all_gather(packed, "gx", axis=1, tiled=True)
    packed = lax.all_gather(packed, "gy", axis=2, tiled=True)
    packed = lax.all_gather(packed, "gz", axis=3, tiled=True)
    whole_rhs = packed[0]
    whole_beta = packed[1]
    whole_alpha = packed[2]
    bottom_operator = level_operator(
        whole_beta, whole_alpha, zero_pad(whole_beta), SHIFT_BASE * 4.0**LEVELS
    )
    whole_correction = chebyshev(
        jnp.zeros_like(whole_rhs), whole_rhs, bottom_operator, BOTTOM, BOTTOM_LOWER, True, zero_pad
    )
    starts = (index_x * local_shape[0], index_y * local_shape[1], index_z * local_shape[2])
    correction = lax.dynamic_slice(whole_correction, starts, local_shape)
    for level in range(LEVELS - 1, -1, -1):
        start_field = smoothed[level] + prolong_copy(correction)
        outs = smooth(
            (rhs_levels[level], betas[level], alphas[level], start_field),
            SHIFT_BASE * 4.0**level,
            SWEEPS,
            SMOOTH_LOWER,
            False,
            level == 0,
        )
        correction = outs[0]
    residual_field = outs[1]
    return (correction, residual_field)


def solution(mesh):
    in_specs = (P("gx", "gy", "gz"), P("gx", "gy", "gz"), P("gx", "gy", "gz"))
    out_specs = (P("gx", "gy", "gz"), P("gx", "gy", "gz"))
    return jax.shard_map(shards, mesh=mesh, in_specs=in_specs, out_specs=out_specs, check_vma=False)
```

```python
import functools

import jax
import jax.numpy as jnp
from jax import lax
from jax.experimental import pallas as pl
from jax.experimental.pallas import tpu as pltpu
from jax.sharding import PartitionSpec as P

MESH = pl.DeviceIdType.MESH
AXES = ("gx", "gy", "gz")

LEVELS = 3
SWEEPS = 4
BOTTOM = 12


SHIFT_BASE = 0.01
UPPER_EIG = 2.0
SMOOTH_LOWER = 0.25
BOTTOM_LOWER = 0.02


def level_kernel(cfg, *refs):
    sizes, shift, count, lower, zero_start, residual, restrict = cfg
    n_in = 3 if zero_start else 4
    b_ref, beta_ref, alpha_ref = refs[0:3]
    v0_ref = None if zero_start else refs[3]
    n_out = 1 + (1 if residual and not restrict else 0) + (3 if restrict else 0)
    outs = refs[n_in : n_in + n_out]
    fld, xh, yzh, coef, dbuf, send_sem, recv_sem = refs[n_in + len(outs) :]
    A, B, C = b_ref.shape
    index = [lax.axis_index(axis) for axis in AXES]
    targets = []
    for k in range(6):
        axis = k // 2
        if k % 2 == 0:
            exists = index[axis] > 0
            other = index[axis] - 1
        else:
            exists = index[axis] < sizes[axis] - 1
            other = index[axis] + 1
        device = tuple(other if a == axis else index[a] for a in range(3))
        targets.append((exists, device))

    def halo(h, slot):
        return xh.at[h, slot] if h < 2 else yzh.at[h - 2, slot]

    barrier = pltpu.get_barrier_semaphore()
    total = jnp.int32(0)
    for exists, device in targets:

        @pl.when(exists)
        def _():
            pl.semaphore_signal(barrier, inc=1, device_id=device, device_id_type=MESH)

        total = total + exists.astype(jnp.int32)
    for h, (exists, device) in enumerate(targets):

        @pl.when(jnp.logical_not(exists))
        def _():
            for slot in range(2):
                buf = halo(h, slot)
                buf[...] = jnp.zeros(buf.shape, buf.dtype)

    if restrict:
        coarse_rows = (
            lax.broadcasted_iota(jnp.int32, (B // 2, B), 1) // 2
            == lax.broadcasted_iota(jnp.int32, (B // 2, B), 0)
        ).astype(jnp.float32)
        coarse_cols = (
            lax.broadcasted_iota(jnp.int32, (C, C // 2), 0) // 2
            == lax.broadcasted_iota(jnp.int32, (C, C // 2), 1)
        ).astype(jnp.float32)

        def restrict_into(src, dst, scale):
            for i in range(A // 2):
                pair = src[2 * i] + src[2 * i + 1]
                half = jnp.dot(
                    coarse_rows, pair, precision=lax.Precision.HIGHEST,
                    preferred_element_type=jnp.float32,
                )
                dst[i] = scale * jnp.dot(
                    half, coarse_cols, precision=lax.Precision.HIGHEST,
                    preferred_element_type=jnp.float32,
                )

        restrict_into(beta_ref, outs[2], 0.125)
        restrict_into(alpha_ref, outs[3], 0.125)
    pl.semaphore_wait(barrier, total)

    def exchange(src, slot):
        sources = (src.at[0], src.at[A - 1], src, src, src, src)
        copies = []
        for k, (exists, device) in enumerate(targets):
            copy = pltpu.make_async_remote_copy(
                src_ref=sources[k],
                dst_ref=halo(k ^ 1, slot),
                send_sem=send_sem.at[k],
                recv_sem=recv_sem.at[slot, k ^ 1],
                device_id=device,
                device_id_type=MESH,
            )
            copies.append(copy)
            pl.when(exists)(copy.start)
        for k, (exists, device) in enumerate(targets):
            incoming = pltpu.make_async_remote_copy(
                src_ref=sources[k ^ 1],
                dst_ref=halo(k, slot),
                send_sem=send_sem.at[k ^ 1],
                recv_sem=recv_sem.at[slot, k],
                device_id=device,
                device_id_type=MESH,
            )
            pl.when(exists)(copies[k].wait_send)
            pl.when(exists)(incoming.wait_recv)

    rows = lax.broadcasted_iota(jnp.int32, (B, C), 0)
    cols = lax.broadcasted_iota(jnp.int32, (B, C), 1)

    def sides(src, i, slot):
        here = src[i]
        lower_x = src[i - 1] if i > 0 else xh[0, slot]
        upper_x = src[i + 1] if i < A - 1 else xh[1, slot]
        lower_y = jnp.where(rows == 0, pltpu.roll(yzh[0, slot, i], 1, 0), pltpu.roll(here, 1, 0))
        upper_y = jnp.where(
            rows == B - 1, pltpu.roll(yzh[1, slot, i], B - 1, 0), pltpu.roll(here, B - 1, 0)
        )
        lower_z = jnp.where(cols == 0, pltpu.roll(yzh[2, slot, i], 1, 1), pltpu.roll(here, 1, 1))
        upper_z = jnp.where(
            cols == C - 1, pltpu.roll(yzh[3, slot, i], C - 1, 1), pltpu.roll(here, C - 1, 1)
        )
        return here, (lower_x, upper_x, lower_y, upper_y, lower_z, upper_z)

    exchanges = [0]

    def next_slot():
        slot = exchanges[0] % 2
        exchanges[0] += 1
        return slot

    slot = next_slot()
    exchange(beta_ref, slot)
    for i in range(A):
        here, others = sides(beta_ref, i, slot)
        diagonal = shift * alpha_ref[i]
        for k in range(6):
            face = 0.5 * (here + others[k])
            coef[k, i] = face
            diagonal = diagonal + face
        coef[6, i] = diagonal

    def apply_rows(src, slot, i):
        here, others = sides(src, i, slot)
        acc = coef[0, i] * others[0]
        for k in range(1, 6):
            acc = acc + coef[k, i] * others[k]
        return b_ref[i] - (coef[6, i] * here - acc)

    center = (UPPER_EIG + lower) / 2.0
    half_width = (UPPER_EIG - lower) / 2.0
    sigma_ratio = center / half_width
    rho_old = 1.0 / sigma_ratio
    current = 0
    if zero_start:
        for i in range(A):
            update = b_ref[i] / coef[6, i] / center
            dbuf[i] = update
            fld[current, i] = update
    else:
        slot = next_slot()
        exchange(v0_ref, slot)
        for i in range(A):
            remain = apply_rows(v0_ref, slot, i)
            update = remain / coef[6, i] / center
            dbuf[i] = update
            fld[current, i] = v0_ref[i] + update
    for sweep in range(count - 1):
        rho_new = 1.0 / (2.0 * sigma_ratio - rho_old)
        slot = next_slot()
        src = fld.at[current]
        exchange(src, slot)
        last = sweep == count - 2
        dst = outs[0] if last else fld.at[1 - current]
        for i in range(A):
            remain = apply_rows(src, slot, i)
            update = (rho_new * rho_old) * dbuf[i] + (2.0 * rho_new / half_width) * (
                remain / coef[6, i]
            )
            dbuf[i] = update
            dst[i] = src[i] + update
        rho_old = rho_new
        current = 1 - current
    if residual:
        slot = next_slot()
        exchange(outs[0], slot)
        remain_ref = dbuf if restrict else outs[1]
        for i in range(A):
            remain_ref[i] = apply_rows(outs[0], slot, i)
        if restrict:
            restrict_into(dbuf, outs[1], 0.5)


KERNELS = {}


def smooth(level_args, shift, count, lower, zero_start, residual, restrict=False):
    A, B, C = level_args[0].shape
    sizes = tuple(lax.axis_size(axis) for axis in AXES)
    cfg = (sizes, shift, count, lower, zero_start, residual, restrict)
    ident = KERNELS.setdefault((A, B, C) + cfg[1:], len(KERNELS))
    vmem = pl.BlockSpec(memory_space=pltpu.VMEM)
    block = jax.ShapeDtypeStruct((A, B, C), jnp.float32)
    coarse = jax.ShapeDtypeStruct((A // 2, B // 2, C // 2), jnp.float32)
    shapes = [block] + ([block] if residual and not restrict else []) + ([coarse] * 3 if restrict else [])
    n_out = len(shapes)
    return pl.pallas_call(
        functools.partial(level_kernel, cfg),
        out_shape=tuple(shapes),
        in_specs=[vmem] * len(level_args),
        out_specs=tuple([vmem] * n_out),
        scratch_shapes=[
            pltpu.VMEM((2, A, B, C), jnp.float32),
            pltpu.VMEM((2, 2, B, C), jnp.float32),
            pltpu.VMEM((4, 2, A, B, C), jnp.float32),
            pltpu.VMEM((7, A, B, C), jnp.float32),
            pltpu.VMEM((A, B, C), jnp.float32),
            pltpu.SemaphoreType.DMA((6,)),
            pltpu.SemaphoreType.DMA((2, 6)),
        ],
        compiler_params=pltpu.CompilerParams(collective_id=ident, has_side_effects=True),
    )(*level_args)


def split_padded(padded):
    return (
        padded[:-2, 1:-1, 1:-1],
        padded[2:, 1:-1, 1:-1],
        padded[1:-1, :-2, 1:-1],
        padded[1:-1, 2:, 1:-1],
        padded[1:-1, 1:-1, :-2],
        padded[1:-1, 1:-1, 2:],
    )


def zero_pad(field):
    return split_padded(jnp.pad(field, 1))


def level_operator(beta_level, alpha_level, beta_sides, shift):
    coeffs = tuple((0.5 * (beta_level + other) for other in beta_sides))
    diagonal = shift * alpha_level
    for coeff in coeffs:
        diagonal = diagonal + coeff
    return (coeffs, diagonal)


def apply_operator(field, operator, pad_field):
    coeffs, diagonal = operator
    others = pad_field(field)
    total = coeffs[0] * others[0]
    for index in range(1, 6):
        total = total + coeffs[index] * others[index]
    return diagonal * field - total


def chebyshev(iterate, rhs_level, operator, count, lower, zero_start, pad_field):
    diagonal = operator[1]
    center = (UPPER_EIG + lower) / 2.0
    half_width = (UPPER_EIG - lower) / 2.0
    sigma_ratio = center / half_width
    rho_old = 1.0 / sigma_ratio
    if zero_start:
        remain = rhs_level
    else:
        remain = rhs_level - apply_operator(iterate, operator, pad_field)
    update = remain / diagonal / center
    iterate = iterate + update
    for sweep_index in range(count - 1):
        remain = rhs_level - apply_operator(iterate, operator, pad_field)
        rho_new = 1.0 / (2.0 * sigma_ratio - rho_old)
        update = rho_new * rho_old * update + 2.0 * rho_new / half_width * (remain / diagonal)
        iterate = iterate + update
        rho_old = rho_new
    return iterate


def restrict_mean(field):
    first, second, third = field.shape
    blocks = field.reshape(first // 2, 2, second // 2, 2, third // 2, 2)
    return jnp.sum(blocks, axis=(1, 3, 5)) * 0.125


def prolong_copy(field):
    return jnp.repeat(jnp.repeat(jnp.repeat(field, 2, axis=0), 2, axis=1), 2, axis=2)


def shards(right_side, alpha_coef, beta_coef):
    betas = [beta_coef]
    alphas = [alpha_coef]
    rhs_levels = [right_side]
    smoothed = []
    for level in range(LEVELS):
        iterate, coarse_rhs, coarse_beta, coarse_alpha = smooth(
            (rhs_levels[level], betas[level], alphas[level]),
            SHIFT_BASE * 4.0**level,
            SWEEPS,
            SMOOTH_LOWER,
            True,
            True,
            True,
        )
        smoothed.append(iterate)
        rhs_levels.append(coarse_rhs)
        betas.append(coarse_beta)
        alphas.append(coarse_alpha)
    coarse_rhs = rhs_levels[LEVELS]
    local_shape = coarse_rhs.shape
    packed = jnp.stack([coarse_rhs, betas[LEVELS], alphas[LEVELS]])
    index_x = lax.axis_index("gx")
    index_y = lax.axis_index("gy")
    index_z = lax.axis_index("gz")
    counts = tuple(lax.axis_size(axis) for axis in AXES)
    packed = lax.all_gather(packed, AXES)
    packed = packed.reshape(counts + packed.shape[1:])
    packed = packed.transpose(3, 0, 4, 1, 5, 2, 6)
    packed = packed.reshape(
        (3,) + tuple(n * s for n, s in zip(counts, local_shape))
    )
    whole_rhs = packed[0]
    whole_beta = packed[1]
    whole_alpha = packed[2]
    bottom_operator = level_operator(
        whole_beta, whole_alpha, zero_pad(whole_beta), SHIFT_BASE * 4.0**LEVELS
    )
    whole_correction = chebyshev(
        jnp.zeros_like(whole_rhs), whole_rhs, bottom_operator, BOTTOM, BOTTOM_LOWER, True, zero_pad
    )
    starts = (index_x * local_shape[0], index_y * local_shape[1], index_z * local_shape[2])
    correction = lax.dynamic_slice(whole_correction, starts, local_shape)
    for level in range(LEVELS - 1, -1, -1):
        start_field = smoothed[level] + prolong_copy(correction)
        outs = smooth(
            (rhs_levels[level], betas[level], alphas[level], start_field),
            SHIFT_BASE * 4.0**level,
            SWEEPS,
            SMOOTH_LOWER,
            False,
            level == 0,
        )
        correction = outs[0]
    residual_field = outs[1]
    return (correction, residual_field)


def solution(mesh):
    in_specs = (P("gx", "gy", "gz"), P("gx", "gy", "gz"), P("gx", "gy", "gz"))
    out_specs = (P("gx", "gy", "gz"), P("gx", "gy", "gz"))
    return jax.shard_map(shards, mesh=mesh, in_specs=in_specs, out_specs=out_specs, check_vma=False)
```

```python
import functools

import jax
import jax.numpy as jnp
from jax import lax
from jax.experimental import pallas as pl
from jax.experimental.pallas import tpu as pltpu
from jax.sharding import PartitionSpec as P

MESH = pl.DeviceIdType.MESH
AXES = ("gx", "gy", "gz")
SLOTS = 3

LEVELS = 3
SWEEPS = 4
BOTTOM = 12


SHIFT_BASE = 0.01
UPPER_EIG = 2.0
SMOOTH_LOWER = 0.25
BOTTOM_LOWER = 0.02


def level_kernel(cfg, *refs):
    sizes, shift, count, lower, zero_start, residual, restrict = cfg
    n_in = 3 if zero_start else 4
    b_ref, beta_ref, alpha_ref = refs[0:3]
    v0_ref = None if zero_start else refs[3]
    n_out = 1 + (1 if residual and not restrict else 0) + (3 if restrict else 0)
    outs = refs[n_in : n_in + n_out]
    fld, xh, yzh, coef, dbuf, send_sem, recv_sem = refs[n_in + len(outs) :]
    A, B, C = b_ref.shape
    index = [lax.axis_index(axis) for axis in AXES]
    targets = []
    for k in range(6):
        axis = k // 2
        if k % 2 == 0:
            exists = index[axis] > 0
            other = index[axis] - 1
        else:
            exists = index[axis] < sizes[axis] - 1
            other = index[axis] + 1
        device = tuple(other if a == axis else index[a] for a in range(3))
        targets.append((exists, device))

    def halo(h, slot):
        return xh.at[h, slot] if h < 2 else yzh.at[h - 2, slot]

    barrier = pltpu.get_barrier_semaphore()
    total = jnp.int32(0)
    for exists, device in targets:

        @pl.when(exists)
        def _():
            pl.semaphore_signal(barrier, inc=1, device_id=device, device_id_type=MESH)

        total = total + exists.astype(jnp.int32)
    for h, (exists, device) in enumerate(targets):

        @pl.when(jnp.logical_not(exists))
        def _():
            for slot in range(SLOTS):
                buf = halo(h, slot)
                buf[...] = jnp.zeros(buf.shape, buf.dtype)

    if restrict:
        coarse_rows = (
            lax.broadcasted_iota(jnp.int32, (B // 2, B), 1) // 2
            == lax.broadcasted_iota(jnp.int32, (B // 2, B), 0)
        ).astype(jnp.float32)
        coarse_cols = (
            lax.broadcasted_iota(jnp.int32, (C, C // 2), 0) // 2
            == lax.broadcasted_iota(jnp.int32, (C, C // 2), 1)
        ).astype(jnp.float32)

        def restrict_into(src, dst, scale):
            for i in range(A // 2):
                pair = src[2 * i] + src[2 * i + 1]
                half = jnp.dot(
                    coarse_rows, pair, precision=lax.Precision.HIGHEST,
                    preferred_element_type=jnp.float32,
                )
                dst[i] = scale * jnp.dot(
                    half, coarse_cols, precision=lax.Precision.HIGHEST,
                    preferred_element_type=jnp.float32,
                )

        restrict_into(beta_ref, outs[2], 0.125)
        restrict_into(alpha_ref, outs[3], 0.125)
    pl.semaphore_wait(barrier, total)

    def exchange_start(src, slot):
        sources = (src.at[0], src.at[A - 1], src, src, src, src)
        waits = []
        for k, (exists, device) in enumerate(targets):
            copy = pltpu.make_async_remote_copy(
                src_ref=sources[k],
                dst_ref=halo(k ^ 1, slot),
                send_sem=send_sem.at[slot, k],
                recv_sem=recv_sem.at[slot, k ^ 1],
                device_id=device,
                device_id_type=MESH,
            )
            pl.when(exists)(copy.start)
            incoming = pltpu.make_async_remote_copy(
                src_ref=sources[k ^ 1],
                dst_ref=halo(k, slot),
                send_sem=send_sem.at[slot, k ^ 1],
                recv_sem=recv_sem.at[slot, k],
                device_id=device,
                device_id_type=MESH,
            )
            waits.append((exists, copy.wait_send))
            waits.append((exists, incoming.wait_recv))
        return waits

    def exchange_finish(waits):
        for exists, wait in waits:
            pl.when(exists)(wait)

    def exchange(src, slot):
        exchange_finish(exchange_start(src, slot))

    rows = lax.broadcasted_iota(jnp.int32, (B, C), 0)
    cols = lax.broadcasted_iota(jnp.int32, (B, C), 1)

    def sides(src, i, slot):
        here = src[i]
        lower_x = src[i - 1] if i > 0 else xh[0, slot]
        upper_x = src[i + 1] if i < A - 1 else xh[1, slot]
        lower_y = jnp.where(rows == 0, pltpu.roll(yzh[0, slot, i], 1, 0), pltpu.roll(here, 1, 0))
        upper_y = jnp.where(
            rows == B - 1, pltpu.roll(yzh[1, slot, i], B - 1, 0), pltpu.roll(here, B - 1, 0)
        )
        lower_z = jnp.where(cols == 0, pltpu.roll(yzh[2, slot, i], 1, 1), pltpu.roll(here, 1, 1))
        upper_z = jnp.where(
            cols == C - 1, pltpu.roll(yzh[3, slot, i], C - 1, 1), pltpu.roll(here, C - 1, 1)
        )
        return here, (lower_x, upper_x, lower_y, upper_y, lower_z, upper_z)

    exchanges = [0]

    def next_slot():
        slot = exchanges[0] % SLOTS
        exchanges[0] += 1
        return slot

    slot = next_slot()
    if zero_start:
        exchange(beta_ref, slot)
    else:
        first_slot = next_slot()
        first_waits = exchange_start(v0_ref, first_slot)
        exchange(beta_ref, slot)
    for i in range(A):
        here, others = sides(beta_ref, i, slot)
        diagonal = shift * alpha_ref[i]
        for k in range(6):
            face = 0.5 * (here + others[k])
            coef[k, i] = face
            diagonal = diagonal + face
        coef[6, i] = diagonal

    def apply_rows(src, slot, i):
        here, others = sides(src, i, slot)
        acc = coef[0, i] * others[0]
        for k in range(1, 6):
            acc = acc + coef[k, i] * others[k]
        return b_ref[i] - (coef[6, i] * here - acc)

    center = (UPPER_EIG + lower) / 2.0
    half_width = (UPPER_EIG - lower) / 2.0
    sigma_ratio = center / half_width
    rho_old = 1.0 / sigma_ratio
    current = 0
    if zero_start:
        for i in range(A):
            update = b_ref[i] / coef[6, i] / center
            dbuf[i] = update
            fld[current, i] = update
    else:
        exchange_finish(first_waits)
        for i in range(A):
            remain = apply_rows(v0_ref, first_slot, i)
            update = remain / coef[6, i] / center
            dbuf[i] = update
            fld[current, i] = v0_ref[i] + update
    for sweep in range(count - 1):
        rho_new = 1.0 / (2.0 * sigma_ratio - rho_old)
        slot = next_slot()
        src = fld.at[current]
        exchange(src, slot)
        last = sweep == count - 2
        dst = outs[0] if last else fld.at[1 - current]
        for i in range(A):
            remain = apply_rows(src, slot, i)
            update = (rho_new * rho_old) * dbuf[i] + (2.0 * rho_new / half_width) * (
                remain / coef[6, i]
            )
            dbuf[i] = update
            dst[i] = src[i] + update
        rho_old = rho_new
        current = 1 - current
    if residual:
        slot = next_slot()
        exchange(outs[0], slot)
        remain_ref = dbuf if restrict else outs[1]
        for i in range(A):
            remain_ref[i] = apply_rows(outs[0], slot, i)
        if restrict:
            restrict_into(dbuf, outs[1], 0.5)


KERNELS = {}


def smooth(level_args, shift, count, lower, zero_start, residual, restrict=False):
    A, B, C = level_args[0].shape
    sizes = tuple(lax.axis_size(axis) for axis in AXES)
    cfg = (sizes, shift, count, lower, zero_start, residual, restrict)
    ident = KERNELS.setdefault((A, B, C) + cfg[1:], len(KERNELS))
    vmem = pl.BlockSpec(memory_space=pltpu.VMEM)
    block = jax.ShapeDtypeStruct((A, B, C), jnp.float32)
    coarse = jax.ShapeDtypeStruct((A // 2, B // 2, C // 2), jnp.float32)
    shapes = [block] + ([block] if residual and not restrict else []) + ([coarse] * 3 if restrict else [])
    n_out = len(shapes)
    return pl.pallas_call(
        functools.partial(level_kernel, cfg),
        out_shape=tuple(shapes),
        in_specs=[vmem] * len(level_args),
        out_specs=tuple([vmem] * n_out),
        scratch_shapes=[
            pltpu.VMEM((2, A, B, C), jnp.float32),
            pltpu.VMEM((2, SLOTS, B, C), jnp.float32),
            pltpu.VMEM((4, SLOTS, A, B, C), jnp.float32),
            pltpu.VMEM((7, A, B, C), jnp.float32),
            pltpu.VMEM((A, B, C), jnp.float32),
            pltpu.SemaphoreType.DMA((SLOTS, 6)),
            pltpu.SemaphoreType.DMA((SLOTS, 6)),
        ],
        compiler_params=pltpu.CompilerParams(collective_id=ident, has_side_effects=True),
    )(*level_args)


def split_padded(padded):
    return (
        padded[:-2, 1:-1, 1:-1],
        padded[2:, 1:-1, 1:-1],
        padded[1:-1, :-2, 1:-1],
        padded[1:-1, 2:, 1:-1],
        padded[1:-1, 1:-1, :-2],
        padded[1:-1, 1:-1, 2:],
    )


def zero_pad(field):
    return split_padded(jnp.pad(field, 1))


def level_operator(beta_level, alpha_level, beta_sides, shift):
    coeffs = tuple((0.5 * (beta_level + other) for other in beta_sides))
    diagonal = shift * alpha_level
    for coeff in coeffs:
        diagonal = diagonal + coeff
    return (coeffs, diagonal)


def apply_operator(field, operator, pad_field):
    coeffs, diagonal = operator
    others = pad_field(field)
    total = coeffs[0] * others[0]
    for index in range(1, 6):
        total = total + coeffs[index] * others[index]
    return diagonal * field - total


def chebyshev(iterate, rhs_level, operator, count, lower, zero_start, pad_field):
    diagonal = operator[1]
    center = (UPPER_EIG + lower) / 2.0
    half_width = (UPPER_EIG - lower) / 2.0
    sigma_ratio = center / half_width
    rho_old = 1.0 / sigma_ratio
    if zero_start:
        remain = rhs_level
    else:
        remain = rhs_level - apply_operator(iterate, operator, pad_field)
    update = remain / diagonal / center
    iterate = iterate + update
    for sweep_index in range(count - 1):
        remain = rhs_level - apply_operator(iterate, operator, pad_field)
        rho_new = 1.0 / (2.0 * sigma_ratio - rho_old)
        update = rho_new * rho_old * update + 2.0 * rho_new / half_width * (remain / diagonal)
        iterate = iterate + update
        rho_old = rho_new
    return iterate


def restrict_mean(field):
    first, second, third = field.shape
    blocks = field.reshape(first // 2, 2, second // 2, 2, third // 2, 2)
    return jnp.sum(blocks, axis=(1, 3, 5)) * 0.125


def prolong_copy(field):
    return jnp.repeat(jnp.repeat(jnp.repeat(field, 2, axis=0), 2, axis=1), 2, axis=2)


def shards(right_side, alpha_coef, beta_coef):
    betas = [beta_coef]
    alphas = [alpha_coef]
    rhs_levels = [right_side]
    smoothed = []
    for level in range(LEVELS):
        iterate, coarse_rhs, coarse_beta, coarse_alpha = smooth(
            (rhs_levels[level], betas[level], alphas[level]),
            SHIFT_BASE * 4.0**level,
            SWEEPS,
            SMOOTH_LOWER,
            True,
            True,
            True,
        )
        smoothed.append(iterate)
        rhs_levels.append(coarse_rhs)
        betas.append(coarse_beta)
        alphas.append(coarse_alpha)
    coarse_rhs = rhs_levels[LEVELS]
    local_shape = coarse_rhs.shape
    packed = jnp.stack([coarse_rhs, betas[LEVELS], alphas[LEVELS]])
    index_x = lax.axis_index("gx")
    index_y = lax.axis_index("gy")
    index_z = lax.axis_index("gz")
    packed = lax.all_gather(packed, "gx", axis=1, tiled=True)
    packed = lax.all_gather(packed, "gy", axis=2, tiled=True)
    packed = lax.all_gather(packed, "gz", axis=3, tiled=True)
    whole_rhs = packed[0]
    whole_beta = packed[1]
    whole_alpha = packed[2]
    bottom_operator = level_operator(
        whole_beta, whole_alpha, zero_pad(whole_beta), SHIFT_BASE * 4.0**LEVELS
    )
    whole_correction = chebyshev(
        jnp.zeros_like(whole_rhs), whole_rhs, bottom_operator, BOTTOM, BOTTOM_LOWER, True, zero_pad
    )
    starts = (index_x * local_shape[0], index_y * local_shape[1], index_z * local_shape[2])
    correction = lax.dynamic_slice(whole_correction, starts, local_shape)
    for level in range(LEVELS - 1, -1, -1):
        start_field = smoothed[level] + prolong_copy(correction)
        outs = smooth(
            (rhs_levels[level], betas[level], alphas[level], start_field),
            SHIFT_BASE * 4.0**level,
            SWEEPS,
            SMOOTH_LOWER,
            False,
            level == 0,
        )
        correction = outs[0]
    residual_field = outs[1]
    return (correction, residual_field)


def solution(mesh):
    in_specs = (P("gx", "gy", "gz"), P("gx", "gy", "gz"), P("gx", "gy", "gz"))
    out_specs = (P("gx", "gy", "gz"), P("gx", "gy", "gz"))
    return jax.shard_map(shards, mesh=mesh, in_specs=in_specs, out_specs=out_specs, check_vma=False)
```

```python
import functools

import jax
import jax.numpy as jnp
from jax import lax
from jax.experimental import pallas as pl
from jax.experimental.pallas import tpu as pltpu
from jax.sharding import PartitionSpec as P

MESH = pl.DeviceIdType.MESH
AXES = ("gx", "gy", "gz")
SLOTS = 3

LEVELS = 3
SWEEPS = 4
BOTTOM = 12


SHIFT_BASE = 0.01
UPPER_EIG = 2.0
SMOOTH_LOWER = 0.25
BOTTOM_LOWER = 0.02


def level_kernel(cfg, *refs):
    sizes, shift, count, lower, zero_start, residual, restrict = cfg
    n_in = 3 if zero_start else 4
    b_ref, beta_ref, alpha_ref = refs[0:3]
    v0_ref = None if zero_start else refs[3]
    n_out = 1 + (1 if residual and not restrict else 0) + (3 if restrict else 0)
    outs = refs[n_in : n_in + n_out]
    fld, xh, yzh, coef, dbuf, send_sem, recv_sem = refs[n_in + len(outs) :]
    A, B, C = b_ref.shape
    index = [lax.axis_index(axis) for axis in AXES]
    targets = []
    for k in range(6):
        axis = k // 2
        if k % 2 == 0:
            exists = index[axis] > 0
            other = index[axis] - 1
        else:
            exists = index[axis] < sizes[axis] - 1
            other = index[axis] + 1
        device = tuple(other if a == axis else index[a] for a in range(3))
        targets.append((exists, device))

    def halo(h, slot):
        return xh.at[h, slot] if h < 2 else yzh.at[h - 2, slot]

    barrier = pltpu.get_barrier_semaphore()
    total = jnp.int32(0)
    for exists, device in targets:

        @pl.when(exists)
        def _():
            pl.semaphore_signal(barrier, inc=1, device_id=device, device_id_type=MESH)

        total = total + exists.astype(jnp.int32)
    for h, (exists, device) in enumerate(targets):

        @pl.when(jnp.logical_not(exists))
        def _():
            for slot in range(SLOTS):
                buf = halo(h, slot)
                buf[...] = jnp.zeros(buf.shape, buf.dtype)

    if restrict:
        coarse_rows = (
            lax.broadcasted_iota(jnp.int32, (B // 2, B), 1) // 2
            == lax.broadcasted_iota(jnp.int32, (B // 2, B), 0)
        ).astype(jnp.float32)
        coarse_cols = (
            lax.broadcasted_iota(jnp.int32, (C, C // 2), 0) // 2
            == lax.broadcasted_iota(jnp.int32, (C, C // 2), 1)
        ).astype(jnp.float32)

        def restrict_into(src, dst, scale):
            for i in range(A // 2):
                pair = src[2 * i] + src[2 * i + 1]
                half = jnp.dot(
                    coarse_rows, pair, precision=lax.Precision.HIGHEST,
                    preferred_element_type=jnp.float32,
                )
                dst[i] = scale * jnp.dot(
                    half, coarse_cols, precision=lax.Precision.HIGHEST,
                    preferred_element_type=jnp.float32,
                )

        restrict_into(beta_ref, outs[2], 0.125)
        restrict_into(alpha_ref, outs[3], 0.125)
    pl.semaphore_wait(barrier, total)

    def exchange_start(src, slot):
        sources = (src.at[0], src.at[A - 1], src, src, src, src)
        waits = []
        for k, (exists, device) in enumerate(targets):
            copy = pltpu.make_async_remote_copy(
                src_ref=sources[k],
                dst_ref=halo(k ^ 1, slot),
                send_sem=send_sem.at[slot, k],
                recv_sem=recv_sem.at[slot, k ^ 1],
                device_id=device,
                device_id_type=MESH,
            )
            pl.when(exists)(copy.start)
            incoming = pltpu.make_async_remote_copy(
                src_ref=sources[k ^ 1],
                dst_ref=halo(k, slot),
                send_sem=send_sem.at[slot, k ^ 1],
                recv_sem=recv_sem.at[slot, k],
                device_id=device,
                device_id_type=MESH,
            )
            waits.append((exists, copy.wait_send))
            waits.append((exists, incoming.wait_recv))
        return waits

    def exchange_finish(waits):
        for exists, wait in waits:
            pl.when(exists)(wait)

    def exchange(src, slot):
        exchange_finish(exchange_start(src, slot))

    rows = lax.broadcasted_iota(jnp.int32, (B, C), 0)
    cols = lax.broadcasted_iota(jnp.int32, (B, C), 1)

    def sides(src, i, slot):
        here = src[i]
        lower_x = src[i - 1] if i > 0 else xh[0, slot]
        upper_x = src[i + 1] if i < A - 1 else xh[1, slot]
        lower_y = jnp.where(rows == 0, pltpu.roll(yzh[0, slot, i], 1, 0), pltpu.roll(here, 1, 0))
        upper_y = jnp.where(
            rows == B - 1, pltpu.roll(yzh[1, slot, i], B - 1, 0), pltpu.roll(here, B - 1, 0)
        )
        lower_z = jnp.where(cols == 0, pltpu.roll(yzh[2, slot, i], 1, 1), pltpu.roll(here, 1, 1))
        upper_z = jnp.where(
            cols == C - 1, pltpu.roll(yzh[3, slot, i], C - 1, 1), pltpu.roll(here, C - 1, 1)
        )
        return here, (lower_x, upper_x, lower_y, upper_y, lower_z, upper_z)

    exchanges = [0]

    def next_slot():
        slot = exchanges[0] % SLOTS
        exchanges[0] += 1
        return slot

    slot = next_slot()
    if zero_start:
        exchange(beta_ref, slot)
    else:
        first_slot = next_slot()
        first_waits = exchange_start(v0_ref, first_slot)
        exchange(beta_ref, slot)
    for i in range(A):
        here, others = sides(beta_ref, i, slot)
        diagonal = shift * alpha_ref[i]
        for k in range(6):
            face = 0.5 * (here + others[k])
            coef[k, i] = face
            diagonal = diagonal + face
        coef[6, i] = diagonal

    def apply_rows(src, slot, i):
        here, others = sides(src, i, slot)
        acc = coef[0, i] * others[0]
        for k in range(1, 6):
            acc = acc + coef[k, i] * others[k]
        return b_ref[i] - (coef[6, i] * here - acc)

    center = (UPPER_EIG + lower) / 2.0
    half_width = (UPPER_EIG - lower) / 2.0
    sigma_ratio = center / half_width
    rho_old = 1.0 / sigma_ratio
    current = 0
    if zero_start:
        for i in range(A):
            update = b_ref[i] / coef[6, i] / center
            dbuf[i] = update
            fld[current, i] = update
    else:
        exchange_finish(first_waits)
        for i in range(A):
            remain = apply_rows(v0_ref, first_slot, i)
            update = remain / coef[6, i] / center
            dbuf[i] = update
            fld[current, i] = v0_ref[i] + update
    for sweep in range(count - 1):
        rho_new = 1.0 / (2.0 * sigma_ratio - rho_old)
        slot = next_slot()
        src = fld.at[current]
        exchange(src, slot)
        last = sweep == count - 2
        dst = outs[0] if last else fld.at[1 - current]
        for i in range(A):
            remain = apply_rows(src, slot, i)
            update = (rho_new * rho_old) * dbuf[i] + (2.0 * rho_new / half_width) * (
                remain / coef[6, i]
            )
            dbuf[i] = update
            dst[i] = src[i] + update
        rho_old = rho_new
        current = 1 - current
    if residual:
        slot = next_slot()
        exchange(outs[0], slot)
        remain_ref = dbuf if restrict else outs[1]
        for i in range(A):
            remain_ref[i] = apply_rows(outs[0], slot, i)
        if restrict:
            restrict_into(dbuf, outs[1], 0.5)


KERNELS = {}


def smooth(level_args, shift, count, lower, zero_start, residual, restrict=False):
    A, B, C = level_args[0].shape
    sizes = tuple(lax.axis_size(axis) for axis in AXES)
    cfg = (sizes, shift, count, lower, zero_start, residual, restrict)
    ident = KERNELS.setdefault((A, B, C) + cfg[1:], len(KERNELS))
    vmem = pl.BlockSpec(memory_space=pltpu.VMEM)
    block = jax.ShapeDtypeStruct((A, B, C), jnp.float32)
    coarse = jax.ShapeDtypeStruct((A // 2, B // 2, C // 2), jnp.float32)
    shapes = [block] + ([block] if residual and not restrict else []) + ([coarse] * 3 if restrict else [])
    n_out = len(shapes)
    return pl.pallas_call(
        functools.partial(level_kernel, cfg),
        out_shape=tuple(shapes),
        in_specs=[vmem] * len(level_args),
        out_specs=tuple([vmem] * n_out),
        scratch_shapes=[
            pltpu.VMEM((2, A, B, C), jnp.float32),
            pltpu.VMEM((2, SLOTS, B, C), jnp.float32),
            pltpu.VMEM((4, SLOTS, A, B, C), jnp.float32),
            pltpu.VMEM((7, A, B, C), jnp.float32),
            pltpu.VMEM((A, B, C), jnp.float32),
            pltpu.SemaphoreType.DMA((SLOTS, 6)),
            pltpu.SemaphoreType.DMA((SLOTS, 6)),
        ],
        compiler_params=pltpu.CompilerParams(collective_id=ident, has_side_effects=True),
    )(*level_args)


def gather_kernel(sizes, row_ref, out_ref, first, dense, second, send_sem, recv_sem):
    index = [lax.axis_index(axis) for axis in AXES]
    nx, ny, nz = sizes

    def device(axis, step):
        return tuple(
            lax.rem(index[a] + step, sizes[a]) if a == axis else index[a] for a in range(3)
        )

    barrier = pltpu.get_barrier_semaphore()
    partners = []
    for axis in (2, 1, 0):
        partners.append([device(axis, step) for step in range(1, sizes[axis])])
    for group in partners:
        for peer in group:
            pl.semaphore_signal(barrier, inc=1, device_id=peer, device_id_type=MESH)
    pl.semaphore_wait(barrier, sum(len(group) for group in partners))

    stages = ((row_ref, first, 2), (dense, second, 1), (second, out_ref, 0))
    for stage, (source, target, axis) in enumerate(stages):
        mine = index[axis]
        waits = []
        for step in range(1, sizes[axis]):
            peer = device(axis, step)
            copy = pltpu.make_async_remote_copy(
                src_ref=source,
                dst_ref=target.at[mine],
                send_sem=send_sem.at[stage, step],
                recv_sem=recv_sem.at[stage, mine],
                device_id=peer,
                device_id_type=MESH,
            )
            copy.start()
            origin = lax.rem(mine + sizes[axis] - step, sizes[axis])
            incoming = pltpu.make_async_remote_copy(
                src_ref=source,
                dst_ref=target.at[origin],
                send_sem=send_sem.at[stage, step],
                recv_sem=recv_sem.at[stage, origin],
                device_id=peer,
                device_id_type=MESH,
            )
            waits.append((copy, incoming))
        if stage == 0:
            target[mine] = source[...]
        else:
            target[mine] = source[...]
        for copy, incoming in waits:
            copy.wait_send()
            incoming.wait_recv()
        if stage == 0:
            for z in range(nz):
                dense[z : z + 1, :] = first[z]


def gather_bottom(packed):
    sizes = tuple(lax.axis_size(axis) for axis in AXES)
    nx, ny, nz = sizes
    width = packed.size
    lanes = -(-width // 128) * 128
    row = jnp.pad(packed.reshape(1, width), ((0, 0), (0, lanes - width)))
    vmem = pl.BlockSpec(memory_space=pltpu.VMEM)
    top = max(sizes)
    whole = pl.pallas_call(
        functools.partial(gather_kernel, sizes),
        out_shape=jax.ShapeDtypeStruct((nx, ny, nz, lanes), jnp.float32),
        in_specs=[vmem],
        out_specs=vmem,
        scratch_shapes=[
            pltpu.VMEM((nz, 1, lanes), jnp.float32),
            pltpu.VMEM((nz, lanes), jnp.float32),
            pltpu.VMEM((ny, nz, lanes), jnp.float32),
            pltpu.SemaphoreType.DMA((3, top)),
            pltpu.SemaphoreType.DMA((3, top)),
        ],
        compiler_params=pltpu.CompilerParams(collective_id=64, has_side_effects=True),
    )(row)
    whole = whole[..., :width].reshape((nx, ny, nz) + packed.shape)
    whole = whole.transpose(3, 0, 4, 1, 5, 2, 6)
    return whole.reshape(
        (packed.shape[0],) + tuple(n * s for n, s in zip(sizes, packed.shape[1:]))
    )


def split_padded(padded):
    return (
        padded[:-2, 1:-1, 1:-1],
        padded[2:, 1:-1, 1:-1],
        padded[1:-1, :-2, 1:-1],
        padded[1:-1, 2:, 1:-1],
        padded[1:-1, 1:-1, :-2],
        padded[1:-1, 1:-1, 2:],
    )


def zero_pad(field):
    return split_padded(jnp.pad(field, 1))


def level_operator(beta_level, alpha_level, beta_sides, shift):
    coeffs = tuple((0.5 * (beta_level + other) for other in beta_sides))
    diagonal = shift * alpha_level
    for coeff in coeffs:
        diagonal = diagonal + coeff
    return (coeffs, diagonal)


def apply_operator(field, operator, pad_field):
    coeffs, diagonal = operator
    others = pad_field(field)
    total = coeffs[0] * others[0]
    for index in range(1, 6):
        total = total + coeffs[index] * others[index]
    return diagonal * field - total


def chebyshev(iterate, rhs_level, operator, count, lower, zero_start, pad_field):
    diagonal = operator[1]
    center = (UPPER_EIG + lower) / 2.0
    half_width = (UPPER_EIG - lower) / 2.0
    sigma_ratio = center / half_width
    rho_old = 1.0 / sigma_ratio
    if zero_start:
        remain = rhs_level
    else:
        remain = rhs_level - apply_operator(iterate, operator, pad_field)
    update = remain / diagonal / center
    iterate = iterate + update
    for sweep_index in range(count - 1):
        remain = rhs_level - apply_operator(iterate, operator, pad_field)
        rho_new = 1.0 / (2.0 * sigma_ratio - rho_old)
        update = rho_new * rho_old * update + 2.0 * rho_new / half_width * (remain / diagonal)
        iterate = iterate + update
        rho_old = rho_new
    return iterate


def restrict_mean(field):
    first, second, third = field.shape
    blocks = field.reshape(first // 2, 2, second // 2, 2, third // 2, 2)
    return jnp.sum(blocks, axis=(1, 3, 5)) * 0.125


def prolong_copy(field):
    return jnp.repeat(jnp.repeat(jnp.repeat(field, 2, axis=0), 2, axis=1), 2, axis=2)


def shards(right_side, alpha_coef, beta_coef):
    betas = [beta_coef]
    alphas = [alpha_coef]
    rhs_levels = [right_side]
    smoothed = []
    for level in range(LEVELS):
        iterate, coarse_rhs, coarse_beta, coarse_alpha = smooth(
            (rhs_levels[level], betas[level], alphas[level]),
            SHIFT_BASE * 4.0**level,
            SWEEPS,
            SMOOTH_LOWER,
            True,
            True,
            True,
        )
        smoothed.append(iterate)
        rhs_levels.append(coarse_rhs)
        betas.append(coarse_beta)
        alphas.append(coarse_alpha)
    coarse_rhs = rhs_levels[LEVELS]
    local_shape = coarse_rhs.shape
    packed = jnp.stack([coarse_rhs, betas[LEVELS], alphas[LEVELS]])
    index_x = lax.axis_index("gx")
    index_y = lax.axis_index("gy")
    index_z = lax.axis_index("gz")
    packed = gather_bottom(packed)
    whole_rhs = packed[0]
    whole_beta = packed[1]
    whole_alpha = packed[2]
    bottom_operator = level_operator(
        whole_beta, whole_alpha, zero_pad(whole_beta), SHIFT_BASE * 4.0**LEVELS
    )
    whole_correction = chebyshev(
        jnp.zeros_like(whole_rhs), whole_rhs, bottom_operator, BOTTOM, BOTTOM_LOWER, True, zero_pad
    )
    starts = (index_x * local_shape[0], index_y * local_shape[1], index_z * local_shape[2])
    correction = lax.dynamic_slice(whole_correction, starts, local_shape)
    for level in range(LEVELS - 1, -1, -1):
        start_field = smoothed[level] + prolong_copy(correction)
        outs = smooth(
            (rhs_levels[level], betas[level], alphas[level], start_field),
            SHIFT_BASE * 4.0**level,
            SWEEPS,
            SMOOTH_LOWER,
            False,
            level == 0,
        )
        correction = outs[0]
    residual_field = outs[1]
    return (correction, residual_field)


def solution(mesh):
    in_specs = (P("gx", "gy", "gz"), P("gx", "gy", "gz"), P("gx", "gy", "gz"))
    out_specs = (P("gx", "gy", "gz"), P("gx", "gy", "gz"))
    return jax.shard_map(shards, mesh=mesh, in_specs=in_specs, out_specs=out_specs, check_vma=False)
```

```python
import functools

import jax
import jax.numpy as jnp
from jax import lax
from jax.experimental import pallas as pl
from jax.experimental.pallas import tpu as pltpu
from jax.sharding import PartitionSpec as P

MESH = pl.DeviceIdType.MESH
AXES = ("gx", "gy", "gz")
SLOTS = 3

LEVELS = 3
SWEEPS = 4
BOTTOM = 12


SHIFT_BASE = 0.01
UPPER_EIG = 2.0
SMOOTH_LOWER = 0.25
BOTTOM_LOWER = 0.02


def level_kernel(cfg, *refs):
    sizes, shift, count, lower, zero_start, residual, restrict = cfg
    n_in = 3 if zero_start else 4
    b_ref, beta_ref, alpha_ref = refs[0:3]
    v0_ref = None if zero_start else refs[3]
    n_out = 1 + (1 if residual and not restrict else 0) + (3 if restrict else 0)
    outs = refs[n_in : n_in + n_out]
    fld, xh, yh, zh, zsend, coef, dbuf, send_sem, recv_sem = refs[n_in + len(outs) :]
    A, B, C = b_ref.shape
    index = [lax.axis_index(axis) for axis in AXES]
    targets = []
    for k in range(6):
        axis = k // 2
        if k % 2 == 0:
            exists = index[axis] > 0
            other = index[axis] - 1
        else:
            exists = index[axis] < sizes[axis] - 1
            other = index[axis] + 1
        device = tuple(other if a == axis else index[a] for a in range(3))
        targets.append((exists, device))

    def halo(h, slot):
        if h < 2:
            return xh.at[h, slot]
        return yh.at[h - 2, slot] if h < 4 else zh.at[h - 4, slot]

    picks = lax.broadcasted_iota(jnp.int32, (8, C), 0)
    lanes = lax.broadcasted_iota(jnp.int32, (8, C), 1)
    selector = jnp.where(
        (picks == 0) & (lanes == 0), 1.0, jnp.where((picks == 1) & (lanes == C - 1), 1.0, 0.0)
    ).astype(jnp.float32)

    barrier = pltpu.get_barrier_semaphore()
    total = jnp.int32(0)
    for exists, device in targets:

        @pl.when(exists)
        def _():
            pl.semaphore_signal(barrier, inc=1, device_id=device, device_id_type=MESH)

        total = total + exists.astype(jnp.int32)
    for h, (exists, device) in enumerate(targets):

        @pl.when(jnp.logical_not(exists))
        def _():
            for slot in range(SLOTS):
                buf = halo(h, slot)
                buf[...] = jnp.zeros(buf.shape, buf.dtype)

    if restrict:
        coarse_rows = (
            lax.broadcasted_iota(jnp.int32, (B // 2, B), 1) // 2
            == lax.broadcasted_iota(jnp.int32, (B // 2, B), 0)
        ).astype(jnp.float32)
        coarse_cols = (
            lax.broadcasted_iota(jnp.int32, (C, C // 2), 0) // 2
            == lax.broadcasted_iota(jnp.int32, (C, C // 2), 1)
        ).astype(jnp.float32)

        def restrict_into(src, dst, scale):
            for i in range(A // 2):
                pair = src[2 * i] + src[2 * i + 1]
                half = jnp.dot(
                    coarse_rows, pair, precision=lax.Precision.HIGHEST,
                    preferred_element_type=jnp.float32,
                )
                dst[i] = scale * jnp.dot(
                    half, coarse_cols, precision=lax.Precision.HIGHEST,
                    preferred_element_type=jnp.float32,
                )

        restrict_into(beta_ref, outs[2], 0.125)
        restrict_into(alpha_ref, outs[3], 0.125)
    pl.semaphore_wait(barrier, total)

    def exchange_start(src, slot):
        block = src[...].reshape(A * B, C)
        zsend[slot] = lax.dot_general(
            selector, block, (((1,), (1,)), ((), ())),
            precision=lax.Precision.HIGHEST, preferred_element_type=jnp.float32,
        )
        sources = (src.at[0], src.at[A - 1], src, src, zsend.at[slot], zsend.at[slot])
        waits = []
        for k, (exists, device) in enumerate(targets):
            copy = pltpu.make_async_remote_copy(
                src_ref=sources[k],
                dst_ref=halo(k ^ 1, slot),
                send_sem=send_sem.at[slot, k],
                recv_sem=recv_sem.at[slot, k ^ 1],
                device_id=device,
                device_id_type=MESH,
            )
            pl.when(exists)(copy.start)
            incoming = pltpu.make_async_remote_copy(
                src_ref=sources[k ^ 1],
                dst_ref=halo(k, slot),
                send_sem=send_sem.at[slot, k ^ 1],
                recv_sem=recv_sem.at[slot, k],
                device_id=device,
                device_id_type=MESH,
            )
            waits.append((exists, copy.wait_send))
            waits.append((exists, incoming.wait_recv))
        return waits

    def exchange_finish(waits):
        for exists, wait in waits:
            pl.when(exists)(wait)

    def exchange(src, slot):
        exchange_finish(exchange_start(src, slot))

    rows = lax.broadcasted_iota(jnp.int32, (B, C), 0)
    cols = lax.broadcasted_iota(jnp.int32, (B, C), 1)

    def z_columns(slot):
        return (jnp.transpose(zh[0, slot]), jnp.transpose(zh[1, slot]))

    def sides(src, i, slot, columns):
        here = src[i]
        lower_x = src[i - 1] if i > 0 else xh[0, slot]
        upper_x = src[i + 1] if i < A - 1 else xh[1, slot]
        lower_y = jnp.where(rows == 0, pltpu.roll(yh[0, slot, i], 1, 0), pltpu.roll(here, 1, 0))
        upper_y = jnp.where(
            rows == B - 1, pltpu.roll(yh[1, slot, i], B - 1, 0), pltpu.roll(here, B - 1, 0)
        )
        lower_z = jnp.where(cols == 0, columns[0][i * B : (i + 1) * B, 1:2], pltpu.roll(here, 1, 1))
        upper_z = jnp.where(
            cols == C - 1, columns[1][i * B : (i + 1) * B, 0:1], pltpu.roll(here, C - 1, 1)
        )
        return here, (lower_x, upper_x, lower_y, upper_y, lower_z, upper_z)

    exchanges = [0]

    def next_slot():
        slot = exchanges[0] % SLOTS
        exchanges[0] += 1
        return slot

    slot = next_slot()
    if zero_start:
        exchange(beta_ref, slot)
    else:
        first_slot = next_slot()
        first_waits = exchange_start(v0_ref, first_slot)
        exchange(beta_ref, slot)
    columns = z_columns(slot)
    for i in range(A):
        here, others = sides(beta_ref, i, slot, columns)
        diagonal = shift * alpha_ref[i]
        for k in range(6):
            face = 0.5 * (here + others[k])
            coef[k, i] = face
            diagonal = diagonal + face
        coef[6, i] = diagonal

    def apply_rows(src, slot, i, columns):
        here, others = sides(src, i, slot, columns)
        acc = coef[0, i] * others[0]
        for k in range(1, 6):
            acc = acc + coef[k, i] * others[k]
        return b_ref[i] - (coef[6, i] * here - acc)

    center = (UPPER_EIG + lower) / 2.0
    half_width = (UPPER_EIG - lower) / 2.0
    sigma_ratio = center / half_width
    rho_old = 1.0 / sigma_ratio
    current = 0
    if zero_start:
        for i in range(A):
            update = b_ref[i] / coef[6, i] / center
            dbuf[i] = update
            fld[current, i] = update
    else:
        exchange_finish(first_waits)
        columns = z_columns(first_slot)
        for i in range(A):
            remain = apply_rows(v0_ref, first_slot, i, columns)
            update = remain / coef[6, i] / center
            dbuf[i] = update
            fld[current, i] = v0_ref[i] + update
    for sweep in range(count - 1):
        rho_new = 1.0 / (2.0 * sigma_ratio - rho_old)
        slot = next_slot()
        src = fld.at[current]
        exchange(src, slot)
        last = sweep == count - 2
        dst = outs[0] if last else fld.at[1 - current]
        columns = z_columns(slot)
        for i in range(A):
            remain = apply_rows(src, slot, i, columns)
            update = (rho_new * rho_old) * dbuf[i] + (2.0 * rho_new / half_width) * (
                remain / coef[6, i]
            )
            dbuf[i] = update
            dst[i] = src[i] + update
        rho_old = rho_new
        current = 1 - current
    if residual:
        slot = next_slot()
        exchange(outs[0], slot)
        remain_ref = dbuf if restrict else outs[1]
        columns = z_columns(slot)
        for i in range(A):
            remain_ref[i] = apply_rows(outs[0], slot, i, columns)
        if restrict:
            restrict_into(dbuf, outs[1], 0.5)


KERNELS = {}


def smooth(level_args, shift, count, lower, zero_start, residual, restrict=False):
    A, B, C = level_args[0].shape
    sizes = tuple(lax.axis_size(axis) for axis in AXES)
    cfg = (sizes, shift, count, lower, zero_start, residual, restrict)
    ident = KERNELS.setdefault((A, B, C) + cfg[1:], len(KERNELS))
    vmem = pl.BlockSpec(memory_space=pltpu.VMEM)
    block = jax.ShapeDtypeStruct((A, B, C), jnp.float32)
    coarse = jax.ShapeDtypeStruct((A // 2, B // 2, C // 2), jnp.float32)
    shapes = [block] + ([block] if residual and not restrict else []) + ([coarse] * 3 if restrict else [])
    n_out = len(shapes)
    return pl.pallas_call(
        functools.partial(level_kernel, cfg),
        out_shape=tuple(shapes),
        in_specs=[vmem] * len(level_args),
        out_specs=tuple([vmem] * n_out),
        scratch_shapes=[
            pltpu.VMEM((2, A, B, C), jnp.float32),
            pltpu.VMEM((2, SLOTS, B, C), jnp.float32),
            pltpu.VMEM((2, SLOTS, A, B, C), jnp.float32),
            pltpu.VMEM((2, SLOTS, 8, A * B), jnp.float32),
            pltpu.VMEM((SLOTS, 8, A * B), jnp.float32),
            pltpu.VMEM((7, A, B, C), jnp.float32),
            pltpu.VMEM((A, B, C), jnp.float32),
            pltpu.SemaphoreType.DMA((SLOTS, 6)),
            pltpu.SemaphoreType.DMA((SLOTS, 6)),
        ],
        compiler_params=pltpu.CompilerParams(collective_id=ident, has_side_effects=True),
    )(*level_args)


def gather_kernel(sizes, row_ref, out_ref, first, dense, second, send_sem, recv_sem):
    index = [lax.axis_index(axis) for axis in AXES]
    nx, ny, nz = sizes

    def device(axis, step):
        return tuple(
            lax.rem(index[a] + step, sizes[a]) if a == axis else index[a] for a in range(3)
        )

    barrier = pltpu.get_barrier_semaphore()
    partners = []
    for axis in (2, 1, 0):
        partners.append([device(axis, step) for step in range(1, sizes[axis])])
    for group in partners:
        for peer in group:
            pl.semaphore_signal(barrier, inc=1, device_id=peer, device_id_type=MESH)
    pl.semaphore_wait(barrier, sum(len(group) for group in partners))

    stages = ((row_ref, first, 2), (dense, second, 1), (second, out_ref, 0))
    for stage, (source, target, axis) in enumerate(stages):
        mine = index[axis]
        waits = []
        for step in range(1, sizes[axis]):
            peer = device(axis, step)
            copy = pltpu.make_async_remote_copy(
                src_ref=source,
                dst_ref=target.at[mine],
                send_sem=send_sem.at[stage, step],
                recv_sem=recv_sem.at[stage, mine],
                device_id=peer,
                device_id_type=MESH,
            )
            copy.start()
            origin = lax.rem(mine + sizes[axis] - step, sizes[axis])
            incoming = pltpu.make_async_remote_copy(
                src_ref=source,
                dst_ref=target.at[origin],
                send_sem=send_sem.at[stage, step],
                recv_sem=recv_sem.at[stage, origin],
                device_id=peer,
                device_id_type=MESH,
            )
            waits.append((copy, incoming))
        if stage == 0:
            target[mine] = source[...]
        else:
            target[mine] = source[...]
        for copy, incoming in waits:
            copy.wait_send()
            incoming.wait_recv()
        if stage == 0:
            for z in range(nz):
                dense[z : z + 1, :] = first[z]


def gather_bottom(packed):
    sizes = tuple(lax.axis_size(axis) for axis in AXES)
    nx, ny, nz = sizes
    width = packed.size
    lanes = -(-width // 128) * 128
    row = jnp.pad(packed.reshape(1, width), ((0, 0), (0, lanes - width)))
    vmem = pl.BlockSpec(memory_space=pltpu.VMEM)
    top = max(sizes)
    whole = pl.pallas_call(
        functools.partial(gather_kernel, sizes),
        out_shape=jax.ShapeDtypeStruct((nx, ny, nz, lanes), jnp.float32),
        in_specs=[vmem],
        out_specs=vmem,
        scratch_shapes=[
            pltpu.VMEM((nz, 1, lanes), jnp.float32),
            pltpu.VMEM((nz, lanes), jnp.float32),
            pltpu.VMEM((ny, nz, lanes), jnp.float32),
            pltpu.SemaphoreType.DMA((3, top)),
            pltpu.SemaphoreType.DMA((3, top)),
        ],
        compiler_params=pltpu.CompilerParams(collective_id=64, has_side_effects=True),
    )(row)
    whole = whole[..., :width].reshape((nx, ny, nz) + packed.shape)
    whole = whole.transpose(3, 0, 4, 1, 5, 2, 6)
    return whole.reshape(
        (packed.shape[0],) + tuple(n * s for n, s in zip(sizes, packed.shape[1:]))
    )


def split_padded(padded):
    return (
        padded[:-2, 1:-1, 1:-1],
        padded[2:, 1:-1, 1:-1],
        padded[1:-1, :-2, 1:-1],
        padded[1:-1, 2:, 1:-1],
        padded[1:-1, 1:-1, :-2],
        padded[1:-1, 1:-1, 2:],
    )


def zero_pad(field):
    return split_padded(jnp.pad(field, 1))


def level_operator(beta_level, alpha_level, beta_sides, shift):
    coeffs = tuple((0.5 * (beta_level + other) for other in beta_sides))
    diagonal = shift * alpha_level
    for coeff in coeffs:
        diagonal = diagonal + coeff
    return (coeffs, diagonal)


def apply_operator(field, operator, pad_field):
    coeffs, diagonal = operator
    others = pad_field(field)
    total = coeffs[0] * others[0]
    for index in range(1, 6):
        total = total + coeffs[index] * others[index]
    return diagonal * field - total


def chebyshev(iterate, rhs_level, operator, count, lower, zero_start, pad_field):
    diagonal = operator[1]
    center = (UPPER_EIG + lower) / 2.0
    half_width = (UPPER_EIG - lower) / 2.0
    sigma_ratio = center / half_width
    rho_old = 1.0 / sigma_ratio
    if zero_start:
        remain = rhs_level
    else:
        remain = rhs_level - apply_operator(iterate, operator, pad_field)
    update = remain / diagonal / center
    iterate = iterate + update
    for sweep_index in range(count - 1):
        remain = rhs_level - apply_operator(iterate, operator, pad_field)
        rho_new = 1.0 / (2.0 * sigma_ratio - rho_old)
        update = rho_new * rho_old * update + 2.0 * rho_new / half_width * (remain / diagonal)
        iterate = iterate + update
        rho_old = rho_new
    return iterate


def restrict_mean(field):
    first, second, third = field.shape
    blocks = field.reshape(first // 2, 2, second // 2, 2, third // 2, 2)
    return jnp.sum(blocks, axis=(1, 3, 5)) * 0.125


def prolong_copy(field):
    return jnp.repeat(jnp.repeat(jnp.repeat(field, 2, axis=0), 2, axis=1), 2, axis=2)


def shards(right_side, alpha_coef, beta_coef):
    betas = [beta_coef]
    alphas = [alpha_coef]
    rhs_levels = [right_side]
    smoothed = []
    for level in range(LEVELS):
        iterate, coarse_rhs, coarse_beta, coarse_alpha = smooth(
            (rhs_levels[level], betas[level], alphas[level]),
            SHIFT_BASE * 4.0**level,
            SWEEPS,
            SMOOTH_LOWER,
            True,
            True,
            True,
        )
        smoothed.append(iterate)
        rhs_levels.append(coarse_rhs)
        betas.append(coarse_beta)
        alphas.append(coarse_alpha)
    coarse_rhs = rhs_levels[LEVELS]
    local_shape = coarse_rhs.shape
    packed = jnp.stack([coarse_rhs, betas[LEVELS], alphas[LEVELS]])
    index_x = lax.axis_index("gx")
    index_y = lax.axis_index("gy")
    index_z = lax.axis_index("gz")
    packed = gather_bottom(packed)
    whole_rhs = packed[0]
    whole_beta = packed[1]
    whole_alpha = packed[2]
    bottom_operator = level_operator(
        whole_beta, whole_alpha, zero_pad(whole_beta), SHIFT_BASE * 4.0**LEVELS
    )
    whole_correction = chebyshev(
        jnp.zeros_like(whole_rhs), whole_rhs, bottom_operator, BOTTOM, BOTTOM_LOWER, True, zero_pad
    )
    starts = (index_x * local_shape[0], index_y * local_shape[1], index_z * local_shape[2])
    correction = lax.dynamic_slice(whole_correction, starts, local_shape)
    for level in range(LEVELS - 1, -1, -1):
        start_field = smoothed[level] + prolong_copy(correction)
        outs = smooth(
            (rhs_levels[level], betas[level], alphas[level], start_field),
            SHIFT_BASE * 4.0**level,
            SWEEPS,
            SMOOTH_LOWER,
            False,
            level == 0,
        )
        correction = outs[0]
    residual_field = outs[1]
    return (correction, residual_field)


def solution(mesh):
    in_specs = (P("gx", "gy", "gz"), P("gx", "gy", "gz"), P("gx", "gy", "gz"))
    out_specs = (P("gx", "gy", "gz"), P("gx", "gy", "gz"))
    return jax.shard_map(shards, mesh=mesh, in_specs=in_specs, out_specs=out_specs, check_vma=False)
```

```python
import functools

import jax
import jax.numpy as jnp
from jax import lax
from jax.experimental import pallas as pl
from jax.experimental.pallas import tpu as pltpu
from jax.sharding import PartitionSpec as P

MESH = pl.DeviceIdType.MESH
AXES = ("gx", "gy", "gz")
SLOTS = 3

LEVELS = 3
SWEEPS = 4
BOTTOM = 12


SHIFT_BASE = 0.01
UPPER_EIG = 2.0
SMOOTH_LOWER = 0.25
BOTTOM_LOWER = 0.02


def level_kernel(cfg, *refs):
    sizes, shift, count, lower, zero_start, residual, restrict = cfg
    n_in = 3 if zero_start else 4
    b_ref, beta_ref, alpha_ref = refs[0:3]
    v0_ref = None if zero_start else refs[3]
    n_out = 1 + (1 if residual and not restrict else 0) + (3 if restrict else 0)
    outs = refs[n_in : n_in + n_out]
    fld, xh, yh, zh, zsend, coef, dbuf, send_sem, recv_sem = refs[n_in + len(outs) :]
    A, B, C = b_ref.shape
    index = [lax.axis_index(axis) for axis in AXES]
    targets = []
    for k in range(6):
        axis = k // 2
        if k % 2 == 0:
            exists = index[axis] > 0
            other = index[axis] - 1
        else:
            exists = index[axis] < sizes[axis] - 1
            other = index[axis] + 1
        device = tuple(other if a == axis else index[a] for a in range(3))
        targets.append((exists, device))

    def halo(h, slot):
        if h < 2:
            return xh.at[h, slot]
        return yh.at[h - 2, slot] if h < 4 else zh.at[h - 4, slot]

    picks = lax.broadcasted_iota(jnp.int32, (8, C), 0)
    lanes = lax.broadcasted_iota(jnp.int32, (8, C), 1)
    selector = jnp.where(
        (picks == 0) & (lanes == 0), 1.0, jnp.where((picks == 1) & (lanes == C - 1), 1.0, 0.0)
    ).astype(jnp.float32)

    barrier = pltpu.get_barrier_semaphore()
    total = jnp.int32(0)
    for exists, device in targets:

        @pl.when(exists)
        def _():
            pl.semaphore_signal(barrier, inc=1, device_id=device, device_id_type=MESH)

        total = total + exists.astype(jnp.int32)
    for h, (exists, device) in enumerate(targets):

        @pl.when(jnp.logical_not(exists))
        def _():
            for slot in range(SLOTS):
                buf = halo(h, slot)
                buf[...] = jnp.zeros(buf.shape, buf.dtype)

    if restrict:
        coarse_rows = (
            lax.broadcasted_iota(jnp.int32, (B // 2, B), 1) // 2
            == lax.broadcasted_iota(jnp.int32, (B // 2, B), 0)
        ).astype(jnp.float32)
        coarse_cols = (
            lax.broadcasted_iota(jnp.int32, (C, C // 2), 0) // 2
            == lax.broadcasted_iota(jnp.int32, (C, C // 2), 1)
        ).astype(jnp.float32)

        def restrict_into(src, dst, scale):
            for i in range(A // 2):
                pair = src[2 * i] + src[2 * i + 1]
                half = jnp.dot(
                    coarse_rows, pair, precision=lax.Precision.HIGHEST,
                    preferred_element_type=jnp.float32,
                )
                dst[i] = scale * jnp.dot(
                    half, coarse_cols, precision=lax.Precision.HIGHEST,
                    preferred_element_type=jnp.float32,
                )

        restrict_into(beta_ref, outs[2], 0.125)
        restrict_into(alpha_ref, outs[3], 0.125)
    pl.semaphore_wait(barrier, total)

    def exchange_start(src, slot):
        block = src[...].reshape(A * B, C)
        zsend[slot] = lax.dot_general(
            selector, block, (((1,), (1,)), ((), ())),
            precision=lax.Precision.HIGHEST, preferred_element_type=jnp.float32,
        )
        sources = (
            src.at[0], src.at[A - 1],
            src.at[:, 0:8, :], src.at[:, B - 8 : B, :],
            zsend.at[slot], zsend.at[slot],
        )
        waits = []
        for k, (exists, device) in enumerate(targets):
            copy = pltpu.make_async_remote_copy(
                src_ref=sources[k],
                dst_ref=halo(k ^ 1, slot),
                send_sem=send_sem.at[slot, k],
                recv_sem=recv_sem.at[slot, k ^ 1],
                device_id=device,
                device_id_type=MESH,
            )
            pl.when(exists)(copy.start)
            incoming = pltpu.make_async_remote_copy(
                src_ref=sources[k ^ 1],
                dst_ref=halo(k, slot),
                send_sem=send_sem.at[slot, k ^ 1],
                recv_sem=recv_sem.at[slot, k],
                device_id=device,
                device_id_type=MESH,
            )
            waits.append((exists, copy.wait_send))
            waits.append((exists, incoming.wait_recv))
        return waits

    def exchange_finish(waits):
        for exists, wait in waits:
            pl.when(exists)(wait)

    def exchange(src, slot):
        exchange_finish(exchange_start(src, slot))

    rows = lax.broadcasted_iota(jnp.int32, (B, C), 0)
    cols = lax.broadcasted_iota(jnp.int32, (B, C), 1)

    def z_columns(slot):
        return (jnp.transpose(zh[0, slot]), jnp.transpose(zh[1, slot]))

    def sides(src, i, slot, columns):
        here = src[i]
        lower_x = src[i - 1] if i > 0 else xh[0, slot]
        upper_x = src[i + 1] if i < A - 1 else xh[1, slot]
        lower_y = jnp.where(rows == 0, yh[0, slot, i, 7:8, :], pltpu.roll(here, 1, 0))
        upper_y = jnp.where(rows == B - 1, yh[1, slot, i, 0:1, :], pltpu.roll(here, B - 1, 0))
        lower_z = jnp.where(cols == 0, columns[0][i * B : (i + 1) * B, 1:2], pltpu.roll(here, 1, 1))
        upper_z = jnp.where(
            cols == C - 1, columns[1][i * B : (i + 1) * B, 0:1], pltpu.roll(here, C - 1, 1)
        )
        return here, (lower_x, upper_x, lower_y, upper_y, lower_z, upper_z)

    exchanges = [0]

    def next_slot():
        slot = exchanges[0] % SLOTS
        exchanges[0] += 1
        return slot

    slot = next_slot()
    if zero_start:
        exchange(beta_ref, slot)
    else:
        first_slot = next_slot()
        first_waits = exchange_start(v0_ref, first_slot)
        exchange(beta_ref, slot)
    columns = z_columns(slot)
    for i in range(A):
        here, others = sides(beta_ref, i, slot, columns)
        diagonal = shift * alpha_ref[i]
        for k in range(6):
            face = 0.5 * (here + others[k])
            coef[k, i] = face
            diagonal = diagonal + face
        coef[6, i] = diagonal

    def apply_rows(src, slot, i, columns):
        here, others = sides(src, i, slot, columns)
        acc = coef[0, i] * others[0]
        for k in range(1, 6):
            acc = acc + coef[k, i] * others[k]
        return b_ref[i] - (coef[6, i] * here - acc)

    center = (UPPER_EIG + lower) / 2.0
    half_width = (UPPER_EIG - lower) / 2.0
    sigma_ratio = center / half_width
    rho_old = 1.0 / sigma_ratio
    current = 0
    if zero_start:
        for i in range(A):
            update = b_ref[i] / coef[6, i] / center
            dbuf[i] = update
            fld[current, i] = update
    else:
        exchange_finish(first_waits)
        columns = z_columns(first_slot)
        for i in range(A):
            remain = apply_rows(v0_ref, first_slot, i, columns)
            update = remain / coef[6, i] / center
            dbuf[i] = update
            fld[current, i] = v0_ref[i] + update
    for sweep in range(count - 1):
        rho_new = 1.0 / (2.0 * sigma_ratio - rho_old)
        slot = next_slot()
        src = fld.at[current]
        exchange(src, slot)
        last = sweep == count - 2
        dst = outs[0] if last else fld.at[1 - current]
        columns = z_columns(slot)
        for i in range(A):
            remain = apply_rows(src, slot, i, columns)
            update = (rho_new * rho_old) * dbuf[i] + (2.0 * rho_new / half_width) * (
                remain / coef[6, i]
            )
            dbuf[i] = update
            dst[i] = src[i] + update
        rho_old = rho_new
        current = 1 - current
    if residual:
        slot = next_slot()
        exchange(outs[0], slot)
        remain_ref = dbuf if restrict else outs[1]
        columns = z_columns(slot)
        for i in range(A):
            remain_ref[i] = apply_rows(outs[0], slot, i, columns)
        if restrict:
            restrict_into(dbuf, outs[1], 0.5)


KERNELS = {}


def smooth(level_args, shift, count, lower, zero_start, residual, restrict=False):
    A, B, C = level_args[0].shape
    sizes = tuple(lax.axis_size(axis) for axis in AXES)
    cfg = (sizes, shift, count, lower, zero_start, residual, restrict)
    ident = KERNELS.setdefault((A, B, C) + cfg[1:], len(KERNELS))
    vmem = pl.BlockSpec(memory_space=pltpu.VMEM)
    block = jax.ShapeDtypeStruct((A, B, C), jnp.float32)
    coarse = jax.ShapeDtypeStruct((A // 2, B // 2, C // 2), jnp.float32)
    shapes = [block] + ([block] if residual and not restrict else []) + ([coarse] * 3 if restrict else [])
    n_out = len(shapes)
    return pl.pallas_call(
        functools.partial(level_kernel, cfg),
        out_shape=tuple(shapes),
        in_specs=[vmem] * len(level_args),
        out_specs=tuple([vmem] * n_out),
        scratch_shapes=[
            pltpu.VMEM((2, A, B, C), jnp.float32),
            pltpu.VMEM((2, SLOTS, B, C), jnp.float32),
            pltpu.VMEM((2, SLOTS, A, 8, C), jnp.float32),
            pltpu.VMEM((2, SLOTS, 8, A * B), jnp.float32),
            pltpu.VMEM((SLOTS, 8, A * B), jnp.float32),
            pltpu.VMEM((7, A, B, C), jnp.float32),
            pltpu.VMEM((A, B, C), jnp.float32),
            pltpu.SemaphoreType.DMA((SLOTS, 6)),
            pltpu.SemaphoreType.DMA((SLOTS, 6)),
        ],
        compiler_params=pltpu.CompilerParams(collective_id=ident, has_side_effects=True),
    )(*level_args)


def gather_kernel(sizes, row_ref, out_ref, first, dense, second, send_sem, recv_sem):
    index = [lax.axis_index(axis) for axis in AXES]
    nx, ny, nz = sizes

    def device(axis, step):
        return tuple(
            lax.rem(index[a] + step, sizes[a]) if a == axis else index[a] for a in range(3)
        )

    barrier = pltpu.get_barrier_semaphore()
    partners = []
    for axis in (2, 1, 0):
        partners.append([device(axis, step) for step in range(1, sizes[axis])])
    for group in partners:
        for peer in group:
            pl.semaphore_signal(barrier, inc=1, device_id=peer, device_id_type=MESH)
    pl.semaphore_wait(barrier, sum(len(group) for group in partners))

    stages = ((row_ref, first, 2), (dense, second, 1), (second, out_ref, 0))
    for stage, (source, target, axis) in enumerate(stages):
        mine = index[axis]
        waits = []
        for step in range(1, sizes[axis]):
            peer = device(axis, step)
            copy = pltpu.make_async_remote_copy(
                src_ref=source,
                dst_ref=target.at[mine],
                send_sem=send_sem.at[stage, step],
                recv_sem=recv_sem.at[stage, mine],
                device_id=peer,
                device_id_type=MESH,
            )
            copy.start()
            origin = lax.rem(mine + sizes[axis] - step, sizes[axis])
            incoming = pltpu.make_async_remote_copy(
                src_ref=source,
                dst_ref=target.at[origin],
                send_sem=send_sem.at[stage, step],
                recv_sem=recv_sem.at[stage, origin],
                device_id=peer,
                device_id_type=MESH,
            )
            waits.append((copy, incoming))
        if stage == 0:
            target[mine] = source[...]
        else:
            target[mine] = source[...]
        for copy, incoming in waits:
            copy.wait_send()
            incoming.wait_recv()
        if stage == 0:
            for z in range(nz):
                dense[z : z + 1, :] = first[z]


def gather_bottom(packed):
    sizes = tuple(lax.axis_size(axis) for axis in AXES)
    nx, ny, nz = sizes
    width = packed.size
    lanes = -(-width // 128) * 128
    row = jnp.pad(packed.reshape(1, width), ((0, 0), (0, lanes - width)))
    vmem = pl.BlockSpec(memory_space=pltpu.VMEM)
    top = max(sizes)
    whole = pl.pallas_call(
        functools.partial(gather_kernel, sizes),
        out_shape=jax.ShapeDtypeStruct((nx, ny, nz, lanes), jnp.float32),
        in_specs=[vmem],
        out_specs=vmem,
        scratch_shapes=[
            pltpu.VMEM((nz, 1, lanes), jnp.float32),
            pltpu.VMEM((nz, lanes), jnp.float32),
            pltpu.VMEM((ny, nz, lanes), jnp.float32),
            pltpu.SemaphoreType.DMA((3, top)),
            pltpu.SemaphoreType.DMA((3, top)),
        ],
        compiler_params=pltpu.CompilerParams(collective_id=64, has_side_effects=True),
    )(row)
    whole = whole[..., :width].reshape((nx, ny, nz) + packed.shape)
    whole = whole.transpose(3, 0, 4, 1, 5, 2, 6)
    return whole.reshape(
        (packed.shape[0],) + tuple(n * s for n, s in zip(sizes, packed.shape[1:]))
    )


def split_padded(padded):
    return (
        padded[:-2, 1:-1, 1:-1],
        padded[2:, 1:-1, 1:-1],
        padded[1:-1, :-2, 1:-1],
        padded[1:-1, 2:, 1:-1],
        padded[1:-1, 1:-1, :-2],
        padded[1:-1, 1:-1, 2:],
    )


def zero_pad(field):
    return split_padded(jnp.pad(field, 1))


def level_operator(beta_level, alpha_level, beta_sides, shift):
    coeffs = tuple((0.5 * (beta_level + other) for other in beta_sides))
    diagonal = shift * alpha_level
    for coeff in coeffs:
        diagonal = diagonal + coeff
    return (coeffs, diagonal)


def apply_operator(field, operator, pad_field):
    coeffs, diagonal = operator
    others = pad_field(field)
    total = coeffs[0] * others[0]
    for index in range(1, 6):
        total = total + coeffs[index] * others[index]
    return diagonal * field - total


def chebyshev(iterate, rhs_level, operator, count, lower, zero_start, pad_field):
    diagonal = operator[1]
    center = (UPPER_EIG + lower) / 2.0
    half_width = (UPPER_EIG - lower) / 2.0
    sigma_ratio = center / half_width
    rho_old = 1.0 / sigma_ratio
    if zero_start:
        remain = rhs_level
    else:
        remain = rhs_level - apply_operator(iterate, operator, pad_field)
    update = remain / diagonal / center
    iterate = iterate + update
    for sweep_index in range(count - 1):
        remain = rhs_level - apply_operator(iterate, operator, pad_field)
        rho_new = 1.0 / (2.0 * sigma_ratio - rho_old)
        update = rho_new * rho_old * update + 2.0 * rho_new / half_width * (remain / diagonal)
        iterate = iterate + update
        rho_old = rho_new
    return iterate


def restrict_mean(field):
    first, second, third = field.shape
    blocks = field.reshape(first // 2, 2, second // 2, 2, third // 2, 2)
    return jnp.sum(blocks, axis=(1, 3, 5)) * 0.125


def prolong_copy(field):
    return jnp.repeat(jnp.repeat(jnp.repeat(field, 2, axis=0), 2, axis=1), 2, axis=2)


def shards(right_side, alpha_coef, beta_coef):
    betas = [beta_coef]
    alphas = [alpha_coef]
    rhs_levels = [right_side]
    smoothed = []
    for level in range(LEVELS):
        iterate, coarse_rhs, coarse_beta, coarse_alpha = smooth(
            (rhs_levels[level], betas[level], alphas[level]),
            SHIFT_BASE * 4.0**level,
            SWEEPS,
            SMOOTH_LOWER,
            True,
            True,
            True,
        )
        smoothed.append(iterate)
        rhs_levels.append(coarse_rhs)
        betas.append(coarse_beta)
        alphas.append(coarse_alpha)
    coarse_rhs = rhs_levels[LEVELS]
    local_shape = coarse_rhs.shape
    packed = jnp.stack([coarse_rhs, betas[LEVELS], alphas[LEVELS]])
    index_x = lax.axis_index("gx")
    index_y = lax.axis_index("gy")
    index_z = lax.axis_index("gz")
    packed = gather_bottom(packed)
    whole_rhs = packed[0]
    whole_beta = packed[1]
    whole_alpha = packed[2]
    bottom_operator = level_operator(
        whole_beta, whole_alpha, zero_pad(whole_beta), SHIFT_BASE * 4.0**LEVELS
    )
    whole_correction = chebyshev(
        jnp.zeros_like(whole_rhs), whole_rhs, bottom_operator, BOTTOM, BOTTOM_LOWER, True, zero_pad
    )
    starts = (index_x * local_shape[0], index_y * local_shape[1], index_z * local_shape[2])
    correction = lax.dynamic_slice(whole_correction, starts, local_shape)
    for level in range(LEVELS - 1, -1, -1):
        start_field = smoothed[level] + prolong_copy(correction)
        outs = smooth(
            (rhs_levels[level], betas[level], alphas[level], start_field),
            SHIFT_BASE * 4.0**level,
            SWEEPS,
            SMOOTH_LOWER,
            False,
            level == 0,
        )
        correction = outs[0]
    residual_field = outs[1]
    return (correction, residual_field)


def solution(mesh):
    in_specs = (P("gx", "gy", "gz"), P("gx", "gy", "gz"), P("gx", "gy", "gz"))
    out_specs = (P("gx", "gy", "gz"), P("gx", "gy", "gz"))
    return jax.shard_map(shards, mesh=mesh, in_specs=in_specs, out_specs=out_specs, check_vma=False)
```

```python
import functools

import jax
import jax.numpy as jnp
from jax import lax
from jax.experimental import pallas as pl
from jax.experimental.pallas import tpu as pltpu
from jax.sharding import PartitionSpec as P

MESH = pl.DeviceIdType.MESH
AXES = ("gx", "gy", "gz")
SLOTS = 3

LEVELS = 3
SWEEPS = 4
BOTTOM = 12


SHIFT_BASE = 0.01
UPPER_EIG = 2.0
SMOOTH_LOWER = 0.25
BOTTOM_LOWER = 0.02


def level_kernel(cfg, *refs):
    sizes, shift, count, lower, zero_start, residual, restrict = cfg
    n_in = 3 if zero_start else 4
    b_ref, beta_ref, alpha_ref = refs[0:3]
    v0_ref = None if zero_start else refs[3]
    n_out = 1 + (1 if residual and not restrict else 0) + (3 if restrict else 0)
    outs = refs[n_in : n_in + n_out]
    fld, xh, yh, zh, zsend, coef, dbuf, send_sem, recv_sem = refs[n_in + len(outs) :]
    A, B, C = b_ref.shape
    index = [lax.axis_index(axis) for axis in AXES]
    targets = []
    for k in range(6):
        axis = k // 2
        if k % 2 == 0:
            exists = index[axis] > 0
            other = index[axis] - 1
        else:
            exists = index[axis] < sizes[axis] - 1
            other = index[axis] + 1
        device = tuple(other if a == axis else index[a] for a in range(3))
        targets.append((exists, device))

    def halo(h, slot):
        if h < 2:
            return xh.at[h, slot]
        return yh.at[h - 2, slot] if h < 4 else zh.at[h - 4, slot]

    picks = lax.broadcasted_iota(jnp.int32, (8, C), 0)
    lanes = lax.broadcasted_iota(jnp.int32, (8, C), 1)
    selector = jnp.where(
        (picks == 0) & (lanes == 0), 1.0, jnp.where((picks == 1) & (lanes == C - 1), 1.0, 0.0)
    ).astype(jnp.float32)

    barrier = pltpu.get_barrier_semaphore()
    total = jnp.int32(0)
    for exists, device in targets:

        @pl.when(exists)
        def _():
            pl.semaphore_signal(barrier, inc=1, device_id=device, device_id_type=MESH)

        total = total + exists.astype(jnp.int32)
    for h, (exists, device) in enumerate(targets):

        @pl.when(jnp.logical_not(exists))
        def _():
            for slot in range(SLOTS):
                buf = halo(h, slot)
                buf[...] = jnp.zeros(buf.shape, buf.dtype)

    if restrict:
        coarse_rows = (
            lax.broadcasted_iota(jnp.int32, (B // 2, B), 1) // 2
            == lax.broadcasted_iota(jnp.int32, (B // 2, B), 0)
        ).astype(jnp.float32)
        coarse_cols = (
            lax.broadcasted_iota(jnp.int32, (C, C // 2), 0) // 2
            == lax.broadcasted_iota(jnp.int32, (C, C // 2), 1)
        ).astype(jnp.float32)

        def restrict_into(src, dst, scale):
            for i in range(A // 2):
                pair = src[2 * i] + src[2 * i + 1]
                half = jnp.dot(
                    coarse_rows, pair, precision=lax.Precision.HIGHEST,
                    preferred_element_type=jnp.float32,
                )
                dst[i] = scale * jnp.dot(
                    half, coarse_cols, precision=lax.Precision.HIGHEST,
                    preferred_element_type=jnp.float32,
                )

        restrict_into(beta_ref, outs[2], 0.125)
        restrict_into(alpha_ref, outs[3], 0.125)
    pl.semaphore_wait(barrier, total)

    def exchange_start(src, slot):
        block = src[...].reshape(A * B, C)
        zsend[slot] = lax.dot_general(
            selector, block, (((1,), (1,)), ((), ())),
            precision=lax.Precision.HIGHEST, preferred_element_type=jnp.float32,
        )
        sources = (
            src.at[0], src.at[A - 1],
            src.at[:, 0:8, :], src.at[:, B - 8 : B, :],
            zsend.at[slot], zsend.at[slot],
        )
        waits = []
        for k, (exists, device) in enumerate(targets):
            copy = pltpu.make_async_remote_copy(
                src_ref=sources[k],
                dst_ref=halo(k ^ 1, slot),
                send_sem=send_sem.at[slot, k],
                recv_sem=recv_sem.at[slot, k ^ 1],
                device_id=device,
                device_id_type=MESH,
            )
            pl.when(exists)(copy.start)
            incoming = pltpu.make_async_remote_copy(
                src_ref=sources[k ^ 1],
                dst_ref=halo(k, slot),
                send_sem=send_sem.at[slot, k ^ 1],
                recv_sem=recv_sem.at[slot, k],
                device_id=device,
                device_id_type=MESH,
            )
            waits.append((exists, copy.wait_send))
            waits.append((exists, incoming.wait_recv))
        return waits

    def exchange_finish(waits):
        for exists, wait in waits:
            pl.when(exists)(wait)

    def exchange(src, slot):
        exchange_finish(exchange_start(src, slot))

    rows = lax.broadcasted_iota(jnp.int32, (B, C), 0)
    cols = lax.broadcasted_iota(jnp.int32, (B, C), 1)

    def z_columns(slot):
        return (jnp.transpose(zh[0, slot]), jnp.transpose(zh[1, slot]))

    def sides(src, i, slot, columns):
        here = src[i]
        lower_x = src[i - 1] if i > 0 else xh[0, slot]
        upper_x = src[i + 1] if i < A - 1 else xh[1, slot]
        lower_y = jnp.where(rows == 0, yh[0, slot, i, 7:8, :], pltpu.roll(here, 1, 0))
        upper_y = jnp.where(rows == B - 1, yh[1, slot, i, 0:1, :], pltpu.roll(here, B - 1, 0))
        lower_z = jnp.where(cols == 0, columns[0][i * B : (i + 1) * B, 1:2], pltpu.roll(here, 1, 1))
        upper_z = jnp.where(
            cols == C - 1, columns[1][i * B : (i + 1) * B, 0:1], pltpu.roll(here, C - 1, 1)
        )
        return here, (lower_x, upper_x, lower_y, upper_y, lower_z, upper_z)

    exchanges = [0]

    def next_slot():
        slot = exchanges[0] % SLOTS
        exchanges[0] += 1
        return slot

    slot = next_slot()
    if zero_start:
        exchange(beta_ref, slot)
    else:
        first_slot = next_slot()
        first_waits = exchange_start(v0_ref, first_slot)
        exchange(beta_ref, slot)
    columns = z_columns(slot)
    for i in range(A):
        here, others = sides(beta_ref, i, slot, columns)
        diagonal = shift * alpha_ref[i]
        for k in range(6):
            face = 0.5 * (here + others[k])
            coef[k, i] = face
            diagonal = diagonal + face
        coef[6, i] = diagonal

    def apply_rows(src, slot, i, columns):
        here, others = sides(src, i, slot, columns)
        acc = coef[0, i] * others[0]
        for k in range(1, 6):
            acc = acc + coef[k, i] * others[k]
        return b_ref[i] - (coef[6, i] * here - acc)

    center = (UPPER_EIG + lower) / 2.0
    half_width = (UPPER_EIG - lower) / 2.0
    sigma_ratio = center / half_width
    rho_old = 1.0 / sigma_ratio
    current = 0
    if zero_start:
        for i in range(A):
            update = b_ref[i] / coef[6, i] / center
            dbuf[i] = update
            fld[current, i] = update
    else:
        exchange_finish(first_waits)
        columns = z_columns(first_slot)
        for i in range(A):
            remain = apply_rows(v0_ref, first_slot, i, columns)
            update = remain / coef[6, i] / center
            dbuf[i] = update
            fld[current, i] = v0_ref[i] + update
    for sweep in range(count - 1):
        rho_new = 1.0 / (2.0 * sigma_ratio - rho_old)
        slot = next_slot()
        src = fld.at[current]
        exchange(src, slot)
        last = sweep == count - 2
        dst = outs[0] if last else fld.at[1 - current]
        columns = z_columns(slot)
        for i in range(A):
            remain = apply_rows(src, slot, i, columns)
            update = (rho_new * rho_old) * dbuf[i] + (2.0 * rho_new / half_width) * (
                remain / coef[6, i]
            )
            dbuf[i] = update
            dst[i] = src[i] + update
        rho_old = rho_new
        current = 1 - current
    if residual:
        slot = next_slot()
        exchange(outs[0], slot)
        remain_ref = dbuf if restrict else outs[1]
        columns = z_columns(slot)
        for i in range(A):
            remain_ref[i] = apply_rows(outs[0], slot, i, columns)
        if restrict:
            restrict_into(dbuf, outs[1], 0.5)


KERNELS = {}


def smooth(level_args, shift, count, lower, zero_start, residual, restrict=False):
    A, B, C = level_args[0].shape
    sizes = tuple(lax.axis_size(axis) for axis in AXES)
    cfg = (sizes, shift, count, lower, zero_start, residual, restrict)
    ident = KERNELS.setdefault((A, B, C) + cfg[1:], len(KERNELS))
    vmem = pl.BlockSpec(memory_space=pltpu.VMEM)
    block = jax.ShapeDtypeStruct((A, B, C), jnp.float32)
    coarse = jax.ShapeDtypeStruct((A // 2, B // 2, C // 2), jnp.float32)
    shapes = [block] + ([block] if residual and not restrict else []) + ([coarse] * 3 if restrict else [])
    n_out = len(shapes)
    return pl.pallas_call(
        functools.partial(level_kernel, cfg),
        out_shape=tuple(shapes),
        in_specs=[vmem] * len(level_args),
        out_specs=tuple([vmem] * n_out),
        scratch_shapes=[
            pltpu.VMEM((2, A, B, C), jnp.float32),
            pltpu.VMEM((2, SLOTS, B, C), jnp.float32),
            pltpu.VMEM((2, SLOTS, A, 8, C), jnp.float32),
            pltpu.VMEM((2, SLOTS, 8, A * B), jnp.float32),
            pltpu.VMEM((SLOTS, 8, A * B), jnp.float32),
            pltpu.VMEM((7, A, B, C), jnp.float32),
            pltpu.VMEM((A, B, C), jnp.float32),
            pltpu.SemaphoreType.DMA((SLOTS, 6)),
            pltpu.SemaphoreType.DMA((SLOTS, 6)),
        ],
        compiler_params=pltpu.CompilerParams(collective_id=ident, has_side_effects=True),
    )(*level_args)


def restrict_into(src, dst, scale):
    A, B, C = src.shape
    coarse_rows = (
        lax.broadcasted_iota(jnp.int32, (B // 2, B), 1) // 2
        == lax.broadcasted_iota(jnp.int32, (B // 2, B), 0)
    ).astype(jnp.float32)
    coarse_cols = (
        lax.broadcasted_iota(jnp.int32, (C, C // 2), 0) // 2
        == lax.broadcasted_iota(jnp.int32, (C, C // 2), 1)
    ).astype(jnp.float32)
    for i in range(A // 2):
        pair = src[2 * i] + src[2 * i + 1]
        half = jnp.dot(
            coarse_rows, pair, precision=lax.Precision.HIGHEST, preferred_element_type=jnp.float32
        )
        dst[i] = scale * jnp.dot(
            half, coarse_cols, precision=lax.Precision.HIGHEST, preferred_element_type=jnp.float32
        )


def neighbour_targets(sizes):
    index = [lax.axis_index(axis) for axis in AXES]
    targets = []
    for k in range(6):
        axis = k // 2
        if k % 2 == 0:
            exists = index[axis] > 0
            other = index[axis] - 1
        else:
            exists = index[axis] < sizes[axis] - 1
            other = index[axis] + 1
        device = tuple(other if a == axis else index[a] for a in range(3))
        targets.append((exists, device))
    return targets


def level_tools(shape, level, targets, bufs, send_sem, recv_sem):
    A, B, C = shape
    fld, xh, yh, zh, zsend, coef, dbuf = bufs

    def halo(h, slot):
        if h < 2:
            return xh.at[h, slot]
        return yh.at[h - 2, slot] if h < 4 else zh.at[h - 4, slot]

    picks = lax.broadcasted_iota(jnp.int32, (8, C), 0)
    lanes = lax.broadcasted_iota(jnp.int32, (8, C), 1)
    selector = jnp.where(
        (picks == 0) & (lanes == 0), 1.0, jnp.where((picks == 1) & (lanes == C - 1), 1.0, 0.0)
    ).astype(jnp.float32)
    rows = lax.broadcasted_iota(jnp.int32, (B, C), 0)
    cols = lax.broadcasted_iota(jnp.int32, (B, C), 1)

    def zero_halos():
        for h, (exists, device) in enumerate(targets):

            @pl.when(jnp.logical_not(exists))
            def _():
                for slot in range(SLOTS):
                    buf = halo(h, slot)
                    buf[...] = jnp.zeros(buf.shape, buf.dtype)

    def exchange_start(src, slot):
        block = src[...].reshape(A * B, C)
        zsend[slot] = lax.dot_general(
            selector, block, (((1,), (1,)), ((), ())),
            precision=lax.Precision.HIGHEST, preferred_element_type=jnp.float32,
        )
        sources = (
            src.at[0], src.at[A - 1],
            src.at[:, 0:8, :], src.at[:, B - 8 : B, :],
            zsend.at[slot], zsend.at[slot],
        )
        waits = []
        for k, (exists, device) in enumerate(targets):
            copy = pltpu.make_async_remote_copy(
                src_ref=sources[k],
                dst_ref=halo(k ^ 1, slot),
                send_sem=send_sem.at[level, slot, k],
                recv_sem=recv_sem.at[level, slot, k ^ 1],
                device_id=device,
                device_id_type=MESH,
            )
            pl.when(exists)(copy.start)
            incoming = pltpu.make_async_remote_copy(
                src_ref=sources[k ^ 1],
                dst_ref=halo(k, slot),
                send_sem=send_sem.at[level, slot, k ^ 1],
                recv_sem=recv_sem.at[level, slot, k],
                device_id=device,
                device_id_type=MESH,
            )
            waits.append((exists, copy.wait_send))
            waits.append((exists, incoming.wait_recv))
        return waits

    def exchange_finish(waits):
        for exists, wait in waits:
            pl.when(exists)(wait)

    def exchange(src, slot):
        exchange_finish(exchange_start(src, slot))

    def z_columns(slot):
        return (jnp.transpose(zh[0, slot]), jnp.transpose(zh[1, slot]))

    def sides(src, i, slot, columns):
        here = src[i]
        lower_x = src[i - 1] if i > 0 else xh[0, slot]
        upper_x = src[i + 1] if i < A - 1 else xh[1, slot]
        lower_y = jnp.where(rows == 0, yh[0, slot, i, 7:8, :], pltpu.roll(here, 1, 0))
        upper_y = jnp.where(rows == B - 1, yh[1, slot, i, 0:1, :], pltpu.roll(here, B - 1, 0))
        lower_z = jnp.where(cols == 0, columns[0][i * B : (i + 1) * B, 1:2], pltpu.roll(here, 1, 1))
        upper_z = jnp.where(
            cols == C - 1, columns[1][i * B : (i + 1) * B, 0:1], pltpu.roll(here, C - 1, 1)
        )
        return here, (lower_x, upper_x, lower_y, upper_y, lower_z, upper_z)

    def build_coef(beta_ref, alpha_ref, slot, shift):
        columns = z_columns(slot)
        for i in range(A):
            here, others = sides(beta_ref, i, slot, columns)
            diagonal = shift * alpha_ref[i]
            for k in range(6):
                face = 0.5 * (here + others[k])
                coef[k, i] = face
                diagonal = diagonal + face
            coef[6, i] = diagonal

    def apply_rows(src, b_ref, slot, i, columns):
        here, others = sides(src, i, slot, columns)
        acc = coef[0, i] * others[0]
        for k in range(1, 6):
            acc = acc + coef[k, i] * others[k]
        return b_ref[i] - (coef[6, i] * here - acc)

    def smooth_down(b_ref, v_out, next_rhs, count, lower):
        center = (UPPER_EIG + lower) / 2.0
        half_width = (UPPER_EIG - lower) / 2.0
        sigma_ratio = center / half_width
        rho_old = 1.0 / sigma_ratio
        current = 0
        for i in range(A):
            update = b_ref[i] / coef[6, i] / center
            dbuf[i] = update
            fld[current, i] = update
        slot = 0
        for sweep in range(count - 1):
            rho_new = 1.0 / (2.0 * sigma_ratio - rho_old)
            slot = (slot + 1) % SLOTS
            src = fld.at[current]
            exchange(src, slot)
            columns = z_columns(slot)
            dst = v_out if sweep == count - 2 else fld.at[1 - current]
            for i in range(A):
                remain = apply_rows(src, b_ref, slot, i, columns)
                update = (rho_new * rho_old) * dbuf[i] + (2.0 * rho_new / half_width) * (
                    remain / coef[6, i]
                )
                dbuf[i] = update
                dst[i] = src[i] + update
            rho_old = rho_new
            current = 1 - current
        slot = (slot + 1) % SLOTS
        exchange(v_out, slot)
        columns = z_columns(slot)
        for i in range(A):
            dbuf[i] = apply_rows(v_out, b_ref, slot, i, columns)
        restrict_into(dbuf, next_rhs, 0.5)

    return zero_halos, exchange_start, exchange_finish, build_coef, smooth_down


def level_scratch(shape):
    A, B, C = shape
    return [
        pltpu.VMEM((2, A, B, C), jnp.float32),
        pltpu.VMEM((2, SLOTS, B, C), jnp.float32),
        pltpu.VMEM((2, SLOTS, A, 8, C), jnp.float32),
        pltpu.VMEM((2, SLOTS, 8, A * B), jnp.float32),
        pltpu.VMEM((SLOTS, 8, A * B), jnp.float32),
        pltpu.VMEM((7, A, B, C), jnp.float32),
        pltpu.VMEM((A, B, C), jnp.float32),
    ]


def down_kernel(cfg, *refs):
    sizes, shapes, shifts = cfg
    depth = len(shapes)
    b0, beta0, alpha0 = refs[0:3]
    outs = refs[3 : 3 + 4 * depth]
    iterates = outs[0:depth]
    rhs = [b0] + list(outs[depth : 2 * depth])
    betas = [beta0] + list(outs[2 * depth : 3 * depth])
    alphas = [alpha0] + list(outs[3 * depth : 4 * depth])
    scratch = refs[3 + 4 * depth :]
    send_sem, recv_sem = scratch[7 * depth], scratch[7 * depth + 1]
    targets = neighbour_targets(sizes)
    barrier = pltpu.get_barrier_semaphore()
    total = jnp.int32(0)
    for exists, device in targets:

        @pl.when(exists)
        def _():
            pl.semaphore_signal(barrier, inc=1, device_id=device, device_id_type=MESH)

        total = total + exists.astype(jnp.int32)
    tools = [
        level_tools(shapes[l], l, targets, scratch[7 * l : 7 * l + 7], send_sem, recv_sem)
        for l in range(depth)
    ]
    for tool in tools:
        tool[0]()
    for l in range(depth):
        restrict_into(betas[l], betas[l + 1], 0.125)
        restrict_into(alphas[l], alphas[l + 1], 0.125)
    pl.semaphore_wait(barrier, total)
    waits = [tools[l][1](betas[l], 0) for l in range(depth)]
    for l in range(depth):
        tools[l][2](waits[l])
        tools[l][3](betas[l], alphas[l], 0, shifts[l])
    for l in range(depth):
        tools[l][4](rhs[l], iterates[l], rhs[l + 1], SWEEPS, SMOOTH_LOWER)


def down_chain(right_side, beta_coef, alpha_coef):
    sizes = tuple(lax.axis_size(axis) for axis in AXES)
    shapes = [tuple(n >> l for n in right_side.shape) for l in range(LEVELS + 1)]
    shifts = tuple(SHIFT_BASE * 4.0**l for l in range(LEVELS))
    cfg = (sizes, tuple(shapes[:LEVELS]), shifts)
    vmem = pl.BlockSpec(memory_space=pltpu.VMEM)
    out_shapes = [jax.ShapeDtypeStruct(s, jnp.float32) for s in shapes[:LEVELS]]
    out_shapes += [jax.ShapeDtypeStruct(s, jnp.float32) for s in shapes[1:]] * 3
    scratch = []
    for s in shapes[:LEVELS]:
        scratch += level_scratch(s)
    scratch += [
        pltpu.SemaphoreType.DMA((LEVELS, SLOTS, 6)),
        pltpu.SemaphoreType.DMA((LEVELS, SLOTS, 6)),
    ]
    outs = pl.pallas_call(
        functools.partial(down_kernel, cfg),
        out_shape=tuple(out_shapes),
        in_specs=[vmem] * 3,
        out_specs=tuple([vmem] * len(out_shapes)),
        scratch_shapes=scratch,
        compiler_params=pltpu.CompilerParams(collective_id=32, has_side_effects=True),
    )(right_side, beta_coef, alpha_coef)
    iterates = list(outs[0:LEVELS])
    rhs_levels = [right_side] + list(outs[LEVELS : 2 * LEVELS])
    betas = [beta_coef] + list(outs[2 * LEVELS : 3 * LEVELS])
    alphas = [alpha_coef] + list(outs[3 * LEVELS : 4 * LEVELS])
    return iterates, rhs_levels, betas, alphas


def gather_kernel(sizes, row_ref, out_ref, first, dense, second, send_sem, recv_sem):
    index = [lax.axis_index(axis) for axis in AXES]
    nx, ny, nz = sizes

    def device(axis, step):
        return tuple(
            lax.rem(index[a] + step, sizes[a]) if a == axis else index[a] for a in range(3)
        )

    barrier = pltpu.get_barrier_semaphore()
    partners = []
    for axis in (2, 1, 0):
        partners.append([device(axis, step) for step in range(1, sizes[axis])])
    for group in partners:
        for peer in group:
            pl.semaphore_signal(barrier, inc=1, device_id=peer, device_id_type=MESH)
    pl.semaphore_wait(barrier, sum(len(group) for group in partners))

    stages = ((row_ref, first, 2), (dense, second, 1), (second, out_ref, 0))
    for stage, (source, target, axis) in enumerate(stages):
        mine = index[axis]
        waits = []
        for step in range(1, sizes[axis]):
            peer = device(axis, step)
            copy = pltpu.make_async_remote_copy(
                src_ref=source,
                dst_ref=target.at[mine],
                send_sem=send_sem.at[stage, step],
                recv_sem=recv_sem.at[stage, mine],
                device_id=peer,
                device_id_type=MESH,
            )
            copy.start()
            origin = lax.rem(mine + sizes[axis] - step, sizes[axis])
            incoming = pltpu.make_async_remote_copy(
                src_ref=source,
                dst_ref=target.at[origin],
                send_sem=send_sem.at[stage, step],
                recv_sem=recv_sem.at[stage, origin],
                device_id=peer,
                device_id_type=MESH,
            )
            waits.append((copy, incoming))
        if stage == 0:
            target[mine] = source[...]
        else:
            target[mine] = source[...]
        for copy, incoming in waits:
            copy.wait_send()
            incoming.wait_recv()
        if stage == 0:
            for z in range(nz):
                dense[z : z + 1, :] = first[z]


def gather_bottom(packed):
    sizes = tuple(lax.axis_size(axis) for axis in AXES)
    nx, ny, nz = sizes
    width = packed.size
    lanes = -(-width // 128) * 128
    row = jnp.pad(packed.reshape(1, width), ((0, 0), (0, lanes - width)))
    vmem = pl.BlockSpec(memory_space=pltpu.VMEM)
    top = max(sizes)
    whole = pl.pallas_call(
        functools.partial(gather_kernel, sizes),
        out_shape=jax.ShapeDtypeStruct((nx, ny, nz, lanes), jnp.float32),
        in_specs=[vmem],
        out_specs=vmem,
        scratch_shapes=[
            pltpu.VMEM((nz, 1, lanes), jnp.float32),
            pltpu.VMEM((nz, lanes), jnp.float32),
            pltpu.VMEM((ny, nz, lanes), jnp.float32),
            pltpu.SemaphoreType.DMA((3, top)),
            pltpu.SemaphoreType.DMA((3, top)),
        ],
        compiler_params=pltpu.CompilerParams(collective_id=64, has_side_effects=True),
    )(row)
    whole = whole[..., :width].reshape((nx, ny, nz) + packed.shape)
    whole = whole.transpose(3, 0, 4, 1, 5, 2, 6)
    return whole.reshape(
        (packed.shape[0],) + tuple(n * s for n, s in zip(sizes, packed.shape[1:]))
    )


def split_padded(padded):
    return (
        padded[:-2, 1:-1, 1:-1],
        padded[2:, 1:-1, 1:-1],
        padded[1:-1, :-2, 1:-1],
        padded[1:-1, 2:, 1:-1],
        padded[1:-1, 1:-1, :-2],
        padded[1:-1, 1:-1, 2:],
    )


def zero_pad(field):
    return split_padded(jnp.pad(field, 1))


def level_operator(beta_level, alpha_level, beta_sides, shift):
    coeffs = tuple((0.5 * (beta_level + other) for other in beta_sides))
    diagonal = shift * alpha_level
    for coeff in coeffs:
        diagonal = diagonal + coeff
    return (coeffs, diagonal)


def apply_operator(field, operator, pad_field):
    coeffs, diagonal = operator
    others = pad_field(field)
    total = coeffs[0] * others[0]
    for index in range(1, 6):
        total = total + coeffs[index] * others[index]
    return diagonal * field - total


def chebyshev(iterate, rhs_level, operator, count, lower, zero_start, pad_field):
    diagonal = operator[1]
    center = (UPPER_EIG + lower) / 2.0
    half_width = (UPPER_EIG - lower) / 2.0
    sigma_ratio = center / half_width
    rho_old = 1.0 / sigma_ratio
    if zero_start:
        remain = rhs_level
    else:
        remain = rhs_level - apply_operator(iterate, operator, pad_field)
    update = remain / diagonal / center
    iterate = iterate + update
    for sweep_index in range(count - 1):
        remain = rhs_level - apply_operator(iterate, operator, pad_field)
        rho_new = 1.0 / (2.0 * sigma_ratio - rho_old)
        update = rho_new * rho_old * update + 2.0 * rho_new / half_width * (remain / diagonal)
        iterate = iterate + update
        rho_old = rho_new
    return iterate


def restrict_mean(field):
    first, second, third = field.shape
    blocks = field.reshape(first // 2, 2, second // 2, 2, third // 2, 2)
    return jnp.sum(blocks, axis=(1, 3, 5)) * 0.125


def prolong_copy(field):
    return jnp.repeat(jnp.repeat(jnp.repeat(field, 2, axis=0), 2, axis=1), 2, axis=2)


def shards(right_side, alpha_coef, beta_coef):
    smoothed, rhs_levels, betas, alphas = down_chain(right_side, beta_coef, alpha_coef)
    coarse_rhs = rhs_levels[LEVELS]
    local_shape = coarse_rhs.shape
    packed = jnp.stack([coarse_rhs, betas[LEVELS], alphas[LEVELS]])
    index_x = lax.axis_index("gx")
    index_y = lax.axis_index("gy")
    index_z = lax.axis_index("gz")
    packed = gather_bottom(packed)
    whole_rhs = packed[0]
    whole_beta = packed[1]
    whole_alpha = packed[2]
    bottom_operator = level_operator(
        whole_beta, whole_alpha, zero_pad(whole_beta), SHIFT_BASE * 4.0**LEVELS
    )
    whole_correction = chebyshev(
        jnp.zeros_like(whole_rhs), whole_rhs, bottom_operator, BOTTOM, BOTTOM_LOWER, True, zero_pad
    )
    starts = (index_x * local_shape[0], index_y * local_shape[1], index_z * local_shape[2])
    correction = lax.dynamic_slice(whole_correction, starts, local_shape)
    for level in range(LEVELS - 1, -1, -1):
        start_field = smoothed[level] + prolong_copy(correction)
        outs = smooth(
            (rhs_levels[level], betas[level], alphas[level], start_field),
            SHIFT_BASE * 4.0**level,
            SWEEPS,
            SMOOTH_LOWER,
            False,
            level == 0,
        )
        correction = outs[0]
    residual_field = outs[1]
    return (correction, residual_field)


def solution(mesh):
    in_specs = (P("gx", "gy", "gz"), P("gx", "gy", "gz"), P("gx", "gy", "gz"))
    out_specs = (P("gx", "gy", "gz"), P("gx", "gy", "gz"))
    return jax.shard_map(shards, mesh=mesh, in_specs=in_specs, out_specs=out_specs, check_vma=False)
```

```python
import functools

import jax
import jax.numpy as jnp
from jax import lax
from jax.experimental import pallas as pl
from jax.experimental.pallas import tpu as pltpu
from jax.sharding import PartitionSpec as P

MESH = pl.DeviceIdType.MESH
AXES = ("gx", "gy", "gz")
SLOTS = 3

LEVELS = 3
SWEEPS = 4
BOTTOM = 12


SHIFT_BASE = 0.01
UPPER_EIG = 2.0
SMOOTH_LOWER = 0.25
BOTTOM_LOWER = 0.02


def level_kernel(cfg, *refs):
    sizes, shift, count, lower, zero_start, residual, restrict = cfg
    n_in = 3 if zero_start else 4
    b_ref, beta_ref, alpha_ref = refs[0:3]
    v0_ref = None if zero_start else refs[3]
    n_out = 1 + (1 if residual and not restrict else 0) + (3 if restrict else 0)
    outs = refs[n_in : n_in + n_out]
    fld, xh, yh, zh, zsend, coef, dbuf, send_sem, recv_sem = refs[n_in + len(outs) :]
    A, B, C = b_ref.shape
    index = [lax.axis_index(axis) for axis in AXES]
    targets = []
    for k in range(6):
        axis = k // 2
        if k % 2 == 0:
            exists = index[axis] > 0
            other = index[axis] - 1
        else:
            exists = index[axis] < sizes[axis] - 1
            other = index[axis] + 1
        device = tuple(other if a == axis else index[a] for a in range(3))
        targets.append((exists, device))

    def halo(h, slot):
        if h < 2:
            return xh.at[h, slot]
        return yh.at[h - 2, slot] if h < 4 else zh.at[h - 4, slot]

    picks = lax.broadcasted_iota(jnp.int32, (8, C), 0)
    lanes = lax.broadcasted_iota(jnp.int32, (8, C), 1)
    selector = jnp.where(
        (picks == 0) & (lanes == 0), 1.0, jnp.where((picks == 1) & (lanes == C - 1), 1.0, 0.0)
    ).astype(jnp.float32)

    barrier = pltpu.get_barrier_semaphore()
    total = jnp.int32(0)
    for exists, device in targets:

        @pl.when(exists)
        def _():
            pl.semaphore_signal(barrier, inc=1, device_id=device, device_id_type=MESH)

        total = total + exists.astype(jnp.int32)
    for h, (exists, device) in enumerate(targets):

        @pl.when(jnp.logical_not(exists))
        def _():
            for slot in range(SLOTS):
                buf = halo(h, slot)
                buf[...] = jnp.zeros(buf.shape, buf.dtype)

    if restrict:
        coarse_rows = (
            lax.broadcasted_iota(jnp.int32, (B // 2, B), 1) // 2
            == lax.broadcasted_iota(jnp.int32, (B // 2, B), 0)
        ).astype(jnp.float32)
        coarse_cols = (
            lax.broadcasted_iota(jnp.int32, (C, C // 2), 0) // 2
            == lax.broadcasted_iota(jnp.int32, (C, C // 2), 1)
        ).astype(jnp.float32)

        def restrict_into(src, dst, scale):
            for i in range(A // 2):
                pair = src[2 * i] + src[2 * i + 1]
                half = jnp.dot(
                    coarse_rows, pair, precision=lax.Precision.HIGHEST,
                    preferred_element_type=jnp.float32,
                )
                dst[i] = scale * jnp.dot(
                    half, coarse_cols, precision=lax.Precision.HIGHEST,
                    preferred_element_type=jnp.float32,
                )

        restrict_into(beta_ref, outs[2], 0.125)
        restrict_into(alpha_ref, outs[3], 0.125)
    pl.semaphore_wait(barrier, total)

    def exchange_start(src, slot):
        block = src[...].reshape(A * B, C)
        zsend[slot] = lax.dot_general(
            selector, block, (((1,), (1,)), ((), ())),
            precision=lax.Precision.HIGHEST, preferred_element_type=jnp.float32,
        )
        sources = (
            src.at[0], src.at[A - 1],
            src.at[:, 0:8, :], src.at[:, B - 8 : B, :],
            zsend.at[slot], zsend.at[slot],
        )
        waits = []
        for k, (exists, device) in enumerate(targets):
            copy = pltpu.make_async_remote_copy(
                src_ref=sources[k],
                dst_ref=halo(k ^ 1, slot),
                send_sem=send_sem.at[slot, k],
                recv_sem=recv_sem.at[slot, k ^ 1],
                device_id=device,
                device_id_type=MESH,
            )
            pl.when(exists)(copy.start)
            incoming = pltpu.make_async_remote_copy(
                src_ref=sources[k ^ 1],
                dst_ref=halo(k, slot),
                send_sem=send_sem.at[slot, k ^ 1],
                recv_sem=recv_sem.at[slot, k],
                device_id=device,
                device_id_type=MESH,
            )
            waits.append((exists, copy.wait_send))
            waits.append((exists, incoming.wait_recv))
        return waits

    def exchange_finish(waits):
        for exists, wait in waits:
            pl.when(exists)(wait)

    def exchange(src, slot):
        exchange_finish(exchange_start(src, slot))

    rows = lax.broadcasted_iota(jnp.int32, (B, C), 0)
    cols = lax.broadcasted_iota(jnp.int32, (B, C), 1)

    def z_columns(slot):
        return (jnp.transpose(zh[0, slot]), jnp.transpose(zh[1, slot]))

    def sides(src, i, slot, columns):
        here = src[i]
        lower_x = src[i - 1] if i > 0 else xh[0, slot]
        upper_x = src[i + 1] if i < A - 1 else xh[1, slot]
        lower_y = jnp.where(rows == 0, yh[0, slot, i, 7:8, :], pltpu.roll(here, 1, 0))
        upper_y = jnp.where(rows == B - 1, yh[1, slot, i, 0:1, :], pltpu.roll(here, B - 1, 0))
        lower_z = jnp.where(cols == 0, columns[0][i * B : (i + 1) * B, 1:2], pltpu.roll(here, 1, 1))
        upper_z = jnp.where(
            cols == C - 1, columns[1][i * B : (i + 1) * B, 0:1], pltpu.roll(here, C - 1, 1)
        )
        return here, (lower_x, upper_x, lower_y, upper_y, lower_z, upper_z)

    exchanges = [0]

    def next_slot():
        slot = exchanges[0] % SLOTS
        exchanges[0] += 1
        return slot

    slot = next_slot()
    if zero_start:
        exchange(beta_ref, slot)
    else:
        first_slot = next_slot()
        first_waits = exchange_start(v0_ref, first_slot)
        exchange(beta_ref, slot)
    columns = z_columns(slot)
    for i in range(A):
        here, others = sides(beta_ref, i, slot, columns)
        diagonal = shift * alpha_ref[i]
        for k in range(6):
            face = 0.5 * (here + others[k])
            coef[k, i] = face
            diagonal = diagonal + face
        coef[6, i] = diagonal

    def apply_rows(src, slot, i, columns):
        here, others = sides(src, i, slot, columns)
        acc = coef[0, i] * others[0]
        for k in range(1, 6):
            acc = acc + coef[k, i] * others[k]
        return b_ref[i] - (coef[6, i] * here - acc)

    center = (UPPER_EIG + lower) / 2.0
    half_width = (UPPER_EIG - lower) / 2.0
    sigma_ratio = center / half_width
    rho_old = 1.0 / sigma_ratio
    current = 0
    if zero_start:
        for i in range(A):
            update = b_ref[i] / coef[6, i] / center
            dbuf[i] = update
            fld[current, i] = update
    else:
        exchange_finish(first_waits)
        columns = z_columns(first_slot)
        for i in range(A):
            remain = apply_rows(v0_ref, first_slot, i, columns)
            update = remain / coef[6, i] / center
            dbuf[i] = update
            fld[current, i] = v0_ref[i] + update
    for sweep in range(count - 1):
        rho_new = 1.0 / (2.0 * sigma_ratio - rho_old)
        slot = next_slot()
        src = fld.at[current]
        exchange(src, slot)
        last = sweep == count - 2
        dst = outs[0] if last else fld.at[1 - current]
        columns = z_columns(slot)
        for i in range(A):
            remain = apply_rows(src, slot, i, columns)
            update = (rho_new * rho_old) * dbuf[i] + (2.0 * rho_new / half_width) * (
                remain / coef[6, i]
            )
            dbuf[i] = update
            dst[i] = src[i] + update
        rho_old = rho_new
        current = 1 - current
    if residual:
        slot = next_slot()
        exchange(outs[0], slot)
        remain_ref = dbuf if restrict else outs[1]
        columns = z_columns(slot)
        for i in range(A):
            remain_ref[i] = apply_rows(outs[0], slot, i, columns)
        if restrict:
            restrict_into(dbuf, outs[1], 0.5)


KERNELS = {}


def smooth(level_args, shift, count, lower, zero_start, residual, restrict=False):
    A, B, C = level_args[0].shape
    sizes = tuple(lax.axis_size(axis) for axis in AXES)
    cfg = (sizes, shift, count, lower, zero_start, residual, restrict)
    ident = KERNELS.setdefault((A, B, C) + cfg[1:], len(KERNELS))
    vmem = pl.BlockSpec(memory_space=pltpu.VMEM)
    block = jax.ShapeDtypeStruct((A, B, C), jnp.float32)
    coarse = jax.ShapeDtypeStruct((A // 2, B // 2, C // 2), jnp.float32)
    shapes = [block] + ([block] if residual and not restrict else []) + ([coarse] * 3 if restrict else [])
    n_out = len(shapes)
    return pl.pallas_call(
        functools.partial(level_kernel, cfg),
        out_shape=tuple(shapes),
        in_specs=[vmem] * len(level_args),
        out_specs=tuple([vmem] * n_out),
        scratch_shapes=[
            pltpu.VMEM((2, A, B, C), jnp.float32),
            pltpu.VMEM((2, SLOTS, B, C), jnp.float32),
            pltpu.VMEM((2, SLOTS, A, 8, C), jnp.float32),
            pltpu.VMEM((2, SLOTS, 8, A * B), jnp.float32),
            pltpu.VMEM((SLOTS, 8, A * B), jnp.float32),
            pltpu.VMEM((7, A, B, C), jnp.float32),
            pltpu.VMEM((A, B, C), jnp.float32),
            pltpu.SemaphoreType.DMA((SLOTS, 6)),
            pltpu.SemaphoreType.DMA((SLOTS, 6)),
        ],
        compiler_params=pltpu.CompilerParams(collective_id=ident, has_side_effects=True),
    )(*level_args)


def restrict_into(src, dst, scale):
    A, B, C = src.shape
    coarse_rows = (
        lax.broadcasted_iota(jnp.int32, (B // 2, B), 1) // 2
        == lax.broadcasted_iota(jnp.int32, (B // 2, B), 0)
    ).astype(jnp.float32)
    coarse_cols = (
        lax.broadcasted_iota(jnp.int32, (C, C // 2), 0) // 2
        == lax.broadcasted_iota(jnp.int32, (C, C // 2), 1)
    ).astype(jnp.float32)
    for i in range(A // 2):
        pair = src[2 * i] + src[2 * i + 1]
        half = jnp.dot(
            coarse_rows, pair, precision=lax.Precision.HIGHEST, preferred_element_type=jnp.float32
        )
        dst[i] = scale * jnp.dot(
            half, coarse_cols, precision=lax.Precision.HIGHEST, preferred_element_type=jnp.float32
        )


def neighbour_targets(sizes):
    index = [lax.axis_index(axis) for axis in AXES]
    targets = []
    for k in range(6):
        axis = k // 2
        if k % 2 == 0:
            exists = index[axis] > 0
            other = index[axis] - 1
        else:
            exists = index[axis] < sizes[axis] - 1
            other = index[axis] + 1
        device = tuple(other if a == axis else index[a] for a in range(3))
        targets.append((exists, device))
    return targets


def level_tools(shape, level, targets, bufs, send_sem, recv_sem):
    A, B, C = shape
    fld, xh, yh, zh, zsend, coef, dbuf = bufs

    def halo(h, slot):
        if h < 2:
            return xh.at[h, slot]
        return yh.at[h - 2, slot] if h < 4 else zh.at[h - 4, slot]

    picks = lax.broadcasted_iota(jnp.int32, (8, C), 0)
    lanes = lax.broadcasted_iota(jnp.int32, (8, C), 1)
    selector = jnp.where(
        (picks == 0) & (lanes == 0), 1.0, jnp.where((picks == 1) & (lanes == C - 1), 1.0, 0.0)
    ).astype(jnp.float32)
    rows = lax.broadcasted_iota(jnp.int32, (B, C), 0)
    cols = lax.broadcasted_iota(jnp.int32, (B, C), 1)

    def zero_halos():
        for h, (exists, device) in enumerate(targets):

            @pl.when(jnp.logical_not(exists))
            def _():
                for slot in range(SLOTS):
                    buf = halo(h, slot)
                    buf[...] = jnp.zeros(buf.shape, buf.dtype)

    def exchange_start(src, slot):
        block = src[...].reshape(A * B, C)
        zsend[slot] = lax.dot_general(
            selector, block, (((1,), (1,)), ((), ())),
            precision=lax.Precision.HIGHEST, preferred_element_type=jnp.float32,
        )
        sources = (
            src.at[0], src.at[A - 1],
            src.at[:, 0:8, :], src.at[:, B - 8 : B, :],
            zsend.at[slot], zsend.at[slot],
        )
        waits = []
        for k, (exists, device) in enumerate(targets):
            copy = pltpu.make_async_remote_copy(
                src_ref=sources[k],
                dst_ref=halo(k ^ 1, slot),
                send_sem=send_sem.at[level, slot, k],
                recv_sem=recv_sem.at[level, slot, k ^ 1],
                device_id=device,
                device_id_type=MESH,
            )
            pl.when(exists)(copy.start)
            incoming = pltpu.make_async_remote_copy(
                src_ref=sources[k ^ 1],
                dst_ref=halo(k, slot),
                send_sem=send_sem.at[level, slot, k ^ 1],
                recv_sem=recv_sem.at[level, slot, k],
                device_id=device,
                device_id_type=MESH,
            )
            waits.append((exists, copy.wait_send))
            waits.append((exists, incoming.wait_recv))
        return waits

    def exchange_finish(waits):
        for exists, wait in waits:
            pl.when(exists)(wait)

    def exchange(src, slot):
        exchange_finish(exchange_start(src, slot))

    def z_columns(slot):
        return (jnp.transpose(zh[0, slot]), jnp.transpose(zh[1, slot]))

    def sides(src, i, slot, columns):
        here = src[i]
        lower_x = src[i - 1] if i > 0 else xh[0, slot]
        upper_x = src[i + 1] if i < A - 1 else xh[1, slot]
        lower_y = jnp.where(rows == 0, yh[0, slot, i, 7:8, :], pltpu.roll(here, 1, 0))
        upper_y = jnp.where(rows == B - 1, yh[1, slot, i, 0:1, :], pltpu.roll(here, B - 1, 0))
        lower_z = jnp.where(cols == 0, columns[0][i * B : (i + 1) * B, 1:2], pltpu.roll(here, 1, 1))
        upper_z = jnp.where(
            cols == C - 1, columns[1][i * B : (i + 1) * B, 0:1], pltpu.roll(here, C - 1, 1)
        )
        return here, (lower_x, upper_x, lower_y, upper_y, lower_z, upper_z)

    def build_coef(beta_ref, alpha_ref, slot, shift):
        columns = z_columns(slot)
        for i in range(A):
            here, others = sides(beta_ref, i, slot, columns)
            diagonal = shift * alpha_ref[i]
            for k in range(6):
                face = 0.5 * (here + others[k])
                coef[k, i] = face
                diagonal = diagonal + face
            coef[6, i] = diagonal

    def apply_rows(src, b_ref, slot, i, columns):
        here, others = sides(src, i, slot, columns)
        acc = coef[0, i] * others[0]
        for k in range(1, 6):
            acc = acc + coef[k, i] * others[k]
        return b_ref[i] - (coef[6, i] * here - acc)

    def smooth_down(b_ref, v_out, next_rhs, count, lower):
        center = (UPPER_EIG + lower) / 2.0
        half_width = (UPPER_EIG - lower) / 2.0
        sigma_ratio = center / half_width
        rho_old = 1.0 / sigma_ratio
        current = 0
        for i in range(A):
            update = b_ref[i] / coef[6, i] / center
            dbuf[i] = update
            fld[current, i] = update
        slot = 0
        for sweep in range(count - 1):
            rho_new = 1.0 / (2.0 * sigma_ratio - rho_old)
            slot = (slot + 1) % SLOTS
            src = fld.at[current]
            exchange(src, slot)
            columns = z_columns(slot)
            dst = v_out if sweep == count - 2 else fld.at[1 - current]
            for i in range(A):
                remain = apply_rows(src, b_ref, slot, i, columns)
                update = (rho_new * rho_old) * dbuf[i] + (2.0 * rho_new / half_width) * (
                    remain / coef[6, i]
                )
                dbuf[i] = update
                dst[i] = src[i] + update
            rho_old = rho_new
            current = 1 - current
        slot = (slot + 1) % SLOTS
        exchange(v_out, slot)
        columns = z_columns(slot)
        for i in range(A):
            dbuf[i] = apply_rows(v_out, b_ref, slot, i, columns)
        restrict_into(dbuf, next_rhs, 0.5)

    def smooth_up(b_ref, v_out, count, lower, first_slot, first_waits, residual_out):
        start = fld.at[1]
        if first_waits is None:
            exchange(start, first_slot)
        else:
            exchange_finish(first_waits)
        center = (UPPER_EIG + lower) / 2.0
        half_width = (UPPER_EIG - lower) / 2.0
        sigma_ratio = center / half_width
        rho_old = 1.0 / sigma_ratio
        columns = z_columns(first_slot)
        for i in range(A):
            remain = apply_rows(start, b_ref, first_slot, i, columns)
            update = remain / coef[6, i] / center
            dbuf[i] = update
            fld[0, i] = start[i] + update
        current = 0
        slot = first_slot
        for sweep in range(count - 1):
            rho_new = 1.0 / (2.0 * sigma_ratio - rho_old)
            slot = (slot + 1) % SLOTS
            src = fld.at[current]
            exchange(src, slot)
            columns = z_columns(slot)
            dst = v_out if sweep == count - 2 else fld.at[1 - current]
            for i in range(A):
                remain = apply_rows(src, b_ref, slot, i, columns)
                update = (rho_new * rho_old) * dbuf[i] + (2.0 * rho_new / half_width) * (
                    remain / coef[6, i]
                )
                dbuf[i] = update
                dst[i] = src[i] + update
            rho_old = rho_new
            current = 1 - current
        if residual_out is not None:
            slot = (slot + 1) % SLOTS
            exchange(v_out, slot)
            columns = z_columns(slot)
            for i in range(A):
                residual_out[i] = apply_rows(v_out, b_ref, slot, i, columns)

    def prolong_start(coarse, smoothed):
        fine_rows = (
            lax.broadcasted_iota(jnp.int32, (B, B // 2), 0) // 2
            == lax.broadcasted_iota(jnp.int32, (B, B // 2), 1)
        ).astype(jnp.float32)
        fine_cols = (
            lax.broadcasted_iota(jnp.int32, (C // 2, C), 1) // 2
            == lax.broadcasted_iota(jnp.int32, (C // 2, C), 0)
        ).astype(jnp.float32)
        for i in range(A):
            half = jnp.dot(
                fine_rows, coarse[i // 2], precision=lax.Precision.HIGHEST,
                preferred_element_type=jnp.float32,
            )
            fine = jnp.dot(
                half, fine_cols, precision=lax.Precision.HIGHEST,
                preferred_element_type=jnp.float32,
            )
            fld[1, i] = smoothed[i] + fine

    return (
        zero_halos, exchange_start, exchange_finish, build_coef, smooth_down, smooth_up,
        prolong_start, fld,
    )


def up_kernel(cfg, *refs):
    sizes, shapes, shifts = cfg
    depth = len(shapes)
    coarsest = refs[0]
    level_in = [refs[1 + 4 * l : 5 + 4 * l] for l in range(depth)]
    solution_out, residual_out = refs[1 + 4 * depth : 3 + 4 * depth]
    scratch = refs[3 + 4 * depth :]
    results = scratch[7 * depth : 7 * depth + depth - 1]
    send_sem, recv_sem = scratch[8 * depth - 1], scratch[8 * depth]
    targets = neighbour_targets(sizes)
    barrier = pltpu.get_barrier_semaphore()
    total = jnp.int32(0)
    for exists, device in targets:

        @pl.when(exists)
        def _():
            pl.semaphore_signal(barrier, inc=1, device_id=device, device_id_type=MESH)

        total = total + exists.astype(jnp.int32)
    tools = [
        level_tools(shapes[l], l, targets, scratch[7 * l : 7 * l + 7], send_sem, recv_sem)
        for l in range(depth)
    ]
    for tool in tools:
        tool[0]()
    top = depth - 1
    tools[top][6](coarsest, level_in[top][0])
    pl.semaphore_wait(barrier, total)
    first_waits = tools[top][1](tools[top][7].at[1], 1)
    waits = [tools[l][1](level_in[l][2], 0) for l in range(depth)]
    for l in range(depth):
        tools[l][2](waits[l])
        tools[l][3](level_in[l][2], level_in[l][3], 0, shifts[l])
    coarse = None
    for l in range(top, -1, -1):
        if l < top:
            tools[l][6](coarse, level_in[l][0])
        v_out = solution_out if l == 0 else results[l - 1]
        tools[l][5](
            level_in[l][1], v_out, SWEEPS, SMOOTH_LOWER, 1,
            first_waits if l == top else None, residual_out if l == 0 else None,
        )
        coarse = v_out


def up_chain(coarsest, smoothed, rhs_levels, betas, alphas):
    sizes = tuple(lax.axis_size(axis) for axis in AXES)
    shapes = [tuple(x.shape) for x in smoothed]
    shifts = tuple(SHIFT_BASE * 4.0**l for l in range(LEVELS))
    cfg = (sizes, tuple(shapes), shifts)
    vmem = pl.BlockSpec(memory_space=pltpu.VMEM)
    args = [coarsest]
    for l in range(LEVELS):
        args += [smoothed[l], rhs_levels[l], betas[l], alphas[l]]
    scratch = []
    for s in shapes:
        scratch += level_scratch(s)
    scratch += [pltpu.VMEM(s, jnp.float32) for s in shapes[1:]]
    scratch += [
        pltpu.SemaphoreType.DMA((LEVELS, SLOTS, 6)),
        pltpu.SemaphoreType.DMA((LEVELS, SLOTS, 6)),
    ]
    fine = jax.ShapeDtypeStruct(shapes[0], jnp.float32)
    return pl.pallas_call(
        functools.partial(up_kernel, cfg),
        out_shape=(fine, fine),
        in_specs=[vmem] * len(args),
        out_specs=(vmem, vmem),
        scratch_shapes=scratch,
        compiler_params=pltpu.CompilerParams(collective_id=48, has_side_effects=True),
    )(*args)


def level_scratch(shape):
    A, B, C = shape
    return [
        pltpu.VMEM((2, A, B, C), jnp.float32),
        pltpu.VMEM((2, SLOTS, B, C), jnp.float32),
        pltpu.VMEM((2, SLOTS, A, 8, C), jnp.float32),
        pltpu.VMEM((2, SLOTS, 8, A * B), jnp.float32),
        pltpu.VMEM((SLOTS, 8, A * B), jnp.float32),
        pltpu.VMEM((7, A, B, C), jnp.float32),
        pltpu.VMEM((A, B, C), jnp.float32),
    ]


def down_kernel(cfg, *refs):
    sizes, shapes, shifts = cfg
    depth = len(shapes)
    b0, beta0, alpha0 = refs[0:3]
    outs = refs[3 : 3 + 4 * depth]
    iterates = outs[0:depth]
    rhs = [b0] + list(outs[depth : 2 * depth])
    betas = [beta0] + list(outs[2 * depth : 3 * depth])
    alphas = [alpha0] + list(outs[3 * depth : 4 * depth])
    scratch = refs[3 + 4 * depth :]
    send_sem, recv_sem = scratch[7 * depth], scratch[7 * depth + 1]
    targets = neighbour_targets(sizes)
    barrier = pltpu.get_barrier_semaphore()
    total = jnp.int32(0)
    for exists, device in targets:

        @pl.when(exists)
        def _():
            pl.semaphore_signal(barrier, inc=1, device_id=device, device_id_type=MESH)

        total = total + exists.astype(jnp.int32)
    tools = [
        level_tools(shapes[l], l, targets, scratch[7 * l : 7 * l + 7], send_sem, recv_sem)
        for l in range(depth)
    ]
    for tool in tools:
        tool[0]()
    for l in range(depth):
        restrict_into(betas[l], betas[l + 1], 0.125)
        restrict_into(alphas[l], alphas[l + 1], 0.125)
    pl.semaphore_wait(barrier, total)
    waits = [tools[l][1](betas[l], 0) for l in range(depth)]
    for l in range(depth):
        tools[l][2](waits[l])
        tools[l][3](betas[l], alphas[l], 0, shifts[l])
    for l in range(depth):
        tools[l][4](rhs[l], iterates[l], rhs[l + 1], SWEEPS, SMOOTH_LOWER)


def down_chain(right_side, beta_coef, alpha_coef):
    sizes = tuple(lax.axis_size(axis) for axis in AXES)
    shapes = [tuple(n >> l for n in right_side.shape) for l in range(LEVELS + 1)]
    shifts = tuple(SHIFT_BASE * 4.0**l for l in range(LEVELS))
    cfg = (sizes, tuple(shapes[:LEVELS]), shifts)
    vmem = pl.BlockSpec(memory_space=pltpu.VMEM)
    out_shapes = [jax.ShapeDtypeStruct(s, jnp.float32) for s in shapes[:LEVELS]]
    out_shapes += [jax.ShapeDtypeStruct(s, jnp.float32) for s in shapes[1:]] * 3
    scratch = []
    for s in shapes[:LEVELS]:
        scratch += level_scratch(s)
    scratch += [
        pltpu.SemaphoreType.DMA((LEVELS, SLOTS, 6)),
        pltpu.SemaphoreType.DMA((LEVELS, SLOTS, 6)),
    ]
    outs = pl.pallas_call(
        functools.partial(down_kernel, cfg),
        out_shape=tuple(out_shapes),
        in_specs=[vmem] * 3,
        out_specs=tuple([vmem] * len(out_shapes)),
        scratch_shapes=scratch,
        compiler_params=pltpu.CompilerParams(collective_id=32, has_side_effects=True),
    )(right_side, beta_coef, alpha_coef)
    iterates = list(outs[0:LEVELS])
    rhs_levels = [right_side] + list(outs[LEVELS : 2 * LEVELS])
    betas = [beta_coef] + list(outs[2 * LEVELS : 3 * LEVELS])
    alphas = [alpha_coef] + list(outs[3 * LEVELS : 4 * LEVELS])
    return iterates, rhs_levels, betas, alphas


def gather_kernel(sizes, row_ref, out_ref, first, dense, second, send_sem, recv_sem):
    index = [lax.axis_index(axis) for axis in AXES]
    nx, ny, nz = sizes

    def device(axis, step):
        return tuple(
            lax.rem(index[a] + step, sizes[a]) if a == axis else index[a] for a in range(3)
        )

    barrier = pltpu.get_barrier_semaphore()
    partners = []
    for axis in (2, 1, 0):
        partners.append([device(axis, step) for step in range(1, sizes[axis])])
    for group in partners:
        for peer in group:
            pl.semaphore_signal(barrier, inc=1, device_id=peer, device_id_type=MESH)
    pl.semaphore_wait(barrier, sum(len(group) for group in partners))

    stages = ((row_ref, first, 2), (dense, second, 1), (second, out_ref, 0))
    for stage, (source, target, axis) in enumerate(stages):
        mine = index[axis]
        waits = []
        for step in range(1, sizes[axis]):
            peer = device(axis, step)
            copy = pltpu.make_async_remote_copy(
                src_ref=source,
                dst_ref=target.at[mine],
                send_sem=send_sem.at[stage, step],
                recv_sem=recv_sem.at[stage, mine],
                device_id=peer,
                device_id_type=MESH,
            )
            copy.start()
            origin = lax.rem(mine + sizes[axis] - step, sizes[axis])
            incoming = pltpu.make_async_remote_copy(
                src_ref=source,
                dst_ref=target.at[origin],
                send_sem=send_sem.at[stage, step],
                recv_sem=recv_sem.at[stage, origin],
                device_id=peer,
                device_id_type=MESH,
            )
            waits.append((copy, incoming))
        if stage == 0:
            target[mine] = source[...]
        else:
            target[mine] = source[...]
        for copy, incoming in waits:
            copy.wait_send()
            incoming.wait_recv()
        if stage == 0:
            for z in range(nz):
                dense[z : z + 1, :] = first[z]


def gather_bottom(packed):
    sizes = tuple(lax.axis_size(axis) for axis in AXES)
    nx, ny, nz = sizes
    width = packed.size
    lanes = -(-width // 128) * 128
    row = jnp.pad(packed.reshape(1, width), ((0, 0), (0, lanes - width)))
    vmem = pl.BlockSpec(memory_space=pltpu.VMEM)
    top = max(sizes)
    whole = pl.pallas_call(
        functools.partial(gather_kernel, sizes),
        out_shape=jax.ShapeDtypeStruct((nx, ny, nz, lanes), jnp.float32),
        in_specs=[vmem],
        out_specs=vmem,
        scratch_shapes=[
            pltpu.VMEM((nz, 1, lanes), jnp.float32),
            pltpu.VMEM((nz, lanes), jnp.float32),
            pltpu.VMEM((ny, nz, lanes), jnp.float32),
            pltpu.SemaphoreType.DMA((3, top)),
            pltpu.SemaphoreType.DMA((3, top)),
        ],
        compiler_params=pltpu.CompilerParams(collective_id=64, has_side_effects=True),
    )(row)
    whole = whole[..., :width].reshape((nx, ny, nz) + packed.shape)
    whole = whole.transpose(3, 0, 4, 1, 5, 2, 6)
    return whole.reshape(
        (packed.shape[0],) + tuple(n * s for n, s in zip(sizes, packed.shape[1:]))
    )


def split_padded(padded):
    return (
        padded[:-2, 1:-1, 1:-1],
        padded[2:, 1:-1, 1:-1],
        padded[1:-1, :-2, 1:-1],
        padded[1:-1, 2:, 1:-1],
        padded[1:-1, 1:-1, :-2],
        padded[1:-1, 1:-1, 2:],
    )


def zero_pad(field):
    return split_padded(jnp.pad(field, 1))


def level_operator(beta_level, alpha_level, beta_sides, shift):
    coeffs = tuple((0.5 * (beta_level + other) for other in beta_sides))
    diagonal = shift * alpha_level
    for coeff in coeffs:
        diagonal = diagonal + coeff
    return (coeffs, diagonal)


def apply_operator(field, operator, pad_field):
    coeffs, diagonal = operator
    others = pad_field(field)
    total = coeffs[0] * others[0]
    for index in range(1, 6):
        total = total + coeffs[index] * others[index]
    return diagonal * field - total


def chebyshev(iterate, rhs_level, operator, count, lower, zero_start, pad_field):
    diagonal = operator[1]
    center = (UPPER_EIG + lower) / 2.0
    half_width = (UPPER_EIG - lower) / 2.0
    sigma_ratio = center / half_width
    rho_old = 1.0 / sigma_ratio
    if zero_start:
        remain = rhs_level
    else:
        remain = rhs_level - apply_operator(iterate, operator, pad_field)
    update = remain / diagonal / center
    iterate = iterate + update
    for sweep_index in range(count - 1):
        remain = rhs_level - apply_operator(iterate, operator, pad_field)
        rho_new = 1.0 / (2.0 * sigma_ratio - rho_old)
        update = rho_new * rho_old * update + 2.0 * rho_new / half_width * (remain / diagonal)
        iterate = iterate + update
        rho_old = rho_new
    return iterate


def restrict_mean(field):
    first, second, third = field.shape
    blocks = field.reshape(first // 2, 2, second // 2, 2, third // 2, 2)
    return jnp.sum(blocks, axis=(1, 3, 5)) * 0.125


def prolong_copy(field):
    return jnp.repeat(jnp.repeat(jnp.repeat(field, 2, axis=0), 2, axis=1), 2, axis=2)


def shards(right_side, alpha_coef, beta_coef):
    smoothed, rhs_levels, betas, alphas = down_chain(right_side, beta_coef, alpha_coef)
    coarse_rhs = rhs_levels[LEVELS]
    local_shape = coarse_rhs.shape
    packed = jnp.stack([coarse_rhs, betas[LEVELS], alphas[LEVELS]])
    index_x = lax.axis_index("gx")
    index_y = lax.axis_index("gy")
    index_z = lax.axis_index("gz")
    packed = gather_bottom(packed)
    whole_rhs = packed[0]
    whole_beta = packed[1]
    whole_alpha = packed[2]
    bottom_operator = level_operator(
        whole_beta, whole_alpha, zero_pad(whole_beta), SHIFT_BASE * 4.0**LEVELS
    )
    whole_correction = chebyshev(
        jnp.zeros_like(whole_rhs), whole_rhs, bottom_operator, BOTTOM, BOTTOM_LOWER, True, zero_pad
    )
    starts = (index_x * local_shape[0], index_y * local_shape[1], index_z * local_shape[2])
    correction = lax.dynamic_slice(whole_correction, starts, local_shape)
    correction, residual_field = up_chain(correction, smoothed, rhs_levels, betas, alphas)
    return (correction, residual_field)


def solution(mesh):
    in_specs = (P("gx", "gy", "gz"), P("gx", "gy", "gz"), P("gx", "gy", "gz"))
    out_specs = (P("gx", "gy", "gz"), P("gx", "gy", "gz"))
    return jax.shard_map(shards, mesh=mesh, in_specs=in_specs, out_specs=out_specs, check_vma=False)
```

```python
import functools

import jax
import jax.numpy as jnp
from jax import lax
from jax.experimental import pallas as pl
from jax.experimental.pallas import tpu as pltpu
from jax.sharding import PartitionSpec as P

MESH = pl.DeviceIdType.MESH
AXES = ("gx", "gy", "gz")
SLOTS = 3

LEVELS = 3
SWEEPS = 4
BOTTOM = 12


SHIFT_BASE = 0.01
UPPER_EIG = 2.0
SMOOTH_LOWER = 0.25
BOTTOM_LOWER = 0.02


def level_kernel(cfg, *refs):
    sizes, shift, count, lower, zero_start, residual, restrict = cfg
    n_in = 3 if zero_start else 4
    b_ref, beta_ref, alpha_ref = refs[0:3]
    v0_ref = None if zero_start else refs[3]
    n_out = 1 + (1 if residual and not restrict else 0) + (3 if restrict else 0)
    outs = refs[n_in : n_in + n_out]
    fld, xh, yh, zh, zsend, coef, dbuf, send_sem, recv_sem = refs[n_in + len(outs) :]
    A, B, C = b_ref.shape
    index = [lax.axis_index(axis) for axis in AXES]
    targets = []
    for k in range(6):
        axis = k // 2
        if k % 2 == 0:
            exists = index[axis] > 0
            other = index[axis] - 1
        else:
            exists = index[axis] < sizes[axis] - 1
            other = index[axis] + 1
        device = tuple(other if a == axis else index[a] for a in range(3))
        targets.append((exists, device))

    def halo(h, slot):
        if h < 2:
            return xh.at[h, slot]
        return yh.at[h - 2, slot] if h < 4 else zh.at[h - 4, slot]

    picks = lax.broadcasted_iota(jnp.int32, (8, C), 0)
    lanes = lax.broadcasted_iota(jnp.int32, (8, C), 1)
    selector = jnp.where(
        (picks == 0) & (lanes == 0), 1.0, jnp.where((picks == 1) & (lanes == C - 1), 1.0, 0.0)
    ).astype(jnp.float32)

    barrier = pltpu.get_barrier_semaphore()
    total = jnp.int32(0)
    for exists, device in targets:

        @pl.when(exists)
        def _():
            pl.semaphore_signal(barrier, inc=1, device_id=device, device_id_type=MESH)

        total = total + exists.astype(jnp.int32)
    for h, (exists, device) in enumerate(targets):

        @pl.when(jnp.logical_not(exists))
        def _():
            for slot in range(SLOTS):
                buf = halo(h, slot)
                buf[...] = jnp.zeros(buf.shape, buf.dtype)

    if restrict:
        coarse_rows = (
            lax.broadcasted_iota(jnp.int32, (B // 2, B), 1) // 2
            == lax.broadcasted_iota(jnp.int32, (B // 2, B), 0)
        ).astype(jnp.float32)
        coarse_cols = (
            lax.broadcasted_iota(jnp.int32, (C, C // 2), 0) // 2
            == lax.broadcasted_iota(jnp.int32, (C, C // 2), 1)
        ).astype(jnp.float32)

        def restrict_into(src, dst, scale):
            for i in range(A // 2):
                pair = src[2 * i] + src[2 * i + 1]
                half = jnp.dot(
                    coarse_rows, pair, precision=lax.Precision.HIGHEST,
                    preferred_element_type=jnp.float32,
                )
                dst[i] = scale * jnp.dot(
                    half, coarse_cols, precision=lax.Precision.HIGHEST,
                    preferred_element_type=jnp.float32,
                )

        restrict_into(beta_ref, outs[2], 0.125)
        restrict_into(alpha_ref, outs[3], 0.125)
    pl.semaphore_wait(barrier, total)

    def exchange_start(src, slot):
        block = src[...].reshape(A * B, C)
        zsend[slot] = lax.dot_general(
            selector, block, (((1,), (1,)), ((), ())),
            precision=lax.Precision.HIGHEST, preferred_element_type=jnp.float32,
        )
        sources = (
            src.at[0], src.at[A - 1],
            src.at[:, 0:8, :], src.at[:, B - 8 : B, :],
            zsend.at[slot], zsend.at[slot],
        )
        waits = []
        for k, (exists, device) in enumerate(targets):
            copy = pltpu.make_async_remote_copy(
                src_ref=sources[k],
                dst_ref=halo(k ^ 1, slot),
                send_sem=send_sem.at[slot, k],
                recv_sem=recv_sem.at[slot, k ^ 1],
                device_id=device,
                device_id_type=MESH,
            )
            pl.when(exists)(copy.start)
            incoming = pltpu.make_async_remote_copy(
                src_ref=sources[k ^ 1],
                dst_ref=halo(k, slot),
                send_sem=send_sem.at[slot, k ^ 1],
                recv_sem=recv_sem.at[slot, k],
                device_id=device,
                device_id_type=MESH,
            )
            waits.append((exists, copy.wait_send))
            waits.append((exists, incoming.wait_recv))
        return waits

    def exchange_finish(waits):
        for exists, wait in waits:
            pl.when(exists)(wait)

    def exchange(src, slot):
        exchange_finish(exchange_start(src, slot))

    rows = lax.broadcasted_iota(jnp.int32, (B, C), 0)
    cols = lax.broadcasted_iota(jnp.int32, (B, C), 1)

    def z_columns(slot):
        return (jnp.transpose(zh[0, slot]), jnp.transpose(zh[1, slot]))

    def sides(src, i, slot, columns):
        here = src[i]
        lower_x = src[i - 1] if i > 0 else xh[0, slot]
        upper_x = src[i + 1] if i < A - 1 else xh[1, slot]
        lower_y = jnp.where(rows == 0, yh[0, slot, i, 7:8, :], pltpu.roll(here, 1, 0))
        upper_y = jnp.where(rows == B - 1, yh[1, slot, i, 0:1, :], pltpu.roll(here, B - 1, 0))
        lower_z = jnp.where(cols == 0, columns[0][i * B : (i + 1) * B, 1:2], pltpu.roll(here, 1, 1))
        upper_z = jnp.where(
            cols == C - 1, columns[1][i * B : (i + 1) * B, 0:1], pltpu.roll(here, C - 1, 1)
        )
        return here, (lower_x, upper_x, lower_y, upper_y, lower_z, upper_z)

    exchanges = [0]

    def next_slot():
        slot = exchanges[0] % SLOTS
        exchanges[0] += 1
        return slot

    slot = next_slot()
    if zero_start:
        exchange(beta_ref, slot)
    else:
        first_slot = next_slot()
        first_waits = exchange_start(v0_ref, first_slot)
        exchange(beta_ref, slot)
    columns = z_columns(slot)
    for i in range(A):
        here, others = sides(beta_ref, i, slot, columns)
        diagonal = shift * alpha_ref[i]
        for k in range(6):
            face = 0.5 * (here + others[k])
            coef[k, i] = face
            diagonal = diagonal + face
        coef[6, i] = diagonal

    def apply_rows(src, slot, i, columns):
        here, others = sides(src, i, slot, columns)
        acc = coef[0, i] * others[0]
        for k in range(1, 6):
            acc = acc + coef[k, i] * others[k]
        return b_ref[i] - (coef[6, i] * here - acc)

    center = (UPPER_EIG + lower) / 2.0
    half_width = (UPPER_EIG - lower) / 2.0
    sigma_ratio = center / half_width
    rho_old = 1.0 / sigma_ratio
    current = 0
    if zero_start:
        for i in range(A):
            update = b_ref[i] / coef[6, i] / center
            dbuf[i] = update
            fld[current, i] = update
    else:
        exchange_finish(first_waits)
        columns = z_columns(first_slot)
        for i in range(A):
            remain = apply_rows(v0_ref, first_slot, i, columns)
            update = remain / coef[6, i] / center
            dbuf[i] = update
            fld[current, i] = v0_ref[i] + update
    for sweep in range(count - 1):
        rho_new = 1.0 / (2.0 * sigma_ratio - rho_old)
        slot = next_slot()
        src = fld.at[current]
        exchange(src, slot)
        last = sweep == count - 2
        dst = outs[0] if last else fld.at[1 - current]
        columns = z_columns(slot)
        for i in range(A):
            remain = apply_rows(src, slot, i, columns)
            update = (rho_new * rho_old) * dbuf[i] + (2.0 * rho_new / half_width) * (
                remain / coef[6, i]
            )
            dbuf[i] = update
            dst[i] = src[i] + update
        rho_old = rho_new
        current = 1 - current
    if residual:
        slot = next_slot()
        exchange(outs[0], slot)
        remain_ref = dbuf if restrict else outs[1]
        columns = z_columns(slot)
        for i in range(A):
            remain_ref[i] = apply_rows(outs[0], slot, i, columns)
        if restrict:
            restrict_into(dbuf, outs[1], 0.5)


KERNELS = {}


def smooth(level_args, shift, count, lower, zero_start, residual, restrict=False):
    A, B, C = level_args[0].shape
    sizes = tuple(lax.axis_size(axis) for axis in AXES)
    cfg = (sizes, shift, count, lower, zero_start, residual, restrict)
    ident = KERNELS.setdefault((A, B, C) + cfg[1:], len(KERNELS))
    vmem = pl.BlockSpec(memory_space=pltpu.VMEM)
    block = jax.ShapeDtypeStruct((A, B, C), jnp.float32)
    coarse = jax.ShapeDtypeStruct((A // 2, B // 2, C // 2), jnp.float32)
    shapes = [block] + ([block] if residual and not restrict else []) + ([coarse] * 3 if restrict else [])
    n_out = len(shapes)
    return pl.pallas_call(
        functools.partial(level_kernel, cfg),
        out_shape=tuple(shapes),
        in_specs=[vmem] * len(level_args),
        out_specs=tuple([vmem] * n_out),
        scratch_shapes=[
            pltpu.VMEM((2, A, B, C), jnp.float32),
            pltpu.VMEM((2, SLOTS, B, C), jnp.float32),
            pltpu.VMEM((2, SLOTS, A, 8, C), jnp.float32),
            pltpu.VMEM((2, SLOTS, 8, A * B), jnp.float32),
            pltpu.VMEM((SLOTS, 8, A * B), jnp.float32),
            pltpu.VMEM((7, A, B, C), jnp.float32),
            pltpu.VMEM((A, B, C), jnp.float32),
            pltpu.SemaphoreType.DMA((SLOTS, 6)),
            pltpu.SemaphoreType.DMA((SLOTS, 6)),
        ],
        compiler_params=pltpu.CompilerParams(collective_id=ident, has_side_effects=True),
    )(*level_args)


def restrict_into(src, dst, scale):
    A, B, C = src.shape
    coarse_rows = (
        lax.broadcasted_iota(jnp.int32, (B // 2, B), 1) // 2
        == lax.broadcasted_iota(jnp.int32, (B // 2, B), 0)
    ).astype(jnp.float32)
    coarse_cols = (
        lax.broadcasted_iota(jnp.int32, (C, C // 2), 0) // 2
        == lax.broadcasted_iota(jnp.int32, (C, C // 2), 1)
    ).astype(jnp.float32)
    for i in range(A // 2):
        pair = src[2 * i] + src[2 * i + 1]
        half = jnp.dot(
            coarse_rows, pair, precision=lax.Precision.HIGHEST, preferred_element_type=jnp.float32
        )
        dst[i] = scale * jnp.dot(
            half, coarse_cols, precision=lax.Precision.HIGHEST, preferred_element_type=jnp.float32
        )


def neighbour_targets(sizes):
    index = [lax.axis_index(axis) for axis in AXES]
    targets = []
    for k in range(6):
        axis = k // 2
        if k % 2 == 0:
            exists = index[axis] > 0
            other = index[axis] - 1
        else:
            exists = index[axis] < sizes[axis] - 1
            other = index[axis] + 1
        device = tuple(other if a == axis else index[a] for a in range(3))
        targets.append((exists, device))
    return targets


def level_tools(shape, level, targets, bufs, send_sem, recv_sem):
    A, B, C = shape
    fld, xh, yh, zh, zsend, coef, dbuf = bufs

    def halo(h, slot):
        if h < 2:
            return xh.at[h, slot]
        return yh.at[h - 2, slot] if h < 4 else zh.at[h - 4, slot]

    picks = lax.broadcasted_iota(jnp.int32, (8, C), 0)
    lanes = lax.broadcasted_iota(jnp.int32, (8, C), 1)
    selector = jnp.where(
        (picks == 0) & (lanes == 0), 1.0, jnp.where((picks == 1) & (lanes == C - 1), 1.0, 0.0)
    ).astype(jnp.float32)
    rows = lax.broadcasted_iota(jnp.int32, (B, C), 0)
    cols = lax.broadcasted_iota(jnp.int32, (B, C), 1)

    def zero_halos():
        for h, (exists, device) in enumerate(targets):

            @pl.when(jnp.logical_not(exists))
            def _():
                for slot in range(SLOTS):
                    buf = halo(h, slot)
                    buf[...] = jnp.zeros(buf.shape, buf.dtype)

    def exchange_start(src, slot):
        block = src[...].reshape(A * B, C)
        zsend[slot] = lax.dot_general(
            selector, block, (((1,), (1,)), ((), ())),
            precision=lax.Precision.HIGHEST, preferred_element_type=jnp.float32,
        )
        sources = (
            src.at[0], src.at[A - 1],
            src.at[:, 0:8, :], src.at[:, B - 8 : B, :],
            zsend.at[slot], zsend.at[slot],
        )
        waits = []
        for k, (exists, device) in enumerate(targets):
            copy = pltpu.make_async_remote_copy(
                src_ref=sources[k],
                dst_ref=halo(k ^ 1, slot),
                send_sem=send_sem.at[level, slot, k],
                recv_sem=recv_sem.at[level, slot, k ^ 1],
                device_id=device,
                device_id_type=MESH,
            )
            pl.when(exists)(copy.start)
            incoming = pltpu.make_async_remote_copy(
                src_ref=sources[k ^ 1],
                dst_ref=halo(k, slot),
                send_sem=send_sem.at[level, slot, k ^ 1],
                recv_sem=recv_sem.at[level, slot, k],
                device_id=device,
                device_id_type=MESH,
            )
            waits.append((exists, copy.wait_send))
            waits.append((exists, incoming.wait_recv))
        return waits

    def exchange_finish(waits):
        for exists, wait in waits:
            pl.when(exists)(wait)

    def exchange(src, slot):
        exchange_finish(exchange_start(src, slot))

    def z_columns(slot):
        return (jnp.transpose(zh[0, slot]), jnp.transpose(zh[1, slot]))

    def sides(src, i, slot, columns):
        here = src[i]
        lower_x = src[i - 1] if i > 0 else xh[0, slot]
        upper_x = src[i + 1] if i < A - 1 else xh[1, slot]
        lower_y = jnp.where(rows == 0, yh[0, slot, i, 7:8, :], pltpu.roll(here, 1, 0))
        upper_y = jnp.where(rows == B - 1, yh[1, slot, i, 0:1, :], pltpu.roll(here, B - 1, 0))
        lower_z = jnp.where(cols == 0, columns[0][i * B : (i + 1) * B, 1:2], pltpu.roll(here, 1, 1))
        upper_z = jnp.where(
            cols == C - 1, columns[1][i * B : (i + 1) * B, 0:1], pltpu.roll(here, C - 1, 1)
        )
        return here, (lower_x, upper_x, lower_y, upper_y, lower_z, upper_z)

    def build_coef(beta_ref, alpha_ref, slot, shift):
        columns = z_columns(slot)
        for i in range(A):
            here, others = sides(beta_ref, i, slot, columns)
            diagonal = shift * alpha_ref[i]
            for k in range(6):
                face = 0.5 * (here + others[k])
                coef[k, i] = face
                diagonal = diagonal + face
            coef[6, i] = diagonal

    def apply_rows(src, b_ref, slot, i, columns):
        here, others = sides(src, i, slot, columns)
        acc = coef[0, i] * others[0]
        for k in range(1, 6):
            acc = acc + coef[k, i] * others[k]
        return b_ref[i] - (coef[6, i] * here - acc)

    def smooth_down(b_ref, v_out, next_rhs, count, lower):
        center = (UPPER_EIG + lower) / 2.0
        half_width = (UPPER_EIG - lower) / 2.0
        sigma_ratio = center / half_width
        rho_old = 1.0 / sigma_ratio
        current = 0
        for i in range(A):
            update = b_ref[i] / coef[6, i] / center
            dbuf[i] = update
            fld[current, i] = update
        slot = 0
        for sweep in range(count - 1):
            rho_new = 1.0 / (2.0 * sigma_ratio - rho_old)
            slot = (slot + 1) % SLOTS
            src = fld.at[current]
            exchange(src, slot)
            columns = z_columns(slot)
            dst = v_out if sweep == count - 2 else fld.at[1 - current]
            for i in range(A):
                remain = apply_rows(src, b_ref, slot, i, columns)
                update = (rho_new * rho_old) * dbuf[i] + (2.0 * rho_new / half_width) * (
                    remain / coef[6, i]
                )
                dbuf[i] = update
                dst[i] = src[i] + update
            rho_old = rho_new
            current = 1 - current
        slot = (slot + 1) % SLOTS
        exchange(v_out, slot)
        columns = z_columns(slot)
        for i in range(A):
            dbuf[i] = apply_rows(v_out, b_ref, slot, i, columns)
        restrict_into(dbuf, next_rhs, 0.5)

    def smooth_up(b_ref, v_out, count, lower, first_slot, first_waits, residual_out):
        start = fld.at[1]
        if first_waits is None:
            exchange(start, first_slot)
        else:
            exchange_finish(first_waits)
        center = (UPPER_EIG + lower) / 2.0
        half_width = (UPPER_EIG - lower) / 2.0
        sigma_ratio = center / half_width
        rho_old = 1.0 / sigma_ratio
        columns = z_columns(first_slot)
        for i in range(A):
            remain = apply_rows(start, b_ref, first_slot, i, columns)
            update = remain / coef[6, i] / center
            dbuf[i] = update
            fld[0, i] = start[i] + update
        current = 0
        slot = first_slot
        for sweep in range(count - 1):
            rho_new = 1.0 / (2.0 * sigma_ratio - rho_old)
            slot = (slot + 1) % SLOTS
            src = fld.at[current]
            exchange(src, slot)
            columns = z_columns(slot)
            dst = v_out if sweep == count - 2 else fld.at[1 - current]
            for i in range(A):
                remain = apply_rows(src, b_ref, slot, i, columns)
                update = (rho_new * rho_old) * dbuf[i] + (2.0 * rho_new / half_width) * (
                    remain / coef[6, i]
                )
                dbuf[i] = update
                dst[i] = src[i] + update
            rho_old = rho_new
            current = 1 - current
        if residual_out is not None:
            slot = (slot + 1) % SLOTS
            exchange(v_out, slot)
            columns = z_columns(slot)
            for i in range(A):
                residual_out[i] = apply_rows(v_out, b_ref, slot, i, columns)

    def prolong_start(coarse, smoothed):
        fine_rows = (
            lax.broadcasted_iota(jnp.int32, (B, B // 2), 0) // 2
            == lax.broadcasted_iota(jnp.int32, (B, B // 2), 1)
        ).astype(jnp.float32)
        fine_cols = (
            lax.broadcasted_iota(jnp.int32, (C // 2, C), 1) // 2
            == lax.broadcasted_iota(jnp.int32, (C // 2, C), 0)
        ).astype(jnp.float32)
        for i in range(A):
            half = jnp.dot(
                fine_rows, coarse[i // 2], precision=lax.Precision.HIGHEST,
                preferred_element_type=jnp.float32,
            )
            fine = jnp.dot(
                half, fine_cols, precision=lax.Precision.HIGHEST,
                preferred_element_type=jnp.float32,
            )
            fld[1, i] = smoothed[i] + fine

    return (
        zero_halos, exchange_start, exchange_finish, build_coef, smooth_down, smooth_up,
        prolong_start, fld,
    )


def up_kernel(cfg, *refs):
    sizes, shapes, shifts = cfg
    depth = len(shapes)
    coarsest = refs[0]
    level_in = [refs[1 + 4 * l : 5 + 4 * l] for l in range(depth)]
    solution_out, residual_out = refs[1 + 4 * depth : 3 + 4 * depth]
    scratch = refs[3 + 4 * depth :]
    results = scratch[7 * depth : 7 * depth + depth - 1]
    send_sem, recv_sem = scratch[8 * depth - 1], scratch[8 * depth]
    targets = neighbour_targets(sizes)
    barrier = pltpu.get_barrier_semaphore()
    total = jnp.int32(0)
    for exists, device in targets:

        @pl.when(exists)
        def _():
            pl.semaphore_signal(barrier, inc=1, device_id=device, device_id_type=MESH)

        total = total + exists.astype(jnp.int32)
    tools = [
        level_tools(shapes[l], l, targets, scratch[7 * l : 7 * l + 7], send_sem, recv_sem)
        for l in range(depth)
    ]
    for tool in tools:
        tool[0]()
    top = depth - 1
    tools[top][6](coarsest, level_in[top][0])
    pl.semaphore_wait(barrier, total)
    first_waits = tools[top][1](tools[top][7].at[1], 1)
    waits = [tools[l][1](level_in[l][2], 0) for l in range(depth)]
    for l in range(depth):
        tools[l][2](waits[l])
        tools[l][3](level_in[l][2], level_in[l][3], 0, shifts[l])
    coarse = None
    for l in range(top, -1, -1):
        if l < top:
            tools[l][6](coarse, level_in[l][0])
        v_out = solution_out if l == 0 else results[l - 1]
        tools[l][5](
            level_in[l][1], v_out, SWEEPS, SMOOTH_LOWER, 1,
            first_waits if l == top else None, residual_out if l == 0 else None,
        )
        coarse = v_out


def up_chain(coarsest, smoothed, rhs_levels, betas, alphas):
    sizes = tuple(lax.axis_size(axis) for axis in AXES)
    shapes = [tuple(x.shape) for x in smoothed]
    shifts = tuple(SHIFT_BASE * 4.0**l for l in range(LEVELS))
    cfg = (sizes, tuple(shapes), shifts)
    vmem = pl.BlockSpec(memory_space=pltpu.VMEM)
    args = [coarsest]
    for l in range(LEVELS):
        args += [smoothed[l], rhs_levels[l], betas[l], alphas[l]]
    scratch = []
    for s in shapes:
        scratch += level_scratch(s)
    scratch += [pltpu.VMEM(s, jnp.float32) for s in shapes[1:]]
    scratch += [
        pltpu.SemaphoreType.DMA((LEVELS, SLOTS, 6)),
        pltpu.SemaphoreType.DMA((LEVELS, SLOTS, 6)),
    ]
    fine = jax.ShapeDtypeStruct(shapes[0], jnp.float32)
    return pl.pallas_call(
        functools.partial(up_kernel, cfg),
        out_shape=(fine, fine),
        in_specs=[vmem] * len(args),
        out_specs=(vmem, vmem),
        scratch_shapes=scratch,
        compiler_params=pltpu.CompilerParams(collective_id=48, has_side_effects=True),
    )(*args)


def level_scratch(shape):
    A, B, C = shape
    return [
        pltpu.VMEM((2, A, B, C), jnp.float32),
        pltpu.VMEM((2, SLOTS, B, C), jnp.float32),
        pltpu.VMEM((2, SLOTS, A, 8, C), jnp.float32),
        pltpu.VMEM((2, SLOTS, 8, A * B), jnp.float32),
        pltpu.VMEM((SLOTS, 8, A * B), jnp.float32),
        pltpu.VMEM((7, A, B, C), jnp.float32),
        pltpu.VMEM((A, B, C), jnp.float32),
    ]


def down_kernel(cfg, *refs):
    sizes, shapes, shifts = cfg
    depth = len(shapes)
    b0, beta0, alpha0 = refs[0:3]
    outs = refs[3 : 3 + 4 * depth]
    iterates = outs[0:depth]
    rhs = [b0] + list(outs[depth : 2 * depth])
    betas = [beta0] + list(outs[2 * depth : 3 * depth])
    alphas = [alpha0] + list(outs[3 * depth : 4 * depth])
    scratch = refs[3 + 4 * depth :]
    send_sem, recv_sem = scratch[7 * depth], scratch[7 * depth + 1]
    targets = neighbour_targets(sizes)
    barrier = pltpu.get_barrier_semaphore()
    total = jnp.int32(0)
    for exists, device in targets:

        @pl.when(exists)
        def _():
            pl.semaphore_signal(barrier, inc=1, device_id=device, device_id_type=MESH)

        total = total + exists.astype(jnp.int32)
    tools = [
        level_tools(shapes[l], l, targets, scratch[7 * l : 7 * l + 7], send_sem, recv_sem)
        for l in range(depth)
    ]
    for tool in tools:
        tool[0]()
    for l in range(depth):
        restrict_into(betas[l], betas[l + 1], 0.125)
        restrict_into(alphas[l], alphas[l + 1], 0.125)
    pl.semaphore_wait(barrier, total)
    waits = [tools[l][1](betas[l], 0) for l in range(depth)]
    for l in range(depth):
        tools[l][2](waits[l])
        tools[l][3](betas[l], alphas[l], 0, shifts[l])
    for l in range(depth):
        tools[l][4](rhs[l], iterates[l], rhs[l + 1], SWEEPS, SMOOTH_LOWER)


def down_chain(right_side, beta_coef, alpha_coef):
    sizes = tuple(lax.axis_size(axis) for axis in AXES)
    shapes = [tuple(n >> l for n in right_side.shape) for l in range(LEVELS + 1)]
    shifts = tuple(SHIFT_BASE * 4.0**l for l in range(LEVELS))
    cfg = (sizes, tuple(shapes[:LEVELS]), shifts)
    vmem = pl.BlockSpec(memory_space=pltpu.VMEM)
    out_shapes = [jax.ShapeDtypeStruct(s, jnp.float32) for s in shapes[:LEVELS]]
    out_shapes += [jax.ShapeDtypeStruct(s, jnp.float32) for s in shapes[1:]] * 3
    scratch = []
    for s in shapes[:LEVELS]:
        scratch += level_scratch(s)
    scratch += [
        pltpu.SemaphoreType.DMA((LEVELS, SLOTS, 6)),
        pltpu.SemaphoreType.DMA((LEVELS, SLOTS, 6)),
    ]
    outs = pl.pallas_call(
        functools.partial(down_kernel, cfg),
        out_shape=tuple(out_shapes),
        in_specs=[vmem] * 3,
        out_specs=tuple([vmem] * len(out_shapes)),
        scratch_shapes=scratch,
        compiler_params=pltpu.CompilerParams(collective_id=32, has_side_effects=True),
    )(right_side, beta_coef, alpha_coef)
    iterates = list(outs[0:LEVELS])
    rhs_levels = [right_side] + list(outs[LEVELS : 2 * LEVELS])
    betas = [beta_coef] + list(outs[2 * LEVELS : 3 * LEVELS])
    alphas = [alpha_coef] + list(outs[3 * LEVELS : 4 * LEVELS])
    return iterates, rhs_levels, betas, alphas


def gather_kernel(sizes, row_ref, out_ref, first, dense, send_sem, recv_sem):
    index = [lax.axis_index(axis) for axis in AXES]
    nx, ny, nz = sizes
    ix, iy, iz = index
    line = [(ix, iy, lax.rem(iz + step, nz)) for step in range(1, nz)]
    plane = []
    for dx in range(nx):
        for dy in range(ny):
            if dx or dy:
                plane.append(((dx, dy), (lax.rem(ix + dx, nx), lax.rem(iy + dy, ny), iz)))

    barrier = pltpu.get_barrier_semaphore()
    for peer in line + [peer for _, peer in plane]:
        pl.semaphore_signal(barrier, inc=1, device_id=peer, device_id_type=MESH)
    pl.semaphore_wait(barrier, len(line) + len(plane))

    waits = []
    for step in range(1, nz):
        copy = pltpu.make_async_remote_copy(
            src_ref=row_ref,
            dst_ref=first.at[iz],
            send_sem=send_sem.at[0, step],
            recv_sem=recv_sem.at[0, iz],
            device_id=line[step - 1],
            device_id_type=MESH,
        )
        copy.start()
        origin = lax.rem(iz + nz - step, nz)
        incoming = pltpu.make_async_remote_copy(
            src_ref=row_ref,
            dst_ref=first.at[origin],
            send_sem=send_sem.at[0, step],
            recv_sem=recv_sem.at[0, origin],
            device_id=line[step - 1],
            device_id_type=MESH,
        )
        waits.append((copy, incoming))
    first[iz] = row_ref[...]
    for copy, incoming in waits:
        copy.wait_send()
        incoming.wait_recv()
    for z in range(nz):
        dense[z : z + 1, :] = first[z]

    mine = ix * ny + iy
    waits = []
    for n, ((dx, dy), peer) in enumerate(plane):
        copy = pltpu.make_async_remote_copy(
            src_ref=dense,
            dst_ref=out_ref.at[ix, iy],
            send_sem=send_sem.at[1, n],
            recv_sem=recv_sem.at[1, mine],
            device_id=peer,
            device_id_type=MESH,
        )
        copy.start()
        ox = lax.rem(ix + nx - dx, nx)
        oy = lax.rem(iy + ny - dy, ny)
        incoming = pltpu.make_async_remote_copy(
            src_ref=dense,
            dst_ref=out_ref.at[ox, oy],
            send_sem=send_sem.at[1, n],
            recv_sem=recv_sem.at[1, ox * ny + oy],
            device_id=peer,
            device_id_type=MESH,
        )
        waits.append((copy, incoming))
    out_ref[ix, iy] = dense[...]
    for copy, incoming in waits:
        copy.wait_send()
        incoming.wait_recv()


def gather_bottom(packed):
    sizes = tuple(lax.axis_size(axis) for axis in AXES)
    nx, ny, nz = sizes
    width = packed.size
    lanes = -(-width // 128) * 128
    row = jnp.pad(packed.reshape(1, width), ((0, 0), (0, lanes - width)))
    vmem = pl.BlockSpec(memory_space=pltpu.VMEM)
    top = max(nz, nx * ny)
    whole = pl.pallas_call(
        functools.partial(gather_kernel, sizes),
        out_shape=jax.ShapeDtypeStruct((nx, ny, nz, lanes), jnp.float32),
        in_specs=[vmem],
        out_specs=vmem,
        scratch_shapes=[
            pltpu.VMEM((nz, 1, lanes), jnp.float32),
            pltpu.VMEM((nz, lanes), jnp.float32),
            pltpu.SemaphoreType.DMA((2, top)),
            pltpu.SemaphoreType.DMA((2, top)),
        ],
        compiler_params=pltpu.CompilerParams(collective_id=64, has_side_effects=True),
    )(row)
    whole = whole[..., :width].reshape((nx, ny, nz) + packed.shape)
    whole = whole.transpose(3, 0, 4, 1, 5, 2, 6)
    return whole.reshape(
        (packed.shape[0],) + tuple(n * s for n, s in zip(sizes, packed.shape[1:]))
    )


def split_padded(padded):
    return (
        padded[:-2, 1:-1, 1:-1],
        padded[2:, 1:-1, 1:-1],
        padded[1:-1, :-2, 1:-1],
        padded[1:-1, 2:, 1:-1],
        padded[1:-1, 1:-1, :-2],
        padded[1:-1, 1:-1, 2:],
    )


def zero_pad(field):
    return split_padded(jnp.pad(field, 1))


def level_operator(beta_level, alpha_level, beta_sides, shift):
    coeffs = tuple((0.5 * (beta_level + other) for other in beta_sides))
    diagonal = shift * alpha_level
    for coeff in coeffs:
        diagonal = diagonal + coeff
    return (coeffs, diagonal)


def apply_operator(field, operator, pad_field):
    coeffs, diagonal = operator
    others = pad_field(field)
    total = coeffs[0] * others[0]
    for index in range(1, 6):
        total = total + coeffs[index] * others[index]
    return diagonal * field - total


def chebyshev(iterate, rhs_level, operator, count, lower, zero_start, pad_field):
    diagonal = operator[1]
    center = (UPPER_EIG + lower) / 2.0
    half_width = (UPPER_EIG - lower) / 2.0
    sigma_ratio = center / half_width
    rho_old = 1.0 / sigma_ratio
    if zero_start:
        remain = rhs_level
    else:
        remain = rhs_level - apply_operator(iterate, operator, pad_field)
    update = remain / diagonal / center
    iterate = iterate + update
    for sweep_index in range(count - 1):
        remain = rhs_level - apply_operator(iterate, operator, pad_field)
        rho_new = 1.0 / (2.0 * sigma_ratio - rho_old)
        update = rho_new * rho_old * update + 2.0 * rho_new / half_width * (remain / diagonal)
        iterate = iterate + update
        rho_old = rho_new
    return iterate


def restrict_mean(field):
    first, second, third = field.shape
    blocks = field.reshape(first // 2, 2, second // 2, 2, third // 2, 2)
    return jnp.sum(blocks, axis=(1, 3, 5)) * 0.125


def prolong_copy(field):
    return jnp.repeat(jnp.repeat(jnp.repeat(field, 2, axis=0), 2, axis=1), 2, axis=2)


def shards(right_side, alpha_coef, beta_coef):
    smoothed, rhs_levels, betas, alphas = down_chain(right_side, beta_coef, alpha_coef)
    coarse_rhs = rhs_levels[LEVELS]
    local_shape = coarse_rhs.shape
    packed = jnp.stack([coarse_rhs, betas[LEVELS], alphas[LEVELS]])
    index_x = lax.axis_index("gx")
    index_y = lax.axis_index("gy")
    index_z = lax.axis_index("gz")
    packed = gather_bottom(packed)
    whole_rhs = packed[0]
    whole_beta = packed[1]
    whole_alpha = packed[2]
    bottom_operator = level_operator(
        whole_beta, whole_alpha, zero_pad(whole_beta), SHIFT_BASE * 4.0**LEVELS
    )
    whole_correction = chebyshev(
        jnp.zeros_like(whole_rhs), whole_rhs, bottom_operator, BOTTOM, BOTTOM_LOWER, True, zero_pad
    )
    starts = (index_x * local_shape[0], index_y * local_shape[1], index_z * local_shape[2])
    correction = lax.dynamic_slice(whole_correction, starts, local_shape)
    correction, residual_field = up_chain(correction, smoothed, rhs_levels, betas, alphas)
    return (correction, residual_field)


def solution(mesh):
    in_specs = (P("gx", "gy", "gz"), P("gx", "gy", "gz"), P("gx", "gy", "gz"))
    out_specs = (P("gx", "gy", "gz"), P("gx", "gy", "gz"))
    return jax.shard_map(shards, mesh=mesh, in_specs=in_specs, out_specs=out_specs, check_vma=False)
```

```python
import functools

import jax
import jax.numpy as jnp
from jax import lax
from jax.experimental import pallas as pl
from jax.experimental.pallas import tpu as pltpu
from jax.sharding import PartitionSpec as P

MESH = pl.DeviceIdType.MESH
AXES = ("gx", "gy", "gz")
SLOTS = 3

LEVELS = 3
SWEEPS = 4
BOTTOM = 12


SHIFT_BASE = 0.01
UPPER_EIG = 2.0
SMOOTH_LOWER = 0.25
BOTTOM_LOWER = 0.02


def level_kernel(cfg, *refs):
    sizes, shift, count, lower, zero_start, residual, restrict = cfg
    n_in = 3 if zero_start else 4
    b_ref, beta_ref, alpha_ref = refs[0:3]
    v0_ref = None if zero_start else refs[3]
    n_out = 1 + (1 if residual and not restrict else 0) + (3 if restrict else 0)
    outs = refs[n_in : n_in + n_out]
    fld, xh, yh, zh, zsend, coef, dbuf, send_sem, recv_sem = refs[n_in + len(outs) :]
    A, B, C = b_ref.shape
    index = [lax.axis_index(axis) for axis in AXES]
    targets = []
    for k in range(6):
        axis = k // 2
        if k % 2 == 0:
            exists = index[axis] > 0
            other = index[axis] - 1
        else:
            exists = index[axis] < sizes[axis] - 1
            other = index[axis] + 1
        device = tuple(other if a == axis else index[a] for a in range(3))
        targets.append((exists, device))

    def halo(h, slot):
        if h < 2:
            return xh.at[h, slot]
        return yh.at[h - 2, slot] if h < 4 else zh.at[h - 4, slot]

    picks = lax.broadcasted_iota(jnp.int32, (8, C), 0)
    lanes = lax.broadcasted_iota(jnp.int32, (8, C), 1)
    selector = jnp.where(
        (picks == 0) & (lanes == 0), 1.0, jnp.where((picks == 1) & (lanes == C - 1), 1.0, 0.0)
    ).astype(jnp.float32)

    barrier = pltpu.get_barrier_semaphore()
    total = jnp.int32(0)
    for exists, device in targets:

        @pl.when(exists)
        def _():
            pl.semaphore_signal(barrier, inc=1, device_id=device, device_id_type=MESH)

        total = total + exists.astype(jnp.int32)
    for h, (exists, device) in enumerate(targets):

        @pl.when(jnp.logical_not(exists))
        def _():
            for slot in range(SLOTS):
                buf = halo(h, slot)
                buf[...] = jnp.zeros(buf.shape, buf.dtype)

    if restrict:
        coarse_rows = (
            lax.broadcasted_iota(jnp.int32, (B // 2, B), 1) // 2
            == lax.broadcasted_iota(jnp.int32, (B // 2, B), 0)
        ).astype(jnp.float32)
        coarse_cols = (
            lax.broadcasted_iota(jnp.int32, (C, C // 2), 0) // 2
            == lax.broadcasted_iota(jnp.int32, (C, C // 2), 1)
        ).astype(jnp.float32)

        def restrict_into(src, dst, scale):
            for i in range(A // 2):
                pair = src[2 * i] + src[2 * i + 1]
                half = jnp.dot(
                    coarse_rows, pair, precision=lax.Precision.HIGHEST,
                    preferred_element_type=jnp.float32,
                )
                dst[i] = scale * jnp.dot(
                    half, coarse_cols, precision=lax.Precision.HIGHEST,
                    preferred_element_type=jnp.float32,
                )

        restrict_into(beta_ref, outs[2], 0.125)
        restrict_into(alpha_ref, outs[3], 0.125)
    pl.semaphore_wait(barrier, total)

    def exchange_start(src, slot):
        block = src[...].reshape(A * B, C)
        zsend[slot] = lax.dot_general(
            selector, block, (((1,), (1,)), ((), ())),
            precision=lax.Precision.HIGHEST, preferred_element_type=jnp.float32,
        )
        sources = (
            src.at[0], src.at[A - 1],
            src.at[:, 0:8, :], src.at[:, B - 8 : B, :],
            zsend.at[slot], zsend.at[slot],
        )
        waits = []
        for k, (exists, device) in enumerate(targets):
            copy = pltpu.make_async_remote_copy(
                src_ref=sources[k],
                dst_ref=halo(k ^ 1, slot),
                send_sem=send_sem.at[slot, k],
                recv_sem=recv_sem.at[slot, k ^ 1],
                device_id=device,
                device_id_type=MESH,
            )
            pl.when(exists)(copy.start)
            incoming = pltpu.make_async_remote_copy(
                src_ref=sources[k ^ 1],
                dst_ref=halo(k, slot),
                send_sem=send_sem.at[slot, k ^ 1],
                recv_sem=recv_sem.at[slot, k],
                device_id=device,
                device_id_type=MESH,
            )
            waits.append((exists, copy.wait_send))
            waits.append((exists, incoming.wait_recv))
        return waits

    def exchange_finish(waits):
        for exists, wait in waits:
            pl.when(exists)(wait)

    def exchange(src, slot):
        exchange_finish(exchange_start(src, slot))

    rows = lax.broadcasted_iota(jnp.int32, (B, C), 0)
    cols = lax.broadcasted_iota(jnp.int32, (B, C), 1)

    def z_columns(slot):
        return (jnp.transpose(zh[0, slot]), jnp.transpose(zh[1, slot]))

    def sides(src, i, slot, columns):
        here = src[i]
        lower_x = src[i - 1] if i > 0 else xh[0, slot]
        upper_x = src[i + 1] if i < A - 1 else xh[1, slot]
        lower_y = jnp.where(rows == 0, yh[0, slot, i, 7:8, :], pltpu.roll(here, 1, 0))
        upper_y = jnp.where(rows == B - 1, yh[1, slot, i, 0:1, :], pltpu.roll(here, B - 1, 0))
        lower_z = jnp.where(cols == 0, columns[0][i * B : (i + 1) * B, 1:2], pltpu.roll(here, 1, 1))
        upper_z = jnp.where(
            cols == C - 1, columns[1][i * B : (i + 1) * B, 0:1], pltpu.roll(here, C - 1, 1)
        )
        return here, (lower_x, upper_x, lower_y, upper_y, lower_z, upper_z)

    exchanges = [0]

    def next_slot():
        slot = exchanges[0] % SLOTS
        exchanges[0] += 1
        return slot

    slot = next_slot()
    if zero_start:
        exchange(beta_ref, slot)
    else:
        first_slot = next_slot()
        first_waits = exchange_start(v0_ref, first_slot)
        exchange(beta_ref, slot)
    columns = z_columns(slot)
    for i in range(A):
        here, others = sides(beta_ref, i, slot, columns)
        diagonal = shift * alpha_ref[i]
        for k in range(6):
            face = 0.5 * (here + others[k])
            coef[k, i] = face
            diagonal = diagonal + face
        coef[6, i] = diagonal

    def apply_rows(src, slot, i, columns):
        here, others = sides(src, i, slot, columns)
        acc = coef[0, i] * others[0]
        for k in range(1, 6):
            acc = acc + coef[k, i] * others[k]
        return b_ref[i] - (coef[6, i] * here - acc)

    center = (UPPER_EIG + lower) / 2.0
    half_width = (UPPER_EIG - lower) / 2.0
    sigma_ratio = center / half_width
    rho_old = 1.0 / sigma_ratio
    current = 0
    if zero_start:
        for i in range(A):
            update = b_ref[i] / coef[6, i] / center
            dbuf[i] = update
            fld[current, i] = update
    else:
        exchange_finish(first_waits)
        columns = z_columns(first_slot)
        for i in range(A):
            remain = apply_rows(v0_ref, first_slot, i, columns)
            update = remain / coef[6, i] / center
            dbuf[i] = update
            fld[current, i] = v0_ref[i] + update
    for sweep in range(count - 1):
        rho_new = 1.0 / (2.0 * sigma_ratio - rho_old)
        slot = next_slot()
        src = fld.at[current]
        exchange(src, slot)
        last = sweep == count - 2
        dst = outs[0] if last else fld.at[1 - current]
        columns = z_columns(slot)
        for i in range(A):
            remain = apply_rows(src, slot, i, columns)
            update = (rho_new * rho_old) * dbuf[i] + (2.0 * rho_new / half_width) * (
                remain / coef[6, i]
            )
            dbuf[i] = update
            dst[i] = src[i] + update
        rho_old = rho_new
        current = 1 - current
    if residual:
        slot = next_slot()
        exchange(outs[0], slot)
        remain_ref = dbuf if restrict else outs[1]
        columns = z_columns(slot)
        for i in range(A):
            remain_ref[i] = apply_rows(outs[0], slot, i, columns)
        if restrict:
            restrict_into(dbuf, outs[1], 0.5)


KERNELS = {}


def smooth(level_args, shift, count, lower, zero_start, residual, restrict=False):
    A, B, C = level_args[0].shape
    sizes = tuple(lax.axis_size(axis) for axis in AXES)
    cfg = (sizes, shift, count, lower, zero_start, residual, restrict)
    ident = KERNELS.setdefault((A, B, C) + cfg[1:], len(KERNELS))
    vmem = pl.BlockSpec(memory_space=pltpu.VMEM)
    block = jax.ShapeDtypeStruct((A, B, C), jnp.float32)
    coarse = jax.ShapeDtypeStruct((A // 2, B // 2, C // 2), jnp.float32)
    shapes = [block] + ([block] if residual and not restrict else []) + ([coarse] * 3 if restrict else [])
    n_out = len(shapes)
    return pl.pallas_call(
        functools.partial(level_kernel, cfg),
        out_shape=tuple(shapes),
        in_specs=[vmem] * len(level_args),
        out_specs=tuple([vmem] * n_out),
        scratch_shapes=[
            pltpu.VMEM((2, A, B, C), jnp.float32),
            pltpu.VMEM((2, SLOTS, B, C), jnp.float32),
            pltpu.VMEM((2, SLOTS, A, 8, C), jnp.float32),
            pltpu.VMEM((2, SLOTS, 8, A * B), jnp.float32),
            pltpu.VMEM((SLOTS, 8, A * B), jnp.float32),
            pltpu.VMEM((7, A, B, C), jnp.float32),
            pltpu.VMEM((A, B, C), jnp.float32),
            pltpu.SemaphoreType.DMA((SLOTS, 6)),
            pltpu.SemaphoreType.DMA((SLOTS, 6)),
        ],
        compiler_params=pltpu.CompilerParams(collective_id=ident, has_side_effects=True),
    )(*level_args)


def restrict_into(src, dst, scale):
    A, B, C = src.shape
    coarse_rows = (
        lax.broadcasted_iota(jnp.int32, (B // 2, B), 1) // 2
        == lax.broadcasted_iota(jnp.int32, (B // 2, B), 0)
    ).astype(jnp.float32)
    coarse_cols = (
        lax.broadcasted_iota(jnp.int32, (C, C // 2), 0) // 2
        == lax.broadcasted_iota(jnp.int32, (C, C // 2), 1)
    ).astype(jnp.float32)
    for i in range(A // 2):
        pair = src[2 * i] + src[2 * i + 1]
        half = jnp.dot(
            coarse_rows, pair, precision=lax.Precision.HIGHEST, preferred_element_type=jnp.float32
        )
        dst[i] = scale * jnp.dot(
            half, coarse_cols, precision=lax.Precision.HIGHEST, preferred_element_type=jnp.float32
        )


def neighbour_targets(sizes):
    index = [lax.axis_index(axis) for axis in AXES]
    targets = []
    for k in range(6):
        axis = k // 2
        if k % 2 == 0:
            exists = index[axis] > 0
            other = index[axis] - 1
        else:
            exists = index[axis] < sizes[axis] - 1
            other = index[axis] + 1
        device = tuple(other if a == axis else index[a] for a in range(3))
        targets.append((exists, device))
    return targets


def level_tools(shape, level, targets, bufs, send_sem, recv_sem):
    A, B, C = shape
    fld, xh, yh, zh, zsend, coef, dbuf = bufs

    def halo(h, slot):
        if h < 2:
            return xh.at[h, slot]
        return yh.at[h - 2, slot] if h < 4 else zh.at[h - 4, slot]

    picks = lax.broadcasted_iota(jnp.int32, (8, C), 0)
    lanes = lax.broadcasted_iota(jnp.int32, (8, C), 1)
    selector = jnp.where(
        (picks == 0) & (lanes == 0), 1.0, jnp.where((picks == 1) & (lanes == C - 1), 1.0, 0.0)
    ).astype(jnp.float32)
    rows = lax.broadcasted_iota(jnp.int32, (B, C), 0)
    cols = lax.broadcasted_iota(jnp.int32, (B, C), 1)

    def zero_halos():
        for h, (exists, device) in enumerate(targets):

            @pl.when(jnp.logical_not(exists))
            def _():
                for slot in range(SLOTS):
                    buf = halo(h, slot)
                    buf[...] = jnp.zeros(buf.shape, buf.dtype)

    def exchange_start(src, slot):
        block = src[...].reshape(A * B, C)
        zsend[slot] = lax.dot_general(
            selector, block, (((1,), (1,)), ((), ())),
            precision=lax.Precision.HIGHEST, preferred_element_type=jnp.float32,
        )
        sources = (
            src.at[0], src.at[A - 1],
            src.at[:, 0:8, :], src.at[:, B - 8 : B, :],
            zsend.at[slot], zsend.at[slot],
        )
        waits = []
        for k, (exists, device) in enumerate(targets):
            copy = pltpu.make_async_remote_copy(
                src_ref=sources[k],
                dst_ref=halo(k ^ 1, slot),
                send_sem=send_sem.at[level, slot, k],
                recv_sem=recv_sem.at[level, slot, k ^ 1],
                device_id=device,
                device_id_type=MESH,
            )
            pl.when(exists)(copy.start)
            incoming = pltpu.make_async_remote_copy(
                src_ref=sources[k ^ 1],
                dst_ref=halo(k, slot),
                send_sem=send_sem.at[level, slot, k ^ 1],
                recv_sem=recv_sem.at[level, slot, k],
                device_id=device,
                device_id_type=MESH,
            )
            waits.append((exists, copy.wait_send))
            waits.append((exists, incoming.wait_recv))
        return waits

    def exchange_finish(waits):
        for exists, wait in waits:
            pl.when(exists)(wait)

    def exchange(src, slot):
        exchange_finish(exchange_start(src, slot))

    def z_columns(slot):
        return (jnp.transpose(zh[0, slot]), jnp.transpose(zh[1, slot]))

    def sides(src, i, slot, columns):
        here = src[i]
        lower_x = src[i - 1] if i > 0 else xh[0, slot]
        upper_x = src[i + 1] if i < A - 1 else xh[1, slot]
        lower_y = jnp.where(rows == 0, yh[0, slot, i, 7:8, :], pltpu.roll(here, 1, 0))
        upper_y = jnp.where(rows == B - 1, yh[1, slot, i, 0:1, :], pltpu.roll(here, B - 1, 0))
        lower_z = jnp.where(cols == 0, columns[0][i * B : (i + 1) * B, 1:2], pltpu.roll(here, 1, 1))
        upper_z = jnp.where(
            cols == C - 1, columns[1][i * B : (i + 1) * B, 0:1], pltpu.roll(here, C - 1, 1)
        )
        return here, (lower_x, upper_x, lower_y, upper_y, lower_z, upper_z)

    def build_coef(beta_ref, alpha_ref, slot, shift):
        columns = z_columns(slot)
        for i in range(A):
            here, others = sides(beta_ref, i, slot, columns)
            diagonal = shift * alpha_ref[i]
            for k in range(6):
                face = 0.5 * (here + others[k])
                coef[k, i] = face
                diagonal = diagonal + face
            coef[6, i] = diagonal

    def apply_rows(src, b_ref, slot, i, columns):
        here, others = sides(src, i, slot, columns)
        acc = coef[0, i] * others[0]
        for k in range(1, 6):
            acc = acc + coef[k, i] * others[k]
        return b_ref[i] - (coef[6, i] * here - acc)

    def smooth_down(b_ref, v_out, next_rhs, count, lower):
        center = (UPPER_EIG + lower) / 2.0
        half_width = (UPPER_EIG - lower) / 2.0
        sigma_ratio = center / half_width
        rho_old = 1.0 / sigma_ratio
        current = 0
        for i in range(A):
            update = b_ref[i] / coef[6, i] / center
            dbuf[i] = update
            fld[current, i] = update
        slot = 0
        for sweep in range(count - 1):
            rho_new = 1.0 / (2.0 * sigma_ratio - rho_old)
            slot = (slot + 1) % SLOTS
            src = fld.at[current]
            exchange(src, slot)
            columns = z_columns(slot)
            dst = v_out if sweep == count - 2 else fld.at[1 - current]
            for i in range(A):
                remain = apply_rows(src, b_ref, slot, i, columns)
                update = (rho_new * rho_old) * dbuf[i] + (2.0 * rho_new / half_width) * (
                    remain / coef[6, i]
                )
                dbuf[i] = update
                dst[i] = src[i] + update
            rho_old = rho_new
            current = 1 - current
        slot = (slot + 1) % SLOTS
        exchange(v_out, slot)
        columns = z_columns(slot)
        for i in range(A):
            dbuf[i] = apply_rows(v_out, b_ref, slot, i, columns)
        restrict_into(dbuf, next_rhs, 0.5)

    def smooth_up(b_ref, v_out, count, lower, first_slot, first_waits, residual_out):
        start = fld.at[1]
        if first_waits is None:
            exchange(start, first_slot)
        else:
            exchange_finish(first_waits)
        center = (UPPER_EIG + lower) / 2.0
        half_width = (UPPER_EIG - lower) / 2.0
        sigma_ratio = center / half_width
        rho_old = 1.0 / sigma_ratio
        columns = z_columns(first_slot)
        for i in range(A):
            remain = apply_rows(start, b_ref, first_slot, i, columns)
            update = remain / coef[6, i] / center
            dbuf[i] = update
            fld[0, i] = start[i] + update
        current = 0
        slot = first_slot
        for sweep in range(count - 1):
            rho_new = 1.0 / (2.0 * sigma_ratio - rho_old)
            slot = (slot + 1) % SLOTS
            src = fld.at[current]
            exchange(src, slot)
            columns = z_columns(slot)
            dst = v_out if sweep == count - 2 else fld.at[1 - current]
            for i in range(A):
                remain = apply_rows(src, b_ref, slot, i, columns)
                update = (rho_new * rho_old) * dbuf[i] + (2.0 * rho_new / half_width) * (
                    remain / coef[6, i]
                )
                dbuf[i] = update
                dst[i] = src[i] + update
            rho_old = rho_new
            current = 1 - current
        if residual_out is not None:
            slot = (slot + 1) % SLOTS
            exchange(v_out, slot)
            columns = z_columns(slot)
            for i in range(A):
                residual_out[i] = apply_rows(v_out, b_ref, slot, i, columns)

    def prolong_start(coarse, smoothed):
        fine_rows = (
            lax.broadcasted_iota(jnp.int32, (B, B // 2), 0) // 2
            == lax.broadcasted_iota(jnp.int32, (B, B // 2), 1)
        ).astype(jnp.float32)
        fine_cols = (
            lax.broadcasted_iota(jnp.int32, (C // 2, C), 1) // 2
            == lax.broadcasted_iota(jnp.int32, (C // 2, C), 0)
        ).astype(jnp.float32)
        for i in range(A):
            half = jnp.dot(
                fine_rows, coarse[i // 2], precision=lax.Precision.HIGHEST,
                preferred_element_type=jnp.float32,
            )
            fine = jnp.dot(
                half, fine_cols, precision=lax.Precision.HIGHEST,
                preferred_element_type=jnp.float32,
            )
            fld[1, i] = smoothed[i] + fine

    return (
        zero_halos, exchange_start, exchange_finish, build_coef, smooth_down, smooth_up,
        prolong_start, fld,
    )


def up_kernel(cfg, *refs):
    sizes, shapes, shifts = cfg
    depth = len(shapes)
    coarsest = refs[0]
    level_in = [refs[1 + 4 * l : 5 + 4 * l] for l in range(depth)]
    solution_out, residual_out = refs[1 + 4 * depth : 3 + 4 * depth]
    scratch = refs[3 + 4 * depth :]
    results = scratch[7 * depth : 7 * depth + depth - 1]
    send_sem, recv_sem = scratch[8 * depth - 1], scratch[8 * depth]
    targets = neighbour_targets(sizes)
    barrier = pltpu.get_barrier_semaphore()
    total = jnp.int32(0)
    for exists, device in targets:

        @pl.when(exists)
        def _():
            pl.semaphore_signal(barrier, inc=1, device_id=device, device_id_type=MESH)

        total = total + exists.astype(jnp.int32)
    tools = [
        level_tools(shapes[l], l, targets, scratch[7 * l : 7 * l + 7], send_sem, recv_sem)
        for l in range(depth)
    ]
    for tool in tools:
        tool[0]()
    top = depth - 1
    tools[top][6](coarsest, level_in[top][0])
    pl.semaphore_wait(barrier, total)
    first_waits = tools[top][1](tools[top][7].at[1], 1)
    waits = [tools[l][1](level_in[l][2], 0) for l in range(depth)]
    for l in range(depth):
        tools[l][2](waits[l])
        tools[l][3](level_in[l][2], level_in[l][3], 0, shifts[l])
    coarse = None
    for l in range(top, -1, -1):
        if l < top:
            tools[l][6](coarse, level_in[l][0])
        v_out = solution_out if l == 0 else results[l - 1]
        tools[l][5](
            level_in[l][1], v_out, SWEEPS, SMOOTH_LOWER, 1,
            first_waits if l == top else None, residual_out if l == 0 else None,
        )
        coarse = v_out


def up_chain(coarsest, smoothed, rhs_levels, betas, alphas):
    sizes = tuple(lax.axis_size(axis) for axis in AXES)
    shapes = [tuple(x.shape) for x in smoothed]
    shifts = tuple(SHIFT_BASE * 4.0**l for l in range(LEVELS))
    cfg = (sizes, tuple(shapes), shifts)
    vmem = pl.BlockSpec(memory_space=pltpu.VMEM)
    args = [coarsest]
    for l in range(LEVELS):
        args += [smoothed[l], rhs_levels[l], betas[l], alphas[l]]
    scratch = []
    for s in shapes:
        scratch += level_scratch(s)
    scratch += [pltpu.VMEM(s, jnp.float32) for s in shapes[1:]]
    scratch += [
        pltpu.SemaphoreType.DMA((LEVELS, SLOTS, 6)),
        pltpu.SemaphoreType.DMA((LEVELS, SLOTS, 6)),
    ]
    fine = jax.ShapeDtypeStruct(shapes[0], jnp.float32)
    return pl.pallas_call(
        functools.partial(up_kernel, cfg),
        out_shape=(fine, fine),
        in_specs=[vmem] * len(args),
        out_specs=(vmem, vmem),
        scratch_shapes=scratch,
        compiler_params=pltpu.CompilerParams(collective_id=48, has_side_effects=True),
    )(*args)


def level_scratch(shape):
    A, B, C = shape
    return [
        pltpu.VMEM((2, A, B, C), jnp.float32),
        pltpu.VMEM((2, SLOTS, B, C), jnp.float32),
        pltpu.VMEM((2, SLOTS, A, 8, C), jnp.float32),
        pltpu.VMEM((2, SLOTS, 8, A * B), jnp.float32),
        pltpu.VMEM((SLOTS, 8, A * B), jnp.float32),
        pltpu.VMEM((7, A, B, C), jnp.float32),
        pltpu.VMEM((A, B, C), jnp.float32),
    ]


def down_kernel(cfg, *refs):
    sizes, shapes, shifts = cfg
    depth = len(shapes)
    b0, beta0, alpha0 = refs[0:3]
    outs = refs[3 : 3 + 4 * depth]
    iterates = outs[0:depth]
    rhs = [b0] + list(outs[depth : 2 * depth])
    betas = [beta0] + list(outs[2 * depth : 3 * depth])
    alphas = [alpha0] + list(outs[3 * depth : 4 * depth])
    gathered = refs[3 + 4 * depth]
    scratch = refs[4 + 4 * depth :]
    send_sem, recv_sem = scratch[7 * depth], scratch[7 * depth + 1]
    row, first, dense, gsend, grecv = scratch[7 * depth + 2 :]
    targets = neighbour_targets(sizes)
    line, plane = gather_peers(sizes)
    barrier = pltpu.get_barrier_semaphore()
    for peer in line + [peer for _, peer in plane]:
        pl.semaphore_signal(barrier, inc=1, device_id=peer, device_id_type=MESH)
    total = len(line) + len(plane)
    tools = [
        level_tools(shapes[l], l, targets, scratch[7 * l : 7 * l + 7], send_sem, recv_sem)
        for l in range(depth)
    ]
    for tool in tools:
        tool[0]()
    for l in range(depth):
        restrict_into(betas[l], betas[l + 1], 0.125)
        restrict_into(alphas[l], alphas[l + 1], 0.125)
    pl.semaphore_wait(barrier, total)
    waits = [tools[l][1](betas[l], 0) for l in range(depth)]
    for l in range(depth):
        tools[l][2](waits[l])
        tools[l][3](betas[l], alphas[l], 0, shifts[l])
    for l in range(depth):
        tools[l][4](rhs[l], iterates[l], rhs[l + 1], SWEEPS, SMOOTH_LOWER)
    lanes = row.shape[1]
    packed = jnp.zeros((1, lanes), jnp.float32)
    offset = 0
    for part in (rhs[depth], betas[depth], alphas[depth]):
        pa, pb, pc = part.shape
        for x in range(pa):
            for j in range(pb):
                pick = (lax.broadcasted_iota(jnp.int32, (1, pb), 1) == j).astype(jnp.float32)
                line_values = jnp.dot(
                    pick, part[x], precision=lax.Precision.HIGHEST,
                    preferred_element_type=jnp.float32,
                )
                place = (
                    lax.broadcasted_iota(jnp.int32, (pc, lanes), 0) + offset
                    == lax.broadcasted_iota(jnp.int32, (pc, lanes), 1)
                ).astype(jnp.float32)
                packed = packed + jnp.dot(
                    line_values, place, precision=lax.Precision.HIGHEST,
                    preferred_element_type=jnp.float32,
                )
                offset += pc
    row[...] = packed
    gather_stages(sizes, line, plane, row, gathered, first, dense, gsend, grecv)


def down_chain(right_side, beta_coef, alpha_coef):
    sizes = tuple(lax.axis_size(axis) for axis in AXES)
    shapes = [tuple(n >> l for n in right_side.shape) for l in range(LEVELS + 1)]
    shifts = tuple(SHIFT_BASE * 4.0**l for l in range(LEVELS))
    cfg = (sizes, tuple(shapes[:LEVELS]), shifts)
    vmem = pl.BlockSpec(memory_space=pltpu.VMEM)
    out_shapes = [jax.ShapeDtypeStruct(s, jnp.float32) for s in shapes[:LEVELS]]
    out_shapes += [jax.ShapeDtypeStruct(s, jnp.float32) for s in shapes[1:]] * 3
    scratch = []
    for s in shapes[:LEVELS]:
        scratch += level_scratch(s)
    nx, ny, nz = sizes
    width = 3 * shapes[LEVELS][0] * shapes[LEVELS][1] * shapes[LEVELS][2]
    lanes = -(-width // 128) * 128
    top = max(nz, nx * ny)
    out_shapes.append(jax.ShapeDtypeStruct((nx, ny, nz, lanes), jnp.float32))
    scratch += [
        pltpu.SemaphoreType.DMA((LEVELS, SLOTS, 6)),
        pltpu.SemaphoreType.DMA((LEVELS, SLOTS, 6)),
        pltpu.VMEM((1, lanes), jnp.float32),
        pltpu.VMEM((nz, 1, lanes), jnp.float32),
        pltpu.VMEM((nz, lanes), jnp.float32),
        pltpu.SemaphoreType.DMA((2, top)),
        pltpu.SemaphoreType.DMA((2, top)),
    ]
    outs = pl.pallas_call(
        functools.partial(down_kernel, cfg),
        out_shape=tuple(out_shapes),
        in_specs=[vmem] * 3,
        out_specs=tuple([vmem] * len(out_shapes)),
        scratch_shapes=scratch,
        compiler_params=pltpu.CompilerParams(collective_id=32, has_side_effects=True),
    )(right_side, beta_coef, alpha_coef)
    iterates = list(outs[0:LEVELS])
    rhs_levels = [right_side] + list(outs[LEVELS : 2 * LEVELS])
    betas = [beta_coef] + list(outs[2 * LEVELS : 3 * LEVELS])
    alphas = [alpha_coef] + list(outs[3 * LEVELS : 4 * LEVELS])
    whole = outs[4 * LEVELS][..., :width].reshape((nx, ny, nz, 3) + shapes[LEVELS])
    whole = whole.transpose(3, 0, 4, 1, 5, 2, 6)
    whole = whole.reshape((3,) + tuple(n * s for n, s in zip(sizes, shapes[LEVELS])))
    return iterates, rhs_levels, betas, alphas, whole


def gather_peers(sizes):
    index = [lax.axis_index(axis) for axis in AXES]
    nx, ny, nz = sizes
    ix, iy, iz = index
    line = [(ix, iy, lax.rem(iz + step, nz)) for step in range(1, nz)]
    plane = []
    for dx in range(nx):
        for dy in range(ny):
            if dx or dy:
                plane.append(((dx, dy), (lax.rem(ix + dx, nx), lax.rem(iy + dy, ny), iz)))

    return line, plane


def gather_stages(sizes, line, plane, row_ref, out_ref, first, dense, send_sem, recv_sem):
    index = [lax.axis_index(axis) for axis in AXES]
    nx, ny, nz = sizes
    ix, iy, iz = index
    waits = []
    for step in range(1, nz):
        copy = pltpu.make_async_remote_copy(
            src_ref=row_ref,
            dst_ref=first.at[iz],
            send_sem=send_sem.at[0, step],
            recv_sem=recv_sem.at[0, iz],
            device_id=line[step - 1],
            device_id_type=MESH,
        )
        copy.start()
        origin = lax.rem(iz + nz - step, nz)
        incoming = pltpu.make_async_remote_copy(
            src_ref=row_ref,
            dst_ref=first.at[origin],
            send_sem=send_sem.at[0, step],
            recv_sem=recv_sem.at[0, origin],
            device_id=line[step - 1],
            device_id_type=MESH,
        )
        waits.append((copy, incoming))
    first[iz] = row_ref[...]
    for copy, incoming in waits:
        copy.wait_send()
        incoming.wait_recv()
    for z in range(nz):
        dense[z : z + 1, :] = first[z]

    mine = ix * ny + iy
    waits = []
    for n, ((dx, dy), peer) in enumerate(plane):
        copy = pltpu.make_async_remote_copy(
            src_ref=dense,
            dst_ref=out_ref.at[ix, iy],
            send_sem=send_sem.at[1, n],
            recv_sem=recv_sem.at[1, mine],
            device_id=peer,
            device_id_type=MESH,
        )
        copy.start()
        ox = lax.rem(ix + nx - dx, nx)
        oy = lax.rem(iy + ny - dy, ny)
        incoming = pltpu.make_async_remote_copy(
            src_ref=dense,
            dst_ref=out_ref.at[ox, oy],
            send_sem=send_sem.at[1, n],
            recv_sem=recv_sem.at[1, ox * ny + oy],
            device_id=peer,
            device_id_type=MESH,
        )
        waits.append((copy, incoming))
    out_ref[ix, iy] = dense[...]
    for copy, incoming in waits:
        copy.wait_send()
        incoming.wait_recv()


def gather_kernel(sizes, row_ref, out_ref, first, dense, send_sem, recv_sem):
    line, plane = gather_peers(sizes)
    barrier = pltpu.get_barrier_semaphore()
    for peer in line + [peer for _, peer in plane]:
        pl.semaphore_signal(barrier, inc=1, device_id=peer, device_id_type=MESH)
    pl.semaphore_wait(barrier, len(line) + len(plane))
    gather_stages(sizes, line, plane, row_ref, out_ref, first, dense, send_sem, recv_sem)


def gather_bottom(packed):
    sizes = tuple(lax.axis_size(axis) for axis in AXES)
    nx, ny, nz = sizes
    width = packed.size
    lanes = -(-width // 128) * 128
    row = jnp.pad(packed.reshape(1, width), ((0, 0), (0, lanes - width)))
    vmem = pl.BlockSpec(memory_space=pltpu.VMEM)
    top = max(nz, nx * ny)
    whole = pl.pallas_call(
        functools.partial(gather_kernel, sizes),
        out_shape=jax.ShapeDtypeStruct((nx, ny, nz, lanes), jnp.float32),
        in_specs=[vmem],
        out_specs=vmem,
        scratch_shapes=[
            pltpu.VMEM((nz, 1, lanes), jnp.float32),
            pltpu.VMEM((nz, lanes), jnp.float32),
            pltpu.SemaphoreType.DMA((2, top)),
            pltpu.SemaphoreType.DMA((2, top)),
        ],
        compiler_params=pltpu.CompilerParams(collective_id=64, has_side_effects=True),
    )(row)
    whole = whole[..., :width].reshape((nx, ny, nz) + packed.shape)
    whole = whole.transpose(3, 0, 4, 1, 5, 2, 6)
    return whole.reshape(
        (packed.shape[0],) + tuple(n * s for n, s in zip(sizes, packed.shape[1:]))
    )


def split_padded(padded):
    return (
        padded[:-2, 1:-1, 1:-1],
        padded[2:, 1:-1, 1:-1],
        padded[1:-1, :-2, 1:-1],
        padded[1:-1, 2:, 1:-1],
        padded[1:-1, 1:-1, :-2],
        padded[1:-1, 1:-1, 2:],
    )


def zero_pad(field):
    return split_padded(jnp.pad(field, 1))


def level_operator(beta_level, alpha_level, beta_sides, shift):
    coeffs = tuple((0.5 * (beta_level + other) for other in beta_sides))
    diagonal = shift * alpha_level
    for coeff in coeffs:
        diagonal = diagonal + coeff
    return (coeffs, diagonal)


def apply_operator(field, operator, pad_field):
    coeffs, diagonal = operator
    others = pad_field(field)
    total = coeffs[0] * others[0]
    for index in range(1, 6):
        total = total + coeffs[index] * others[index]
    return diagonal * field - total


def chebyshev(iterate, rhs_level, operator, count, lower, zero_start, pad_field):
    diagonal = operator[1]
    center = (UPPER_EIG + lower) / 2.0
    half_width = (UPPER_EIG - lower) / 2.0
    sigma_ratio = center / half_width
    rho_old = 1.0 / sigma_ratio
    if zero_start:
        remain = rhs_level
    else:
        remain = rhs_level - apply_operator(iterate, operator, pad_field)
    update = remain / diagonal / center
    iterate = iterate + update
    for sweep_index in range(count - 1):
        remain = rhs_level - apply_operator(iterate, operator, pad_field)
        rho_new = 1.0 / (2.0 * sigma_ratio - rho_old)
        update = rho_new * rho_old * update + 2.0 * rho_new / half_width * (remain / diagonal)
        iterate = iterate + update
        rho_old = rho_new
    return iterate


def restrict_mean(field):
    first, second, third = field.shape
    blocks = field.reshape(first // 2, 2, second // 2, 2, third // 2, 2)
    return jnp.sum(blocks, axis=(1, 3, 5)) * 0.125


def prolong_copy(field):
    return jnp.repeat(jnp.repeat(jnp.repeat(field, 2, axis=0), 2, axis=1), 2, axis=2)


def shards(right_side, alpha_coef, beta_coef):
    smoothed, rhs_levels, betas, alphas, packed = down_chain(right_side, beta_coef, alpha_coef)
    local_shape = rhs_levels[LEVELS].shape
    index_x = lax.axis_index("gx")
    index_y = lax.axis_index("gy")
    index_z = lax.axis_index("gz")
    whole_rhs = packed[0]
    whole_beta = packed[1]
    whole_alpha = packed[2]
    bottom_operator = level_operator(
        whole_beta, whole_alpha, zero_pad(whole_beta), SHIFT_BASE * 4.0**LEVELS
    )
    whole_correction = chebyshev(
        jnp.zeros_like(whole_rhs), whole_rhs, bottom_operator, BOTTOM, BOTTOM_LOWER, True, zero_pad
    )
    starts = (index_x * local_shape[0], index_y * local_shape[1], index_z * local_shape[2])
    correction = lax.dynamic_slice(whole_correction, starts, local_shape)
    correction, residual_field = up_chain(correction, smoothed, rhs_levels, betas, alphas)
    return (correction, residual_field)


def solution(mesh):
    in_specs = (P("gx", "gy", "gz"), P("gx", "gy", "gz"), P("gx", "gy", "gz"))
    out_specs = (P("gx", "gy", "gz"), P("gx", "gy", "gz"))
    return jax.shard_map(shards, mesh=mesh, in_specs=in_specs, out_specs=out_specs, check_vma=False)
```

```python
import functools

import jax
import jax.numpy as jnp
from jax import lax
from jax.experimental import pallas as pl
from jax.experimental.pallas import tpu as pltpu
from jax.sharding import PartitionSpec as P

MESH = pl.DeviceIdType.MESH
AXES = ("gx", "gy", "gz")
SLOTS = 3

LEVELS = 3
SWEEPS = 4
BOTTOM = 12


SHIFT_BASE = 0.01
UPPER_EIG = 2.0
SMOOTH_LOWER = 0.25
BOTTOM_LOWER = 0.02


def level_kernel(cfg, *refs):
    sizes, shift, count, lower, zero_start, residual, restrict = cfg
    n_in = 3 if zero_start else 4
    b_ref, beta_ref, alpha_ref = refs[0:3]
    v0_ref = None if zero_start else refs[3]
    n_out = 1 + (1 if residual and not restrict else 0) + (3 if restrict else 0)
    outs = refs[n_in : n_in + n_out]
    fld, xh, yh, zh, zsend, coef, dbuf, send_sem, recv_sem = refs[n_in + len(outs) :]
    A, B, C = b_ref.shape
    index = [lax.axis_index(axis) for axis in AXES]
    targets = []
    for k in range(6):
        axis = k // 2
        if k % 2 == 0:
            exists = index[axis] > 0
            other = index[axis] - 1
        else:
            exists = index[axis] < sizes[axis] - 1
            other = index[axis] + 1
        device = tuple(other if a == axis else index[a] for a in range(3))
        targets.append((exists, device))

    def halo(h, slot):
        if h < 2:
            return xh.at[h, slot]
        return yh.at[h - 2, slot] if h < 4 else zh.at[h - 4, slot]

    picks = lax.broadcasted_iota(jnp.int32, (8, C), 0)
    lanes = lax.broadcasted_iota(jnp.int32, (8, C), 1)
    selector = jnp.where(
        (picks == 0) & (lanes == 0), 1.0, jnp.where((picks == 1) & (lanes == C - 1), 1.0, 0.0)
    ).astype(jnp.float32)

    barrier = pltpu.get_barrier_semaphore()
    total = jnp.int32(0)
    for exists, device in targets:

        @pl.when(exists)
        def _():
            pl.semaphore_signal(barrier, inc=1, device_id=device, device_id_type=MESH)

        total = total + exists.astype(jnp.int32)
    for h, (exists, device) in enumerate(targets):

        @pl.when(jnp.logical_not(exists))
        def _():
            for slot in range(SLOTS):
                buf = halo(h, slot)
                buf[...] = jnp.zeros(buf.shape, buf.dtype)

    if restrict:
        coarse_rows = (
            lax.broadcasted_iota(jnp.int32, (B // 2, B), 1) // 2
            == lax.broadcasted_iota(jnp.int32, (B // 2, B), 0)
        ).astype(jnp.float32)
        coarse_cols = (
            lax.broadcasted_iota(jnp.int32, (C, C // 2), 0) // 2
            == lax.broadcasted_iota(jnp.int32, (C, C // 2), 1)
        ).astype(jnp.float32)

        def restrict_into(src, dst, scale):
            for i in range(A // 2):
                pair = src[2 * i] + src[2 * i + 1]
                half = jnp.dot(
                    coarse_rows, pair, precision=lax.Precision.HIGHEST,
                    preferred_element_type=jnp.float32,
                )
                dst[i] = scale * jnp.dot(
                    half, coarse_cols, precision=lax.Precision.HIGHEST,
                    preferred_element_type=jnp.float32,
                )

        restrict_into(beta_ref, outs[2], 0.125)
        restrict_into(alpha_ref, outs[3], 0.125)
    pl.semaphore_wait(barrier, total)

    def exchange_start(src, slot):
        block = src[...].reshape(A * B, C)
        zsend[slot] = lax.dot_general(
            selector, block, (((1,), (1,)), ((), ())),
            precision=lax.Precision.HIGHEST, preferred_element_type=jnp.float32,
        )
        sources = (
            src.at[0], src.at[A - 1],
            src.at[:, 0:8, :], src.at[:, B - 8 : B, :],
            zsend.at[slot], zsend.at[slot],
        )
        waits = []
        for k, (exists, device) in enumerate(targets):
            copy = pltpu.make_async_remote_copy(
                src_ref=sources[k],
                dst_ref=halo(k ^ 1, slot),
                send_sem=send_sem.at[slot, k],
                recv_sem=recv_sem.at[slot, k ^ 1],
                device_id=device,
                device_id_type=MESH,
            )
            pl.when(exists)(copy.start)
            incoming = pltpu.make_async_remote_copy(
                src_ref=sources[k ^ 1],
                dst_ref=halo(k, slot),
                send_sem=send_sem.at[slot, k ^ 1],
                recv_sem=recv_sem.at[slot, k],
                device_id=device,
                device_id_type=MESH,
            )
            waits.append((exists, copy.wait_send))
            waits.append((exists, incoming.wait_recv))
        return waits

    def exchange_finish(waits):
        for exists, wait in waits:
            pl.when(exists)(wait)

    def exchange(src, slot):
        exchange_finish(exchange_start(src, slot))

    rows = lax.broadcasted_iota(jnp.int32, (B, C), 0)
    cols = lax.broadcasted_iota(jnp.int32, (B, C), 1)

    def z_columns(slot):
        return (jnp.transpose(zh[0, slot]), jnp.transpose(zh[1, slot]))

    def sides(src, i, slot, columns):
        here = src[i]
        lower_x = src[i - 1] if i > 0 else xh[0, slot]
        upper_x = src[i + 1] if i < A - 1 else xh[1, slot]
        lower_y = jnp.where(rows == 0, yh[0, slot, i, 7:8, :], pltpu.roll(here, 1, 0))
        upper_y = jnp.where(rows == B - 1, yh[1, slot, i, 0:1, :], pltpu.roll(here, B - 1, 0))
        lower_z = jnp.where(cols == 0, columns[0][i * B : (i + 1) * B, 1:2], pltpu.roll(here, 1, 1))
        upper_z = jnp.where(
            cols == C - 1, columns[1][i * B : (i + 1) * B, 0:1], pltpu.roll(here, C - 1, 1)
        )
        return here, (lower_x, upper_x, lower_y, upper_y, lower_z, upper_z)

    exchanges = [0]

    def next_slot():
        slot = exchanges[0] % SLOTS
        exchanges[0] += 1
        return slot

    slot = next_slot()
    if zero_start:
        exchange(beta_ref, slot)
    else:
        first_slot = next_slot()
        first_waits = exchange_start(v0_ref, first_slot)
        exchange(beta_ref, slot)
    columns = z_columns(slot)
    for i in range(A):
        here, others = sides(beta_ref, i, slot, columns)
        diagonal = shift * alpha_ref[i]
        for k in range(6):
            face = 0.5 * (here + others[k])
            coef[k, i] = face
            diagonal = diagonal + face
        coef[6, i] = diagonal

    def apply_rows(src, slot, i, columns):
        here, others = sides(src, i, slot, columns)
        acc = coef[0, i] * others[0]
        for k in range(1, 6):
            acc = acc + coef[k, i] * others[k]
        return b_ref[i] - (coef[6, i] * here - acc)

    center = (UPPER_EIG + lower) / 2.0
    half_width = (UPPER_EIG - lower) / 2.0
    sigma_ratio = center / half_width
    rho_old = 1.0 / sigma_ratio
    current = 0
    if zero_start:
        for i in range(A):
            update = b_ref[i] / coef[6, i] / center
            dbuf[i] = update
            fld[current, i] = update
    else:
        exchange_finish(first_waits)
        columns = z_columns(first_slot)
        for i in range(A):
            remain = apply_rows(v0_ref, first_slot, i, columns)
            update = remain / coef[6, i] / center
            dbuf[i] = update
            fld[current, i] = v0_ref[i] + update
    for sweep in range(count - 1):
        rho_new = 1.0 / (2.0 * sigma_ratio - rho_old)
        slot = next_slot()
        src = fld.at[current]
        exchange(src, slot)
        last = sweep == count - 2
        dst = outs[0] if last else fld.at[1 - current]
        columns = z_columns(slot)
        for i in range(A):
            remain = apply_rows(src, slot, i, columns)
            update = (rho_new * rho_old) * dbuf[i] + (2.0 * rho_new / half_width) * (
                remain / coef[6, i]
            )
            dbuf[i] = update
            dst[i] = src[i] + update
        rho_old = rho_new
        current = 1 - current
    if residual:
        slot = next_slot()
        exchange(outs[0], slot)
        remain_ref = dbuf if restrict else outs[1]
        columns = z_columns(slot)
        for i in range(A):
            remain_ref[i] = apply_rows(outs[0], slot, i, columns)
        if restrict:
            restrict_into(dbuf, outs[1], 0.5)


KERNELS = {}


def smooth(level_args, shift, count, lower, zero_start, residual, restrict=False):
    A, B, C = level_args[0].shape
    sizes = tuple(lax.axis_size(axis) for axis in AXES)
    cfg = (sizes, shift, count, lower, zero_start, residual, restrict)
    ident = KERNELS.setdefault((A, B, C) + cfg[1:], len(KERNELS))
    vmem = pl.BlockSpec(memory_space=pltpu.VMEM)
    block = jax.ShapeDtypeStruct((A, B, C), jnp.float32)
    coarse = jax.ShapeDtypeStruct((A // 2, B // 2, C // 2), jnp.float32)
    shapes = [block] + ([block] if residual and not restrict else []) + ([coarse] * 3 if restrict else [])
    n_out = len(shapes)
    return pl.pallas_call(
        functools.partial(level_kernel, cfg),
        out_shape=tuple(shapes),
        in_specs=[vmem] * len(level_args),
        out_specs=tuple([vmem] * n_out),
        scratch_shapes=[
            pltpu.VMEM((2, A, B, C), jnp.float32),
            pltpu.VMEM((2, SLOTS, B, C), jnp.float32),
            pltpu.VMEM((2, SLOTS, A, 8, C), jnp.float32),
            pltpu.VMEM((2, SLOTS, 8, A * B), jnp.float32),
            pltpu.VMEM((SLOTS, 8, A * B), jnp.float32),
            pltpu.VMEM((7, A, B, C), jnp.float32),
            pltpu.VMEM((A, B, C), jnp.float32),
            pltpu.SemaphoreType.DMA((SLOTS, 6)),
            pltpu.SemaphoreType.DMA((SLOTS, 6)),
        ],
        compiler_params=pltpu.CompilerParams(collective_id=ident, has_side_effects=True),
    )(*level_args)


def restrict_into(src, dst, scale):
    A, B, C = src.shape
    coarse_rows = (
        lax.broadcasted_iota(jnp.int32, (B // 2, B), 1) // 2
        == lax.broadcasted_iota(jnp.int32, (B // 2, B), 0)
    ).astype(jnp.float32)
    coarse_cols = (
        lax.broadcasted_iota(jnp.int32, (C, C // 2), 0) // 2
        == lax.broadcasted_iota(jnp.int32, (C, C // 2), 1)
    ).astype(jnp.float32)
    for i in range(A // 2):
        pair = src[2 * i] + src[2 * i + 1]
        half = jnp.dot(
            coarse_rows, pair, precision=lax.Precision.HIGHEST, preferred_element_type=jnp.float32
        )
        dst[i] = scale * jnp.dot(
            half, coarse_cols, precision=lax.Precision.HIGHEST, preferred_element_type=jnp.float32
        )


def neighbour_targets(sizes):
    index = [lax.axis_index(axis) for axis in AXES]
    targets = []
    for k in range(6):
        axis = k // 2
        if k % 2 == 0:
            exists = index[axis] > 0
            other = index[axis] - 1
        else:
            exists = index[axis] < sizes[axis] - 1
            other = index[axis] + 1
        device = tuple(other if a == axis else index[a] for a in range(3))
        targets.append((exists, device))
    return targets


def level_tools(shape, level, targets, bufs, send_sem, recv_sem):
    A, B, C = shape
    fld, xh, yh, zh, zsend, coef, dbuf = bufs

    def halo(h, slot):
        if h < 2:
            return xh.at[h, slot]
        return yh.at[h - 2, slot] if h < 4 else zh.at[h - 4, slot]

    picks = lax.broadcasted_iota(jnp.int32, (8, C), 0)
    lanes = lax.broadcasted_iota(jnp.int32, (8, C), 1)
    selector = jnp.where(
        (picks == 0) & (lanes == 0), 1.0, jnp.where((picks == 1) & (lanes == C - 1), 1.0, 0.0)
    ).astype(jnp.float32)
    rows = lax.broadcasted_iota(jnp.int32, (B, C), 0)
    cols = lax.broadcasted_iota(jnp.int32, (B, C), 1)

    def zero_halos():
        for h, (exists, device) in enumerate(targets):

            @pl.when(jnp.logical_not(exists))
            def _():
                for slot in range(SLOTS):
                    buf = halo(h, slot)
                    buf[...] = jnp.zeros(buf.shape, buf.dtype)

    def exchange_start(src, slot):
        block = src[...].reshape(A * B, C)
        zsend[slot] = lax.dot_general(
            selector, block, (((1,), (1,)), ((), ())),
            precision=lax.Precision.HIGHEST, preferred_element_type=jnp.float32,
        )
        sources = (
            src.at[0], src.at[A - 1],
            src.at[:, 0:8, :], src.at[:, B - 8 : B, :],
            zsend.at[slot], zsend.at[slot],
        )
        waits = []
        for k, (exists, device) in enumerate(targets):
            copy = pltpu.make_async_remote_copy(
                src_ref=sources[k],
                dst_ref=halo(k ^ 1, slot),
                send_sem=send_sem.at[level, slot, k],
                recv_sem=recv_sem.at[level, slot, k ^ 1],
                device_id=device,
                device_id_type=MESH,
            )
            pl.when(exists)(copy.start)
            incoming = pltpu.make_async_remote_copy(
                src_ref=sources[k ^ 1],
                dst_ref=halo(k, slot),
                send_sem=send_sem.at[level, slot, k ^ 1],
                recv_sem=recv_sem.at[level, slot, k],
                device_id=device,
                device_id_type=MESH,
            )
            waits.append((exists, copy.wait_send))
            waits.append((exists, incoming.wait_recv))
        return waits

    def exchange_finish(waits):
        for exists, wait in waits:
            pl.when(exists)(wait)

    def exchange(src, slot):
        exchange_finish(exchange_start(src, slot))

    def z_columns(slot):
        return (jnp.transpose(zh[0, slot]), jnp.transpose(zh[1, slot]))

    def sides(src, i, slot, columns):
        here = src[i]
        lower_x = src[i - 1] if i > 0 else xh[0, slot]
        upper_x = src[i + 1] if i < A - 1 else xh[1, slot]
        lower_y = jnp.where(rows == 0, yh[0, slot, i, 7:8, :], pltpu.roll(here, 1, 0))
        upper_y = jnp.where(rows == B - 1, yh[1, slot, i, 0:1, :], pltpu.roll(here, B - 1, 0))
        lower_z = jnp.where(cols == 0, columns[0][i * B : (i + 1) * B, 1:2], pltpu.roll(here, 1, 1))
        upper_z = jnp.where(
            cols == C - 1, columns[1][i * B : (i + 1) * B, 0:1], pltpu.roll(here, C - 1, 1)
        )
        return here, (lower_x, upper_x, lower_y, upper_y, lower_z, upper_z)

    def build_coef(beta_ref, alpha_ref, slot, shift):
        columns = z_columns(slot)
        for i in range(A):
            here, others = sides(beta_ref, i, slot, columns)
            diagonal = shift * alpha_ref[i]
            for k in range(6):
                face = 0.5 * (here + others[k])
                coef[k, i] = face
                diagonal = diagonal + face
            coef[6, i] = diagonal

    def apply_op(src, slot, i, columns):
        here, others = sides(src, i, slot, columns)
        acc = coef[0, i] * others[0]
        for k in range(1, 6):
            acc = acc + coef[k, i] * others[k]
        return coef[6, i] * here - acc

    def apply_rows(src, b_ref, slot, i, columns):
        return b_ref[i] - apply_op(src, slot, i, columns)

    def smooth_down(b_ref, v_out, next_rhs, count, lower):
        center = (UPPER_EIG + lower) / 2.0
        half_width = (UPPER_EIG - lower) / 2.0
        sigma_ratio = center / half_width
        rho_old = 1.0 / sigma_ratio
        current = 0
        for i in range(A):
            update = b_ref[i] / coef[6, i] / center
            dbuf[i] = update
            fld[current, i] = update
        slot = 0
        for sweep in range(count - 1):
            rho_new = 1.0 / (2.0 * sigma_ratio - rho_old)
            slot = (slot + 1) % SLOTS
            src = fld.at[current]
            exchange(src, slot)
            columns = z_columns(slot)
            dst = v_out if sweep == count - 2 else fld.at[1 - current]
            for i in range(A):
                remain = apply_rows(src, b_ref, slot, i, columns)
                update = (rho_new * rho_old) * dbuf[i] + (2.0 * rho_new / half_width) * (
                    remain / coef[6, i]
                )
                dbuf[i] = update
                dst[i] = src[i] + update
            rho_old = rho_new
            current = 1 - current
        slot = (slot + 1) % SLOTS
        exchange(v_out, slot)
        columns = z_columns(slot)
        for i in range(A):
            dbuf[i] = apply_rows(v_out, b_ref, slot, i, columns)
        restrict_into(dbuf, next_rhs, 0.5)

    def smooth_up(b_ref, v_out, count, lower, first_slot, first_waits, residual_out, split):
        start = fld.at[1]
        if first_waits is None:
            exchange(start, first_slot)
        else:
            exchange_finish(first_waits)
        center = (UPPER_EIG + lower) / 2.0
        half_width = (UPPER_EIG - lower) / 2.0
        sigma_ratio = center / half_width
        rho_old = 1.0 / sigma_ratio
        columns = z_columns(first_slot)
        for i in range(A):
            remain = apply_rows(start, b_ref, first_slot, i, columns)
            update = remain / coef[6, i] / center
            dbuf[i] = update
            fld[0, i] = start[i] + update
        current = 0
        slot = first_slot
        for sweep in range(count - 1):
            rho_new = 1.0 / (2.0 * sigma_ratio - rho_old)
            slot = (slot + 1) % SLOTS
            src = fld.at[current]
            exchange(src, slot)
            columns = z_columns(slot)
            dst = v_out if sweep == count - 2 else fld.at[1 - current]
            for i in range(A):
                remain = apply_rows(src, b_ref, slot, i, columns)
                update = (rho_new * rho_old) * dbuf[i] + (2.0 * rho_new / half_width) * (
                    remain / coef[6, i]
                )
                dbuf[i] = update
                dst[i] = src[i] + update
                if split is not None and sweep == count - 2:
                    split[0][i] = src[i]
                    split[1][i] = update
            rho_old = rho_new
            current = 1 - current
        if residual_out is not None:
            slot = (slot + 1) % SLOTS
            exchange(v_out, slot)
            columns = z_columns(slot)
            for i in range(A):
                residual_out[i] = apply_op(v_out, slot, i, columns)

    def prolong_start(coarse, smoothed):
        fine_rows = (
            lax.broadcasted_iota(jnp.int32, (B, B // 2), 0) // 2
            == lax.broadcasted_iota(jnp.int32, (B, B // 2), 1)
        ).astype(jnp.float32)
        fine_cols = (
            lax.broadcasted_iota(jnp.int32, (C // 2, C), 1) // 2
            == lax.broadcasted_iota(jnp.int32, (C // 2, C), 0)
        ).astype(jnp.float32)
        for i in range(A):
            half = jnp.dot(
                fine_rows, coarse[i // 2], precision=lax.Precision.HIGHEST,
                preferred_element_type=jnp.float32,
            )
            fine = jnp.dot(
                half, fine_cols, precision=lax.Precision.HIGHEST,
                preferred_element_type=jnp.float32,
            )
            fld[1, i] = smoothed[i] + fine

    return (
        zero_halos, exchange_start, exchange_finish, build_coef, smooth_down, smooth_up,
        prolong_start, fld,
    )


def up_kernel(cfg, *refs):
    sizes, shapes, shifts = cfg
    depth = len(shapes)
    coarsest = refs[0]
    level_in = [refs[1 + 4 * l : 5 + 4 * l] for l in range(depth)]
    previous_out, update_out, operator_out = refs[1 + 4 * depth : 4 + 4 * depth]
    scratch = refs[4 + 4 * depth :]
    results = scratch[7 * depth : 8 * depth]
    send_sem, recv_sem = scratch[8 * depth], scratch[8 * depth + 1]
    targets = neighbour_targets(sizes)
    barrier = pltpu.get_barrier_semaphore()
    total = jnp.int32(0)
    for exists, device in targets:

        @pl.when(exists)
        def _():
            pl.semaphore_signal(barrier, inc=1, device_id=device, device_id_type=MESH)

        total = total + exists.astype(jnp.int32)
    tools = [
        level_tools(shapes[l], l, targets, scratch[7 * l : 7 * l + 7], send_sem, recv_sem)
        for l in range(depth)
    ]
    for tool in tools:
        tool[0]()
    top = depth - 1
    tools[top][6](coarsest, level_in[top][0])
    pl.semaphore_wait(barrier, total)
    first_waits = tools[top][1](tools[top][7].at[1], 1)
    waits = [tools[l][1](level_in[l][2], 0) for l in range(depth)]
    for l in range(depth):
        tools[l][2](waits[l])
        tools[l][3](level_in[l][2], level_in[l][3], 0, shifts[l])
    coarse = None
    for l in range(top, -1, -1):
        if l < top:
            tools[l][6](coarse, level_in[l][0])
        v_out = results[l]
        tools[l][5](
            level_in[l][1], v_out, SWEEPS, SMOOTH_LOWER, 1,
            first_waits if l == top else None, operator_out if l == 0 else None,
            (previous_out, update_out) if l == 0 else None,
        )
        coarse = v_out


def up_chain(coarsest, smoothed, rhs_levels, betas, alphas):
    sizes = tuple(lax.axis_size(axis) for axis in AXES)
    shapes = [tuple(x.shape) for x in smoothed]
    shifts = tuple(SHIFT_BASE * 4.0**l for l in range(LEVELS))
    cfg = (sizes, tuple(shapes), shifts)
    vmem = pl.BlockSpec(memory_space=pltpu.VMEM)
    args = [coarsest]
    for l in range(LEVELS):
        args += [smoothed[l], rhs_levels[l], betas[l], alphas[l]]
    scratch = []
    for s in shapes:
        scratch += level_scratch(s)
    scratch += [pltpu.VMEM(s, jnp.float32) for s in shapes]
    scratch += [
        pltpu.SemaphoreType.DMA((LEVELS, SLOTS, 6)),
        pltpu.SemaphoreType.DMA((LEVELS, SLOTS, 6)),
    ]
    fine = jax.ShapeDtypeStruct(shapes[0], jnp.float32)
    previous, update, operator = pl.pallas_call(
        functools.partial(up_kernel, cfg),
        out_shape=(fine, fine, fine),
        in_specs=[vmem] * len(args),
        out_specs=(vmem, vmem, vmem),
        scratch_shapes=scratch,
        compiler_params=pltpu.CompilerParams(collective_id=48, has_side_effects=True),
    )(*args)
    return previous + update, rhs_levels[0] - operator


def level_scratch(shape):
    A, B, C = shape
    return [
        pltpu.VMEM((2, A, B, C), jnp.float32),
        pltpu.VMEM((2, SLOTS, B, C), jnp.float32),
        pltpu.VMEM((2, SLOTS, A, 8, C), jnp.float32),
        pltpu.VMEM((2, SLOTS, 8, A * B), jnp.float32),
        pltpu.VMEM((SLOTS, 8, A * B), jnp.float32),
        pltpu.VMEM((7, A, B, C), jnp.float32),
        pltpu.VMEM((A, B, C), jnp.float32),
    ]


def down_kernel(cfg, *refs):
    sizes, shapes, shifts = cfg
    depth = len(shapes)
    b0, beta0, alpha0 = refs[0:3]
    outs = refs[3 : 3 + 4 * depth]
    iterates = outs[0:depth]
    rhs = [b0] + list(outs[depth : 2 * depth])
    betas = [beta0] + list(outs[2 * depth : 3 * depth])
    alphas = [alpha0] + list(outs[3 * depth : 4 * depth])
    gathered = refs[3 + 4 * depth]
    scratch = refs[4 + 4 * depth :]
    send_sem, recv_sem = scratch[7 * depth], scratch[7 * depth + 1]
    row, first, dense, gsend, grecv = scratch[7 * depth + 2 :]
    targets = neighbour_targets(sizes)
    line, plane = gather_peers(sizes)
    barrier = pltpu.get_barrier_semaphore()
    for peer in line + [peer for _, peer in plane]:
        pl.semaphore_signal(barrier, inc=1, device_id=peer, device_id_type=MESH)
    total = len(line) + len(plane)
    tools = [
        level_tools(shapes[l], l, targets, scratch[7 * l : 7 * l + 7], send_sem, recv_sem)
        for l in range(depth)
    ]
    for tool in tools:
        tool[0]()
    for l in range(depth):
        restrict_into(betas[l], betas[l + 1], 0.125)
        restrict_into(alphas[l], alphas[l + 1], 0.125)
    pl.semaphore_wait(barrier, total)
    waits = [tools[l][1](betas[l], 0) for l in range(depth)]
    for l in range(depth):
        tools[l][2](waits[l])
        tools[l][3](betas[l], alphas[l], 0, shifts[l])
    for l in range(depth):
        tools[l][4](rhs[l], iterates[l], rhs[l + 1], SWEEPS, SMOOTH_LOWER)
    lanes = row.shape[1]
    packed = jnp.zeros((1, lanes), jnp.float32)
    offset = 0
    for part in (rhs[depth], betas[depth], alphas[depth]):
        pa, pb, pc = part.shape
        for x in range(pa):
            for j in range(pb):
                pick = (lax.broadcasted_iota(jnp.int32, (1, pb), 1) == j).astype(jnp.float32)
                line_values = jnp.dot(
                    pick, part[x], precision=lax.Precision.HIGHEST,
                    preferred_element_type=jnp.float32,
                )
                place = (
                    lax.broadcasted_iota(jnp.int32, (pc, lanes), 0) + offset
                    == lax.broadcasted_iota(jnp.int32, (pc, lanes), 1)
                ).astype(jnp.float32)
                packed = packed + jnp.dot(
                    line_values, place, precision=lax.Precision.HIGHEST,
                    preferred_element_type=jnp.float32,
                )
                offset += pc
    row[...] = packed
    gather_stages(sizes, line, plane, row, gathered, first, dense, gsend, grecv)


def down_chain(right_side, beta_coef, alpha_coef):
    sizes = tuple(lax.axis_size(axis) for axis in AXES)
    shapes = [tuple(n >> l for n in right_side.shape) for l in range(LEVELS + 1)]
    shifts = tuple(SHIFT_BASE * 4.0**l for l in range(LEVELS))
    cfg = (sizes, tuple(shapes[:LEVELS]), shifts)
    vmem = pl.BlockSpec(memory_space=pltpu.VMEM)
    out_shapes = [jax.ShapeDtypeStruct(s, jnp.float32) for s in shapes[:LEVELS]]
    out_shapes += [jax.ShapeDtypeStruct(s, jnp.float32) for s in shapes[1:]] * 3
    scratch = []
    for s in shapes[:LEVELS]:
        scratch += level_scratch(s)
    nx, ny, nz = sizes
    width = 3 * shapes[LEVELS][0] * shapes[LEVELS][1] * shapes[LEVELS][2]
    lanes = -(-width // 128) * 128
    top = max(nz, nx * ny)
    out_shapes.append(jax.ShapeDtypeStruct((nx, ny, nz, lanes), jnp.float32))
    scratch += [
        pltpu.SemaphoreType.DMA((LEVELS, SLOTS, 6)),
        pltpu.SemaphoreType.DMA((LEVELS, SLOTS, 6)),
        pltpu.VMEM((1, lanes), jnp.float32),
        pltpu.VMEM((nz, 1, lanes), jnp.float32),
        pltpu.VMEM((nz, lanes), jnp.float32),
        pltpu.SemaphoreType.DMA((2, top)),
        pltpu.SemaphoreType.DMA((2, top)),
    ]
    outs = pl.pallas_call(
        functools.partial(down_kernel, cfg),
        out_shape=tuple(out_shapes),
        in_specs=[vmem] * 3,
        out_specs=tuple([vmem] * len(out_shapes)),
        scratch_shapes=scratch,
        compiler_params=pltpu.CompilerParams(collective_id=32, has_side_effects=True),
    )(right_side, beta_coef, alpha_coef)
    iterates = list(outs[0:LEVELS])
    rhs_levels = [right_side] + list(outs[LEVELS : 2 * LEVELS])
    betas = [beta_coef] + list(outs[2 * LEVELS : 3 * LEVELS])
    alphas = [alpha_coef] + list(outs[3 * LEVELS : 4 * LEVELS])
    whole = outs[4 * LEVELS][..., :width].reshape((nx, ny, nz, 3) + shapes[LEVELS])
    whole = whole.transpose(3, 0, 4, 1, 5, 2, 6)
    whole = whole.reshape((3,) + tuple(n * s for n, s in zip(sizes, shapes[LEVELS])))
    return iterates, rhs_levels, betas, alphas, whole


def gather_peers(sizes):
    index = [lax.axis_index(axis) for axis in AXES]
    nx, ny, nz = sizes
    ix, iy, iz = index
    line = [(ix, iy, lax.rem(iz + step, nz)) for step in range(1, nz)]
    plane = []
    for dx in range(nx):
        for dy in range(ny):
            if dx or dy:
                plane.append(((dx, dy), (lax.rem(ix + dx, nx), lax.rem(iy + dy, ny), iz)))

    return line, plane


def gather_stages(sizes, line, plane, row_ref, out_ref, first, dense, send_sem, recv_sem):
    index = [lax.axis_index(axis) for axis in AXES]
    nx, ny, nz = sizes
    ix, iy, iz = index
    waits = []
    for step in range(1, nz):
        copy = pltpu.make_async_remote_copy(
            src_ref=row_ref,
            dst_ref=first.at[iz],
            send_sem=send_sem.at[0, step],
            recv_sem=recv_sem.at[0, iz],
            device_id=line[step - 1],
            device_id_type=MESH,
        )
        copy.start()
        origin = lax.rem(iz + nz - step, nz)
        incoming = pltpu.make_async_remote_copy(
            src_ref=row_ref,
            dst_ref=first.at[origin],
            send_sem=send_sem.at[0, step],
            recv_sem=recv_sem.at[0, origin],
            device_id=line[step - 1],
            device_id_type=MESH,
        )
        waits.append((copy, incoming))
    first[iz] = row_ref[...]
    for copy, incoming in waits:
        copy.wait_send()
        incoming.wait_recv()
    for z in range(nz):
        dense[z : z + 1, :] = first[z]

    mine = ix * ny + iy
    waits = []
    for n, ((dx, dy), peer) in enumerate(plane):
        copy = pltpu.make_async_remote_copy(
            src_ref=dense,
            dst_ref=out_ref.at[ix, iy],
            send_sem=send_sem.at[1, n],
            recv_sem=recv_sem.at[1, mine],
            device_id=peer,
            device_id_type=MESH,
        )
        copy.start()
        ox = lax.rem(ix + nx - dx, nx)
        oy = lax.rem(iy + ny - dy, ny)
        incoming = pltpu.make_async_remote_copy(
            src_ref=dense,
            dst_ref=out_ref.at[ox, oy],
            send_sem=send_sem.at[1, n],
            recv_sem=recv_sem.at[1, ox * ny + oy],
            device_id=peer,
            device_id_type=MESH,
        )
        waits.append((copy, incoming))
    out_ref[ix, iy] = dense[...]
    for copy, incoming in waits:
        copy.wait_send()
        incoming.wait_recv()


def gather_kernel(sizes, row_ref, out_ref, first, dense, send_sem, recv_sem):
    line, plane = gather_peers(sizes)
    barrier = pltpu.get_barrier_semaphore()
    for peer in line + [peer for _, peer in plane]:
        pl.semaphore_signal(barrier, inc=1, device_id=peer, device_id_type=MESH)
    pl.semaphore_wait(barrier, len(line) + len(plane))
    gather_stages(sizes, line, plane, row_ref, out_ref, first, dense, send_sem, recv_sem)


def gather_bottom(packed):
    sizes = tuple(lax.axis_size(axis) for axis in AXES)
    nx, ny, nz = sizes
    width = packed.size
    lanes = -(-width // 128) * 128
    row = jnp.pad(packed.reshape(1, width), ((0, 0), (0, lanes - width)))
    vmem = pl.BlockSpec(memory_space=pltpu.VMEM)
    top = max(nz, nx * ny)
    whole = pl.pallas_call(
        functools.partial(gather_kernel, sizes),
        out_shape=jax.ShapeDtypeStruct((nx, ny, nz, lanes), jnp.float32),
        in_specs=[vmem],
        out_specs=vmem,
        scratch_shapes=[
            pltpu.VMEM((nz, 1, lanes), jnp.float32),
            pltpu.VMEM((nz, lanes), jnp.float32),
            pltpu.SemaphoreType.DMA((2, top)),
            pltpu.SemaphoreType.DMA((2, top)),
        ],
        compiler_params=pltpu.CompilerParams(collective_id=64, has_side_effects=True),
    )(row)
    whole = whole[..., :width].reshape((nx, ny, nz) + packed.shape)
    whole = whole.transpose(3, 0, 4, 1, 5, 2, 6)
    return whole.reshape(
        (packed.shape[0],) + tuple(n * s for n, s in zip(sizes, packed.shape[1:]))
    )


def split_padded(padded):
    return (
        padded[:-2, 1:-1, 1:-1],
        padded[2:, 1:-1, 1:-1],
        padded[1:-1, :-2, 1:-1],
        padded[1:-1, 2:, 1:-1],
        padded[1:-1, 1:-1, :-2],
        padded[1:-1, 1:-1, 2:],
    )


def zero_pad(field):
    return split_padded(jnp.pad(field, 1))


def level_operator(beta_level, alpha_level, beta_sides, shift):
    coeffs = tuple((0.5 * (beta_level + other) for other in beta_sides))
    diagonal = shift * alpha_level
    for coeff in coeffs:
        diagonal = diagonal + coeff
    return (coeffs, diagonal)


def apply_operator(field, operator, pad_field):
    coeffs, diagonal = operator
    others = pad_field(field)
    total = coeffs[0] * others[0]
    for index in range(1, 6):
        total = total + coeffs[index] * others[index]
    return diagonal * field - total


def chebyshev(iterate, rhs_level, operator, count, lower, zero_start, pad_field):
    diagonal = operator[1]
    center = (UPPER_EIG + lower) / 2.0
    half_width = (UPPER_EIG - lower) / 2.0
    sigma_ratio = center / half_width
    rho_old = 1.0 / sigma_ratio
    if zero_start:
        remain = rhs_level
    else:
        remain = rhs_level - apply_operator(iterate, operator, pad_field)
    update = remain / diagonal / center
    iterate = iterate + update
    for sweep_index in range(count - 1):
        remain = rhs_level - apply_operator(iterate, operator, pad_field)
        rho_new = 1.0 / (2.0 * sigma_ratio - rho_old)
        update = rho_new * rho_old * update + 2.0 * rho_new / half_width * (remain / diagonal)
        iterate = iterate + update
        rho_old = rho_new
    return iterate


def restrict_mean(field):
    first, second, third = field.shape
    blocks = field.reshape(first // 2, 2, second // 2, 2, third // 2, 2)
    return jnp.sum(blocks, axis=(1, 3, 5)) * 0.125


def prolong_copy(field):
    return jnp.repeat(jnp.repeat(jnp.repeat(field, 2, axis=0), 2, axis=1), 2, axis=2)


def shards(right_side, alpha_coef, beta_coef):
    smoothed, rhs_levels, betas, alphas, packed = down_chain(right_side, beta_coef, alpha_coef)
    local_shape = rhs_levels[LEVELS].shape
    index_x = lax.axis_index("gx")
    index_y = lax.axis_index("gy")
    index_z = lax.axis_index("gz")
    whole_rhs = packed[0]
    whole_beta = packed[1]
    whole_alpha = packed[2]
    bottom_operator = level_operator(
        whole_beta, whole_alpha, zero_pad(whole_beta), SHIFT_BASE * 4.0**LEVELS
    )
    whole_correction = chebyshev(
        jnp.zeros_like(whole_rhs), whole_rhs, bottom_operator, BOTTOM, BOTTOM_LOWER, True, zero_pad
    )
    starts = (index_x * local_shape[0], index_y * local_shape[1], index_z * local_shape[2])
    correction = lax.dynamic_slice(whole_correction, starts, local_shape)
    correction, residual_field = up_chain(correction, smoothed, rhs_levels, betas, alphas)
    return (correction, residual_field)


def solution(mesh):
    in_specs = (P("gx", "gy", "gz"), P("gx", "gy", "gz"), P("gx", "gy", "gz"))
    out_specs = (P("gx", "gy", "gz"), P("gx", "gy", "gz"))
    return jax.shard_map(shards, mesh=mesh, in_specs=in_specs, out_specs=out_specs, check_vma=False)
```

```python
import functools

import jax
import jax.numpy as jnp
from jax import lax
from jax.experimental import pallas as pl
from jax.experimental.pallas import tpu as pltpu
from jax.sharding import PartitionSpec as P

MESH = pl.DeviceIdType.MESH
AXES = ("gx", "gy", "gz")
SLOTS = 3

LEVELS = 3
SWEEPS = 4
BOTTOM = 12


SHIFT_BASE = 0.01
UPPER_EIG = 2.0
SMOOTH_LOWER = 0.25
BOTTOM_LOWER = 0.02


def level_kernel(cfg, *refs):
    sizes, shift, count, lower, zero_start, residual, restrict = cfg
    n_in = 3 if zero_start else 4
    b_ref, beta_ref, alpha_ref = refs[0:3]
    v0_ref = None if zero_start else refs[3]
    n_out = 1 + (1 if residual and not restrict else 0) + (3 if restrict else 0)
    outs = refs[n_in : n_in + n_out]
    fld, xh, yh, zh, zsend, coef, dbuf, send_sem, recv_sem = refs[n_in + len(outs) :]
    A, B, C = b_ref.shape
    index = [lax.axis_index(axis) for axis in AXES]
    targets = []
    for k in range(6):
        axis = k // 2
        if k % 2 == 0:
            exists = index[axis] > 0
            other = index[axis] - 1
        else:
            exists = index[axis] < sizes[axis] - 1
            other = index[axis] + 1
        device = tuple(other if a == axis else index[a] for a in range(3))
        targets.append((exists, device))

    def halo(h, slot):
        if h < 2:
            return xh.at[h, slot]
        return yh.at[h - 2, slot] if h < 4 else zh.at[h - 4, slot]

    picks = lax.broadcasted_iota(jnp.int32, (8, C), 0)
    lanes = lax.broadcasted_iota(jnp.int32, (8, C), 1)
    selector = jnp.where(
        (picks == 0) & (lanes == 0), 1.0, jnp.where((picks == 1) & (lanes == C - 1), 1.0, 0.0)
    ).astype(jnp.float32)

    barrier = pltpu.get_barrier_semaphore()
    total = jnp.int32(0)
    for exists, device in targets:

        @pl.when(exists)
        def _():
            pl.semaphore_signal(barrier, inc=1, device_id=device, device_id_type=MESH)

        total = total + exists.astype(jnp.int32)
    for h, (exists, device) in enumerate(targets):

        @pl.when(jnp.logical_not(exists))
        def _():
            for slot in range(SLOTS):
                buf = halo(h, slot)
                buf[...] = jnp.zeros(buf.shape, buf.dtype)

    if restrict:
        coarse_rows = (
            lax.broadcasted_iota(jnp.int32, (B // 2, B), 1) // 2
            == lax.broadcasted_iota(jnp.int32, (B // 2, B), 0)
        ).astype(jnp.float32)
        coarse_cols = (
            lax.broadcasted_iota(jnp.int32, (C, C // 2), 0) // 2
            == lax.broadcasted_iota(jnp.int32, (C, C // 2), 1)
        ).astype(jnp.float32)

        def restrict_into(src, dst, scale):
            for i in range(A // 2):
                pair = src[2 * i] + src[2 * i + 1]
                half = jnp.dot(
                    coarse_rows, pair, precision=lax.Precision.HIGHEST,
                    preferred_element_type=jnp.float32,
                )
                dst[i] = scale * jnp.dot(
                    half, coarse_cols, precision=lax.Precision.HIGHEST,
                    preferred_element_type=jnp.float32,
                )

        restrict_into(beta_ref, outs[2], 0.125)
        restrict_into(alpha_ref, outs[3], 0.125)
    pl.semaphore_wait(barrier, total)

    def exchange_start(src, slot):
        block = src[...].reshape(A * B, C)
        zsend[slot] = lax.dot_general(
            selector, block, (((1,), (1,)), ((), ())),
            precision=lax.Precision.HIGHEST, preferred_element_type=jnp.float32,
        )
        sources = (
            src.at[0], src.at[A - 1],
            src.at[:, 0:8, :], src.at[:, B - 8 : B, :],
            zsend.at[slot], zsend.at[slot],
        )
        waits = []
        for k, (exists, device) in enumerate(targets):
            copy = pltpu.make_async_remote_copy(
                src_ref=sources[k],
                dst_ref=halo(k ^ 1, slot),
                send_sem=send_sem.at[slot, k],
                recv_sem=recv_sem.at[slot, k ^ 1],
                device_id=device,
                device_id_type=MESH,
            )
            pl.when(exists)(copy.start)
            incoming = pltpu.make_async_remote_copy(
                src_ref=sources[k ^ 1],
                dst_ref=halo(k, slot),
                send_sem=send_sem.at[slot, k ^ 1],
                recv_sem=recv_sem.at[slot, k],
                device_id=device,
                device_id_type=MESH,
            )
            waits.append((exists, copy.wait_send))
            waits.append((exists, incoming.wait_recv))
        return waits

    def exchange_finish(waits):
        for exists, wait in waits:
            pl.when(exists)(wait)

    def exchange(src, slot):
        exchange_finish(exchange_start(src, slot))

    rows = lax.broadcasted_iota(jnp.int32, (B, C), 0)
    cols = lax.broadcasted_iota(jnp.int32, (B, C), 1)

    def z_columns(slot):
        return (jnp.transpose(zh[0, slot]), jnp.transpose(zh[1, slot]))

    def sides(src, i, slot, columns):
        here = src[i]
        lower_x = src[i - 1] if i > 0 else xh[0, slot]
        upper_x = src[i + 1] if i < A - 1 else xh[1, slot]
        lower_y = jnp.where(rows == 0, yh[0, slot, i, 7:8, :], pltpu.roll(here, 1, 0))
        upper_y = jnp.where(rows == B - 1, yh[1, slot, i, 0:1, :], pltpu.roll(here, B - 1, 0))
        lower_z = jnp.where(cols == 0, columns[0][i * B : (i + 1) * B, 1:2], pltpu.roll(here, 1, 1))
        upper_z = jnp.where(
            cols == C - 1, columns[1][i * B : (i + 1) * B, 0:1], pltpu.roll(here, C - 1, 1)
        )
        return here, (lower_x, upper_x, lower_y, upper_y, lower_z, upper_z)

    exchanges = [0]

    def next_slot():
        slot = exchanges[0] % SLOTS
        exchanges[0] += 1
        return slot

    slot = next_slot()
    if zero_start:
        exchange(beta_ref, slot)
    else:
        first_slot = next_slot()
        first_waits = exchange_start(v0_ref, first_slot)
        exchange(beta_ref, slot)
    columns = z_columns(slot)
    for i in range(A):
        here, others = sides(beta_ref, i, slot, columns)
        diagonal = shift * alpha_ref[i]
        for k in range(6):
            face = 0.5 * (here + others[k])
            coef[k, i] = face
            diagonal = diagonal + face
        coef[6, i] = diagonal

    def apply_rows(src, slot, i, columns):
        here, others = sides(src, i, slot, columns)
        acc = coef[0, i] * others[0]
        for k in range(1, 6):
            acc = acc + coef[k, i] * others[k]
        return b_ref[i] - (coef[6, i] * here - acc)

    center = (UPPER_EIG + lower) / 2.0
    half_width = (UPPER_EIG - lower) / 2.0
    sigma_ratio = center / half_width
    rho_old = 1.0 / sigma_ratio
    current = 0
    if zero_start:
        for i in range(A):
            update = b_ref[i] / coef[6, i] / center
            dbuf[i] = update
            fld[current, i] = update
    else:
        exchange_finish(first_waits)
        columns = z_columns(first_slot)
        for i in range(A):
            remain = apply_rows(v0_ref, first_slot, i, columns)
            update = remain / coef[6, i] / center
            dbuf[i] = update
            fld[current, i] = v0_ref[i] + update
    for sweep in range(count - 1):
        rho_new = 1.0 / (2.0 * sigma_ratio - rho_old)
        slot = next_slot()
        src = fld.at[current]
        exchange(src, slot)
        last = sweep == count - 2
        dst = outs[0] if last else fld.at[1 - current]
        columns = z_columns(slot)
        for i in range(A):
            remain = apply_rows(src, slot, i, columns)
            update = (rho_new * rho_old) * dbuf[i] + (2.0 * rho_new / half_width) * (
                remain / coef[6, i]
            )
            dbuf[i] = update
            dst[i] = src[i] + update
        rho_old = rho_new
        current = 1 - current
    if residual:
        slot = next_slot()
        exchange(outs[0], slot)
        remain_ref = dbuf if restrict else outs[1]
        columns = z_columns(slot)
        for i in range(A):
            remain_ref[i] = apply_rows(outs[0], slot, i, columns)
        if restrict:
            restrict_into(dbuf, outs[1], 0.5)


KERNELS = {}


def smooth(level_args, shift, count, lower, zero_start, residual, restrict=False):
    A, B, C = level_args[0].shape
    sizes = tuple(lax.axis_size(axis) for axis in AXES)
    cfg = (sizes, shift, count, lower, zero_start, residual, restrict)
    ident = KERNELS.setdefault((A, B, C) + cfg[1:], len(KERNELS))
    vmem = pl.BlockSpec(memory_space=pltpu.VMEM)
    block = jax.ShapeDtypeStruct((A, B, C), jnp.float32)
    coarse = jax.ShapeDtypeStruct((A // 2, B // 2, C // 2), jnp.float32)
    shapes = [block] + ([block] if residual and not restrict else []) + ([coarse] * 3 if restrict else [])
    n_out = len(shapes)
    return pl.pallas_call(
        functools.partial(level_kernel, cfg),
        out_shape=tuple(shapes),
        in_specs=[vmem] * len(level_args),
        out_specs=tuple([vmem] * n_out),
        scratch_shapes=[
            pltpu.VMEM((2, A, B, C), jnp.float32),
            pltpu.VMEM((2, SLOTS, B, C), jnp.float32),
            pltpu.VMEM((2, SLOTS, A, 8, C), jnp.float32),
            pltpu.VMEM((2, SLOTS, 8, A * B), jnp.float32),
            pltpu.VMEM((SLOTS, 8, A * B), jnp.float32),
            pltpu.VMEM((7, A, B, C), jnp.float32),
            pltpu.VMEM((A, B, C), jnp.float32),
            pltpu.SemaphoreType.DMA((SLOTS, 6)),
            pltpu.SemaphoreType.DMA((SLOTS, 6)),
        ],
        compiler_params=pltpu.CompilerParams(collective_id=ident, has_side_effects=True),
    )(*level_args)


def restrict_into(src, dst, scale):
    A, B, C = src.shape
    coarse_rows = (
        lax.broadcasted_iota(jnp.int32, (B // 2, B), 1) // 2
        == lax.broadcasted_iota(jnp.int32, (B // 2, B), 0)
    ).astype(jnp.float32)
    coarse_cols = (
        lax.broadcasted_iota(jnp.int32, (C, C // 2), 0) // 2
        == lax.broadcasted_iota(jnp.int32, (C, C // 2), 1)
    ).astype(jnp.float32)
    for i in range(A // 2):
        pair = src[2 * i] + src[2 * i + 1]
        half = jnp.dot(
            coarse_rows, pair, precision=lax.Precision.HIGHEST, preferred_element_type=jnp.float32
        )
        dst[i] = scale * jnp.dot(
            half, coarse_cols, precision=lax.Precision.HIGHEST, preferred_element_type=jnp.float32
        )


def neighbour_targets(sizes):
    index = [lax.axis_index(axis) for axis in AXES]
    targets = []
    for k in range(6):
        axis = k // 2
        if k % 2 == 0:
            exists = index[axis] > 0
            other = index[axis] - 1
        else:
            exists = index[axis] < sizes[axis] - 1
            other = index[axis] + 1
        device = tuple(other if a == axis else index[a] for a in range(3))
        targets.append((exists, device))
    return targets


def level_tools(shape, level, targets, bufs, send_sem, recv_sem):
    A, B, C = shape
    fld, xh, yh, zh, zsend, coef, dbuf = bufs

    def halo(h, slot):
        if h < 2:
            return xh.at[h, slot]
        return yh.at[h - 2, slot] if h < 4 else zh.at[h - 4, slot]

    picks = lax.broadcasted_iota(jnp.int32, (8, C), 0)
    lanes = lax.broadcasted_iota(jnp.int32, (8, C), 1)
    selector = jnp.where(
        (picks == 0) & (lanes == 0), 1.0, jnp.where((picks == 1) & (lanes == C - 1), 1.0, 0.0)
    ).astype(jnp.float32)
    rows = lax.broadcasted_iota(jnp.int32, (B, C), 0)
    cols = lax.broadcasted_iota(jnp.int32, (B, C), 1)

    def zero_halos():
        for h, (exists, device) in enumerate(targets):

            @pl.when(jnp.logical_not(exists))
            def _():
                for slot in range(SLOTS):
                    buf = halo(h, slot)
                    buf[...] = jnp.zeros(buf.shape, buf.dtype)

    def exchange_start(src, slot):
        block = src[...].reshape(A * B, C)
        zsend[slot] = lax.dot_general(
            selector, block, (((1,), (1,)), ((), ())),
            precision=lax.Precision.HIGHEST, preferred_element_type=jnp.float32,
        )
        sources = (
            src.at[0], src.at[A - 1],
            src.at[:, 0:8, :], src.at[:, B - 8 : B, :],
            zsend.at[slot], zsend.at[slot],
        )
        waits = []
        for k, (exists, device) in enumerate(targets):
            copy = pltpu.make_async_remote_copy(
                src_ref=sources[k],
                dst_ref=halo(k ^ 1, slot),
                send_sem=send_sem.at[level, slot, k],
                recv_sem=recv_sem.at[level, slot, k ^ 1],
                device_id=device,
                device_id_type=MESH,
            )
            pl.when(exists)(copy.start)
            incoming = pltpu.make_async_remote_copy(
                src_ref=sources[k ^ 1],
                dst_ref=halo(k, slot),
                send_sem=send_sem.at[level, slot, k ^ 1],
                recv_sem=recv_sem.at[level, slot, k],
                device_id=device,
                device_id_type=MESH,
            )
            waits.append((exists, copy.wait_send))
            waits.append((exists, incoming.wait_recv))
        return waits

    def exchange_finish(waits):
        for exists, wait in waits:
            pl.when(exists)(wait)

    def exchange(src, slot):
        exchange_finish(exchange_start(src, slot))

    def z_columns(slot):
        return (jnp.transpose(zh[0, slot]), jnp.transpose(zh[1, slot]))

    def sides(src, i, slot, columns):
        here = src[i]
        lower_x = src[i - 1] if i > 0 else xh[0, slot]
        upper_x = src[i + 1] if i < A - 1 else xh[1, slot]
        lower_y = jnp.where(rows == 0, yh[0, slot, i, 7:8, :], pltpu.roll(here, 1, 0))
        upper_y = jnp.where(rows == B - 1, yh[1, slot, i, 0:1, :], pltpu.roll(here, B - 1, 0))
        lower_z = jnp.where(cols == 0, columns[0][i * B : (i + 1) * B, 1:2], pltpu.roll(here, 1, 1))
        upper_z = jnp.where(
            cols == C - 1, columns[1][i * B : (i + 1) * B, 0:1], pltpu.roll(here, C - 1, 1)
        )
        return here, (lower_x, upper_x, lower_y, upper_y, lower_z, upper_z)

    def build_coef(beta_ref, alpha_ref, slot, shift):
        columns = z_columns(slot)
        for i in range(A):
            here, others = sides(beta_ref, i, slot, columns)
            diagonal = shift * alpha_ref[i]
            for k in range(6):
                face = 0.5 * (here + others[k])
                coef[k, i] = face
                diagonal = diagonal + face
            coef[6, i] = diagonal

    def apply_op(src, slot, i, columns):
        here, others = sides(src, i, slot, columns)
        acc = coef[0, i] * others[0]
        for k in range(1, 6):
            acc = acc + coef[k, i] * others[k]
        return coef[6, i] * here - acc

    def apply_rows(src, b_ref, slot, i, columns):
        return b_ref[i] - apply_op(src, slot, i, columns)

    def smooth_down(b_ref, v_out, next_rhs, count, lower):
        center = (UPPER_EIG + lower) / 2.0
        half_width = (UPPER_EIG - lower) / 2.0
        sigma_ratio = center / half_width
        rho_old = 1.0 / sigma_ratio
        current = 0
        for i in range(A):
            update = b_ref[i] / coef[6, i] / center
            dbuf[i] = update
            fld[current, i] = update
        slot = 0
        for sweep in range(count - 1):
            rho_new = 1.0 / (2.0 * sigma_ratio - rho_old)
            slot = (slot + 1) % SLOTS
            src = fld.at[current]
            exchange(src, slot)
            columns = z_columns(slot)
            dst = v_out if sweep == count - 2 else fld.at[1 - current]
            for i in range(A):
                remain = apply_rows(src, b_ref, slot, i, columns)
                update = (rho_new * rho_old) * dbuf[i] + (2.0 * rho_new / half_width) * (
                    remain / coef[6, i]
                )
                dbuf[i] = update
                dst[i] = src[i] + update
            rho_old = rho_new
            current = 1 - current
        slot = (slot + 1) % SLOTS
        exchange(v_out, slot)
        columns = z_columns(slot)
        for i in range(A):
            dbuf[i] = apply_rows(v_out, b_ref, slot, i, columns)
        restrict_into(dbuf, next_rhs, 0.5)

    def smooth_up(b_ref, v_out, count, lower, first_slot, first_waits, residual_out, split):
        start = fld.at[1]
        if first_waits is None:
            exchange(start, first_slot)
        else:
            exchange_finish(first_waits)
        center = (UPPER_EIG + lower) / 2.0
        half_width = (UPPER_EIG - lower) / 2.0
        sigma_ratio = center / half_width
        rho_old = 1.0 / sigma_ratio
        columns = z_columns(first_slot)
        for i in range(A):
            remain = apply_rows(start, b_ref, first_slot, i, columns)
            update = remain / coef[6, i] / center
            dbuf[i] = update
            fld[0, i] = start[i] + update
        current = 0
        slot = first_slot
        for sweep in range(count - 1):
            rho_new = 1.0 / (2.0 * sigma_ratio - rho_old)
            slot = (slot + 1) % SLOTS
            src = fld.at[current]
            exchange(src, slot)
            columns = z_columns(slot)
            dst = v_out if sweep == count - 2 else fld.at[1 - current]
            for i in range(A):
                remain = apply_rows(src, b_ref, slot, i, columns)
                update = (rho_new * rho_old) * dbuf[i] + (2.0 * rho_new / half_width) * (
                    remain / coef[6, i]
                )
                dbuf[i] = update
                dst[i] = src[i] + update
                if split is not None and sweep == count - 2:
                    split[0][i] = src[i]
                    split[1][i] = update
            rho_old = rho_new
            current = 1 - current
        if residual_out is not None:
            slot = (slot + 1) % SLOTS
            exchange(v_out, slot)
            columns = z_columns(slot)
            for i in range(A):
                residual_out[i] = apply_op(v_out, slot, i, columns)

    def prolong_start(coarse, smoothed):
        fine_rows = (
            lax.broadcasted_iota(jnp.int32, (B, B // 2), 0) // 2
            == lax.broadcasted_iota(jnp.int32, (B, B // 2), 1)
        ).astype(jnp.float32)
        fine_cols = (
            lax.broadcasted_iota(jnp.int32, (C // 2, C), 1) // 2
            == lax.broadcasted_iota(jnp.int32, (C // 2, C), 0)
        ).astype(jnp.float32)
        for i in range(A):
            half = jnp.dot(
                fine_rows, coarse[i // 2], precision=lax.Precision.HIGHEST,
                preferred_element_type=jnp.float32,
            )
            fine = jnp.dot(
                half, fine_cols, precision=lax.Precision.HIGHEST,
                preferred_element_type=jnp.float32,
            )
            fld[1, i] = smoothed[i] + fine

    return (
        zero_halos, exchange_start, exchange_finish, build_coef, smooth_down, smooth_up,
        prolong_start, fld,
    )


def up_kernel(cfg, *refs):
    sizes, shapes, shifts = cfg
    depth = len(shapes)
    coarsest = refs[0]
    level_in = [refs[1 + 4 * l : 5 + 4 * l] for l in range(depth)]
    parts_out = refs[1 + 4 * depth]
    previous_out, update_out, operator_out = (parts_out.at[n] for n in range(3))
    scratch = refs[2 + 4 * depth :]
    results = scratch[7 * depth : 8 * depth]
    send_sem, recv_sem = scratch[8 * depth], scratch[8 * depth + 1]
    targets = neighbour_targets(sizes)
    barrier = pltpu.get_barrier_semaphore()
    total = jnp.int32(0)
    for exists, device in targets:

        @pl.when(exists)
        def _():
            pl.semaphore_signal(barrier, inc=1, device_id=device, device_id_type=MESH)

        total = total + exists.astype(jnp.int32)
    tools = [
        level_tools(shapes[l], l, targets, scratch[7 * l : 7 * l + 7], send_sem, recv_sem)
        for l in range(depth)
    ]
    for tool in tools:
        tool[0]()
    top = depth - 1
    tools[top][6](coarsest, level_in[top][0])
    pl.semaphore_wait(barrier, total)
    first_waits = tools[top][1](tools[top][7].at[1], 1)
    waits = [tools[l][1](level_in[l][2], 0) for l in range(depth)]
    for l in range(depth):
        tools[l][2](waits[l])
        tools[l][3](level_in[l][2], level_in[l][3], 0, shifts[l])
    coarse = None
    for l in range(top, -1, -1):
        if l < top:
            tools[l][6](coarse, level_in[l][0])
        v_out = results[l]
        tools[l][5](
            level_in[l][1], v_out, SWEEPS, SMOOTH_LOWER, 1,
            first_waits if l == top else None, operator_out if l == 0 else None,
            (previous_out, update_out) if l == 0 else None,
        )
        coarse = v_out


def up_chain(coarsest, smoothed, rhs_levels, betas, alphas):
    sizes = tuple(lax.axis_size(axis) for axis in AXES)
    shapes = [tuple(x.shape) for x in smoothed]
    shifts = tuple(SHIFT_BASE * 4.0**l for l in range(LEVELS))
    cfg = (sizes, tuple(shapes), shifts)
    vmem = pl.BlockSpec(memory_space=pltpu.VMEM)
    args = [coarsest]
    for l in range(LEVELS):
        args += [smoothed[l], rhs_levels[l], betas[l], alphas[l]]
    scratch = []
    for s in shapes:
        scratch += level_scratch(s)
    scratch += [pltpu.VMEM(s, jnp.float32) for s in shapes]
    scratch += [
        pltpu.SemaphoreType.DMA((LEVELS, SLOTS, 6)),
        pltpu.SemaphoreType.DMA((LEVELS, SLOTS, 6)),
    ]
    fine = jax.ShapeDtypeStruct(shapes[0], jnp.float32)
    stacked = jax.ShapeDtypeStruct((3,) + shapes[0], jnp.float32)
    parts = pl.pallas_call(
        functools.partial(up_kernel, cfg),
        out_shape=stacked,
        in_specs=[vmem] * len(args),
        out_specs=vmem,
        scratch_shapes=scratch,
        compiler_params=pltpu.CompilerParams(collective_id=48, has_side_effects=True),
    )(*args)
    return pl.pallas_call(
        finish_kernel,
        out_shape=(fine, fine),
        in_specs=[vmem, vmem],
        out_specs=(vmem, vmem),
    )(parts, rhs_levels[0])


def finish_kernel(parts_ref, rhs_ref, solution_ref, residual_ref):
    solution_ref[...] = parts_ref[0] + parts_ref[1]
    residual_ref[...] = rhs_ref[...] - parts_ref[2]


def level_scratch(shape):
    A, B, C = shape
    return [
        pltpu.VMEM((2, A, B, C), jnp.float32),
        pltpu.VMEM((2, SLOTS, B, C), jnp.float32),
        pltpu.VMEM((2, SLOTS, A, 8, C), jnp.float32),
        pltpu.VMEM((2, SLOTS, 8, A * B), jnp.float32),
        pltpu.VMEM((SLOTS, 8, A * B), jnp.float32),
        pltpu.VMEM((7, A, B, C), jnp.float32),
        pltpu.VMEM((A, B, C), jnp.float32),
    ]


def down_kernel(cfg, *refs):
    sizes, shapes, shifts = cfg
    depth = len(shapes)
    b0, beta0, alpha0 = refs[0:3]
    outs = refs[3 : 3 + 4 * depth]
    iterates = outs[0:depth]
    rhs = [b0] + list(outs[depth : 2 * depth])
    betas = [beta0] + list(outs[2 * depth : 3 * depth])
    alphas = [alpha0] + list(outs[3 * depth : 4 * depth])
    gathered = refs[3 + 4 * depth]
    scratch = refs[4 + 4 * depth :]
    send_sem, recv_sem = scratch[7 * depth], scratch[7 * depth + 1]
    row, first, dense, gsend, grecv = scratch[7 * depth + 2 :]
    targets = neighbour_targets(sizes)
    line, plane = gather_peers(sizes)
    barrier = pltpu.get_barrier_semaphore()
    for peer in line + [peer for _, peer in plane]:
        pl.semaphore_signal(barrier, inc=1, device_id=peer, device_id_type=MESH)
    total = len(line) + len(plane)
    tools = [
        level_tools(shapes[l], l, targets, scratch[7 * l : 7 * l + 7], send_sem, recv_sem)
        for l in range(depth)
    ]
    for tool in tools:
        tool[0]()
    for l in range(depth):
        restrict_into(betas[l], betas[l + 1], 0.125)
        restrict_into(alphas[l], alphas[l + 1], 0.125)
    pl.semaphore_wait(barrier, total)
    waits = [tools[l][1](betas[l], 0) for l in range(depth)]
    for l in range(depth):
        tools[l][2](waits[l])
        tools[l][3](betas[l], alphas[l], 0, shifts[l])
    for l in range(depth):
        tools[l][4](rhs[l], iterates[l], rhs[l + 1], SWEEPS, SMOOTH_LOWER)
    lanes = row.shape[1]
    packed = jnp.zeros((1, lanes), jnp.float32)
    offset = 0
    for part in (rhs[depth], betas[depth], alphas[depth]):
        pa, pb, pc = part.shape
        for x in range(pa):
            for j in range(pb):
                pick = (lax.broadcasted_iota(jnp.int32, (1, pb), 1) == j).astype(jnp.float32)
                line_values = jnp.dot(
                    pick, part[x], precision=lax.Precision.HIGHEST,
                    preferred_element_type=jnp.float32,
                )
                place = (
                    lax.broadcasted_iota(jnp.int32, (pc, lanes), 0) + offset
                    == lax.broadcasted_iota(jnp.int32, (pc, lanes), 1)
                ).astype(jnp.float32)
                packed = packed + jnp.dot(
                    line_values, place, precision=lax.Precision.HIGHEST,
                    preferred_element_type=jnp.float32,
                )
                offset += pc
    row[...] = packed
    gather_stages(sizes, line, plane, row, gathered, first, dense, gsend, grecv)


def down_chain(right_side, beta_coef, alpha_coef):
    sizes = tuple(lax.axis_size(axis) for axis in AXES)
    shapes = [tuple(n >> l for n in right_side.shape) for l in range(LEVELS + 1)]
    shifts = tuple(SHIFT_BASE * 4.0**l for l in range(LEVELS))
    cfg = (sizes, tuple(shapes[:LEVELS]), shifts)
    vmem = pl.BlockSpec(memory_space=pltpu.VMEM)
    out_shapes = [jax.ShapeDtypeStruct(s, jnp.float32) for s in shapes[:LEVELS]]
    out_shapes += [jax.ShapeDtypeStruct(s, jnp.float32) for s in shapes[1:]] * 3
    scratch = []
    for s in shapes[:LEVELS]:
        scratch += level_scratch(s)
    nx, ny, nz = sizes
    width = 3 * shapes[LEVELS][0] * shapes[LEVELS][1] * shapes[LEVELS][2]
    lanes = -(-width // 128) * 128
    top = max(nz, nx * ny)
    out_shapes.append(jax.ShapeDtypeStruct((nx, ny, nz, lanes), jnp.float32))
    scratch += [
        pltpu.SemaphoreType.DMA((LEVELS, SLOTS, 6)),
        pltpu.SemaphoreType.DMA((LEVELS, SLOTS, 6)),
        pltpu.VMEM((1, lanes), jnp.float32),
        pltpu.VMEM((nz, 1, lanes), jnp.float32),
        pltpu.VMEM((nz, lanes), jnp.float32),
        pltpu.SemaphoreType.DMA((2, top)),
        pltpu.SemaphoreType.DMA((2, top)),
    ]
    outs = pl.pallas_call(
        functools.partial(down_kernel, cfg),
        out_shape=tuple(out_shapes),
        in_specs=[vmem] * 3,
        out_specs=tuple([vmem] * len(out_shapes)),
        scratch_shapes=scratch,
        compiler_params=pltpu.CompilerParams(collective_id=32, has_side_effects=True),
    )(right_side, beta_coef, alpha_coef)
    iterates = list(outs[0:LEVELS])
    rhs_levels = [right_side] + list(outs[LEVELS : 2 * LEVELS])
    betas = [beta_coef] + list(outs[2 * LEVELS : 3 * LEVELS])
    alphas = [alpha_coef] + list(outs[3 * LEVELS : 4 * LEVELS])
    whole = outs[4 * LEVELS][..., :width].reshape((nx, ny, nz, 3) + shapes[LEVELS])
    whole = whole.transpose(3, 0, 4, 1, 5, 2, 6)
    whole = whole.reshape((3,) + tuple(n * s for n, s in zip(sizes, shapes[LEVELS])))
    return iterates, rhs_levels, betas, alphas, whole


def gather_peers(sizes):
    index = [lax.axis_index(axis) for axis in AXES]
    nx, ny, nz = sizes
    ix, iy, iz = index
    line = [(ix, iy, lax.rem(iz + step, nz)) for step in range(1, nz)]
    plane = []
    for dx in range(nx):
        for dy in range(ny):
            if dx or dy:
                plane.append(((dx, dy), (lax.rem(ix + dx, nx), lax.rem(iy + dy, ny), iz)))

    return line, plane


def gather_stages(sizes, line, plane, row_ref, out_ref, first, dense, send_sem, recv_sem):
    index = [lax.axis_index(axis) for axis in AXES]
    nx, ny, nz = sizes
    ix, iy, iz = index
    waits = []
    for step in range(1, nz):
        copy = pltpu.make_async_remote_copy(
            src_ref=row_ref,
            dst_ref=first.at[iz],
            send_sem=send_sem.at[0, step],
            recv_sem=recv_sem.at[0, iz],
            device_id=line[step - 1],
            device_id_type=MESH,
        )
        copy.start()
        origin = lax.rem(iz + nz - step, nz)
        incoming = pltpu.make_async_remote_copy(
            src_ref=row_ref,
            dst_ref=first.at[origin],
            send_sem=send_sem.at[0, step],
            recv_sem=recv_sem.at[0, origin],
            device_id=line[step - 1],
            device_id_type=MESH,
        )
        waits.append((copy, incoming))
    first[iz] = row_ref[...]
    for copy, incoming in waits:
        copy.wait_send()
        incoming.wait_recv()
    for z in range(nz):
        dense[z : z + 1, :] = first[z]

    mine = ix * ny + iy
    waits = []
    for n, ((dx, dy), peer) in enumerate(plane):
        copy = pltpu.make_async_remote_copy(
            src_ref=dense,
            dst_ref=out_ref.at[ix, iy],
            send_sem=send_sem.at[1, n],
            recv_sem=recv_sem.at[1, mine],
            device_id=peer,
            device_id_type=MESH,
        )
        copy.start()
        ox = lax.rem(ix + nx - dx, nx)
        oy = lax.rem(iy + ny - dy, ny)
        incoming = pltpu.make_async_remote_copy(
            src_ref=dense,
            dst_ref=out_ref.at[ox, oy],
            send_sem=send_sem.at[1, n],
            recv_sem=recv_sem.at[1, ox * ny + oy],
            device_id=peer,
            device_id_type=MESH,
        )
        waits.append((copy, incoming))
    out_ref[ix, iy] = dense[...]
    for copy, incoming in waits:
        copy.wait_send()
        incoming.wait_recv()


def gather_kernel(sizes, row_ref, out_ref, first, dense, send_sem, recv_sem):
    line, plane = gather_peers(sizes)
    barrier = pltpu.get_barrier_semaphore()
    for peer in line + [peer for _, peer in plane]:
        pl.semaphore_signal(barrier, inc=1, device_id=peer, device_id_type=MESH)
    pl.semaphore_wait(barrier, len(line) + len(plane))
    gather_stages(sizes, line, plane, row_ref, out_ref, first, dense, send_sem, recv_sem)


def gather_bottom(packed):
    sizes = tuple(lax.axis_size(axis) for axis in AXES)
    nx, ny, nz = sizes
    width = packed.size
    lanes = -(-width // 128) * 128
    row = jnp.pad(packed.reshape(1, width), ((0, 0), (0, lanes - width)))
    vmem = pl.BlockSpec(memory_space=pltpu.VMEM)
    top = max(nz, nx * ny)
    whole = pl.pallas_call(
        functools.partial(gather_kernel, sizes),
        out_shape=jax.ShapeDtypeStruct((nx, ny, nz, lanes), jnp.float32),
        in_specs=[vmem],
        out_specs=vmem,
        scratch_shapes=[
            pltpu.VMEM((nz, 1, lanes), jnp.float32),
            pltpu.VMEM((nz, lanes), jnp.float32),
            pltpu.SemaphoreType.DMA((2, top)),
            pltpu.SemaphoreType.DMA((2, top)),
        ],
        compiler_params=pltpu.CompilerParams(collective_id=64, has_side_effects=True),
    )(row)
    whole = whole[..., :width].reshape((nx, ny, nz) + packed.shape)
    whole = whole.transpose(3, 0, 4, 1, 5, 2, 6)
    return whole.reshape(
        (packed.shape[0],) + tuple(n * s for n, s in zip(sizes, packed.shape[1:]))
    )


def split_padded(padded):
    return (
        padded[:-2, 1:-1, 1:-1],
        padded[2:, 1:-1, 1:-1],
        padded[1:-1, :-2, 1:-1],
        padded[1:-1, 2:, 1:-1],
        padded[1:-1, 1:-1, :-2],
        padded[1:-1, 1:-1, 2:],
    )


def zero_pad(field):
    return split_padded(jnp.pad(field, 1))


def level_operator(beta_level, alpha_level, beta_sides, shift):
    coeffs = tuple((0.5 * (beta_level + other) for other in beta_sides))
    diagonal = shift * alpha_level
    for coeff in coeffs:
        diagonal = diagonal + coeff
    return (coeffs, diagonal)


def apply_operator(field, operator, pad_field):
    coeffs, diagonal = operator
    others = pad_field(field)
    total = coeffs[0] * others[0]
    for index in range(1, 6):
        total = total + coeffs[index] * others[index]
    return diagonal * field - total


def chebyshev(iterate, rhs_level, operator, count, lower, zero_start, pad_field):
    diagonal = operator[1]
    center = (UPPER_EIG + lower) / 2.0
    half_width = (UPPER_EIG - lower) / 2.0
    sigma_ratio = center / half_width
    rho_old = 1.0 / sigma_ratio
    if zero_start:
        remain = rhs_level
    else:
        remain = rhs_level - apply_operator(iterate, operator, pad_field)
    update = remain / diagonal / center
    iterate = iterate + update
    for sweep_index in range(count - 1):
        remain = rhs_level - apply_operator(iterate, operator, pad_field)
        rho_new = 1.0 / (2.0 * sigma_ratio - rho_old)
        update = rho_new * rho_old * update + 2.0 * rho_new / half_width * (remain / diagonal)
        iterate = iterate + update
        rho_old = rho_new
    return iterate


def restrict_mean(field):
    first, second, third = field.shape
    blocks = field.reshape(first // 2, 2, second // 2, 2, third // 2, 2)
    return jnp.sum(blocks, axis=(1, 3, 5)) * 0.125


def prolong_copy(field):
    return jnp.repeat(jnp.repeat(jnp.repeat(field, 2, axis=0), 2, axis=1), 2, axis=2)


def shards(right_side, alpha_coef, beta_coef):
    smoothed, rhs_levels, betas, alphas, packed = down_chain(right_side, beta_coef, alpha_coef)
    local_shape = rhs_levels[LEVELS].shape
    index_x = lax.axis_index("gx")
    index_y = lax.axis_index("gy")
    index_z = lax.axis_index("gz")
    whole_rhs = packed[0]
    whole_beta = packed[1]
    whole_alpha = packed[2]
    bottom_operator = level_operator(
        whole_beta, whole_alpha, zero_pad(whole_beta), SHIFT_BASE * 4.0**LEVELS
    )
    whole_correction = chebyshev(
        jnp.zeros_like(whole_rhs), whole_rhs, bottom_operator, BOTTOM, BOTTOM_LOWER, True, zero_pad
    )
    starts = (index_x * local_shape[0], index_y * local_shape[1], index_z * local_shape[2])
    correction = lax.dynamic_slice(whole_correction, starts, local_shape)
    correction, residual_field = up_chain(correction, smoothed, rhs_levels, betas, alphas)
    return (correction, residual_field)


def solution(mesh):
    in_specs = (P("gx", "gy", "gz"), P("gx", "gy", "gz"), P("gx", "gy", "gz"))
    out_specs = (P("gx", "gy", "gz"), P("gx", "gy", "gz"))
    return jax.shard_map(shards, mesh=mesh, in_specs=in_specs, out_specs=out_specs, check_vma=False)
```

```python
import functools

import jax
import jax.numpy as jnp
from jax import lax
from jax.experimental import pallas as pl
from jax.experimental.pallas import tpu as pltpu
from jax.sharding import PartitionSpec as P

MESH = pl.DeviceIdType.MESH
AXES = ("gx", "gy", "gz")
SLOTS = 3

LEVELS = 3
SWEEPS = 4
BOTTOM = 12


SHIFT_BASE = 0.01
UPPER_EIG = 2.0
SMOOTH_LOWER = 0.25
BOTTOM_LOWER = 0.02


def level_kernel(cfg, *refs):
    sizes, shift, count, lower, zero_start, residual, restrict = cfg
    n_in = 3 if zero_start else 4
    b_ref, beta_ref, alpha_ref = refs[0:3]
    v0_ref = None if zero_start else refs[3]
    n_out = 1 + (1 if residual and not restrict else 0) + (3 if restrict else 0)
    outs = refs[n_in : n_in + n_out]
    fld, xh, yh, zh, zsend, coef, dbuf, send_sem, recv_sem = refs[n_in + len(outs) :]
    A, B, C = b_ref.shape
    index = [lax.axis_index(axis) for axis in AXES]
    targets = []
    for k in range(6):
        axis = k // 2
        if k % 2 == 0:
            exists = index[axis] > 0
            other = index[axis] - 1
        else:
            exists = index[axis] < sizes[axis] - 1
            other = index[axis] + 1
        device = tuple(other if a == axis else index[a] for a in range(3))
        targets.append((exists, device))

    def halo(h, slot):
        if h < 2:
            return xh.at[h, slot]
        return yh.at[h - 2, slot] if h < 4 else zh.at[h - 4, slot]

    picks = lax.broadcasted_iota(jnp.int32, (8, C), 0)
    lanes = lax.broadcasted_iota(jnp.int32, (8, C), 1)
    selector = jnp.where(
        (picks == 0) & (lanes == 0), 1.0, jnp.where((picks == 1) & (lanes == C - 1), 1.0, 0.0)
    ).astype(jnp.float32)

    barrier = pltpu.get_barrier_semaphore()
    total = jnp.int32(0)
    for exists, device in targets:

        @pl.when(exists)
        def _():
            pl.semaphore_signal(barrier, inc=1, device_id=device, device_id_type=MESH)

        total = total + exists.astype(jnp.int32)
    for h, (exists, device) in enumerate(targets):

        @pl.when(jnp.logical_not(exists))
        def _():
            for slot in range(SLOTS):
                buf = halo(h, slot)
                buf[...] = jnp.zeros(buf.shape, buf.dtype)

    if restrict:
        coarse_rows = (
            lax.broadcasted_iota(jnp.int32, (B // 2, B), 1) // 2
            == lax.broadcasted_iota(jnp.int32, (B // 2, B), 0)
        ).astype(jnp.float32)
        coarse_cols = (
            lax.broadcasted_iota(jnp.int32, (C, C // 2), 0) // 2
            == lax.broadcasted_iota(jnp.int32, (C, C // 2), 1)
        ).astype(jnp.float32)

        def restrict_into(src, dst, scale):
            for i in range(A // 2):
                pair = src[2 * i] + src[2 * i + 1]
                half = jnp.dot(
                    coarse_rows, pair, precision=lax.Precision.HIGHEST,
                    preferred_element_type=jnp.float32,
                )
                dst[i] = scale * jnp.dot(
                    half, coarse_cols, precision=lax.Precision.HIGHEST,
                    preferred_element_type=jnp.float32,
                )

        restrict_into(beta_ref, outs[2], 0.125)
        restrict_into(alpha_ref, outs[3], 0.125)
    pl.semaphore_wait(barrier, total)

    def exchange_start(src, slot):
        block = src[...].reshape(A * B, C)
        zsend[slot] = lax.dot_general(
            selector, block, (((1,), (1,)), ((), ())),
            precision=lax.Precision.HIGHEST, preferred_element_type=jnp.float32,
        )
        sources = (
            src.at[0], src.at[A - 1],
            src.at[:, 0:8, :], src.at[:, B - 8 : B, :],
            zsend.at[slot], zsend.at[slot],
        )
        waits = []
        for k, (exists, device) in enumerate(targets):
            copy = pltpu.make_async_remote_copy(
                src_ref=sources[k],
                dst_ref=halo(k ^ 1, slot),
                send_sem=send_sem.at[slot, k],
                recv_sem=recv_sem.at[slot, k ^ 1],
                device_id=device,
                device_id_type=MESH,
            )
            pl.when(exists)(copy.start)
            incoming = pltpu.make_async_remote_copy(
                src_ref=sources[k ^ 1],
                dst_ref=halo(k, slot),
                send_sem=send_sem.at[slot, k ^ 1],
                recv_sem=recv_sem.at[slot, k],
                device_id=device,
                device_id_type=MESH,
            )
            waits.append((exists, copy.wait_send))
            waits.append((exists, incoming.wait_recv))
        return waits

    def exchange_finish(waits):
        for exists, wait in waits:
            pl.when(exists)(wait)

    def exchange(src, slot):
        exchange_finish(exchange_start(src, slot))

    rows = lax.broadcasted_iota(jnp.int32, (B, C), 0)
    cols = lax.broadcasted_iota(jnp.int32, (B, C), 1)

    def z_columns(slot):
        return (jnp.transpose(zh[0, slot]), jnp.transpose(zh[1, slot]))

    def sides(src, i, slot, columns):
        here = src[i]
        lower_x = src[i - 1] if i > 0 else xh[0, slot]
        upper_x = src[i + 1] if i < A - 1 else xh[1, slot]
        lower_y = jnp.where(rows == 0, yh[0, slot, i, 7:8, :], pltpu.roll(here, 1, 0))
        upper_y = jnp.where(rows == B - 1, yh[1, slot, i, 0:1, :], pltpu.roll(here, B - 1, 0))
        lower_z = jnp.where(cols == 0, columns[0][i * B : (i + 1) * B, 1:2], pltpu.roll(here, 1, 1))
        upper_z = jnp.where(
            cols == C - 1, columns[1][i * B : (i + 1) * B, 0:1], pltpu.roll(here, C - 1, 1)
        )
        return here, (lower_x, upper_x, lower_y, upper_y, lower_z, upper_z)

    exchanges = [0]

    def next_slot():
        slot = exchanges[0] % SLOTS
        exchanges[0] += 1
        return slot

    slot = next_slot()
    if zero_start:
        exchange(beta_ref, slot)
    else:
        first_slot = next_slot()
        first_waits = exchange_start(v0_ref, first_slot)
        exchange(beta_ref, slot)
    columns = z_columns(slot)
    for i in range(A):
        here, others = sides(beta_ref, i, slot, columns)
        diagonal = shift * alpha_ref[i]
        for k in range(6):
            face = 0.5 * (here + others[k])
            coef[k, i] = face
            diagonal = diagonal + face
        coef[6, i] = diagonal

    def apply_rows(src, slot, i, columns):
        here, others = sides(src, i, slot, columns)
        acc = coef[0, i] * others[0]
        for k in range(1, 6):
            acc = acc + coef[k, i] * others[k]
        return b_ref[i] - (coef[6, i] * here - acc)

    center = (UPPER_EIG + lower) / 2.0
    half_width = (UPPER_EIG - lower) / 2.0
    sigma_ratio = center / half_width
    rho_old = 1.0 / sigma_ratio
    current = 0
    if zero_start:
        for i in range(A):
            update = b_ref[i] / coef[6, i] / center
            dbuf[i] = update
            fld[current, i] = update
    else:
        exchange_finish(first_waits)
        columns = z_columns(first_slot)
        for i in range(A):
            remain = apply_rows(v0_ref, first_slot, i, columns)
            update = remain / coef[6, i] / center
            dbuf[i] = update
            fld[current, i] = v0_ref[i] + update
    for sweep in range(count - 1):
        rho_new = 1.0 / (2.0 * sigma_ratio - rho_old)
        slot = next_slot()
        src = fld.at[current]
        exchange(src, slot)
        last = sweep == count - 2
        dst = outs[0] if last else fld.at[1 - current]
        columns = z_columns(slot)
        for i in range(A):
            remain = apply_rows(src, slot, i, columns)
            update = (rho_new * rho_old) * dbuf[i] + (2.0 * rho_new / half_width) * (
                remain / coef[6, i]
            )
            dbuf[i] = update
            dst[i] = src[i] + update
        rho_old = rho_new
        current = 1 - current
    if residual:
        slot = next_slot()
        exchange(outs[0], slot)
        remain_ref = dbuf if restrict else outs[1]
        columns = z_columns(slot)
        for i in range(A):
            remain_ref[i] = apply_rows(outs[0], slot, i, columns)
        if restrict:
            restrict_into(dbuf, outs[1], 0.5)


KERNELS = {}


def smooth(level_args, shift, count, lower, zero_start, residual, restrict=False):
    A, B, C = level_args[0].shape
    sizes = tuple(lax.axis_size(axis) for axis in AXES)
    cfg = (sizes, shift, count, lower, zero_start, residual, restrict)
    ident = KERNELS.setdefault((A, B, C) + cfg[1:], len(KERNELS))
    vmem = pl.BlockSpec(memory_space=pltpu.VMEM)
    block = jax.ShapeDtypeStruct((A, B, C), jnp.float32)
    coarse = jax.ShapeDtypeStruct((A // 2, B // 2, C // 2), jnp.float32)
    shapes = [block] + ([block] if residual and not restrict else []) + ([coarse] * 3 if restrict else [])
    n_out = len(shapes)
    return pl.pallas_call(
        functools.partial(level_kernel, cfg),
        out_shape=tuple(shapes),
        in_specs=[vmem] * len(level_args),
        out_specs=tuple([vmem] * n_out),
        scratch_shapes=[
            pltpu.VMEM((2, A, B, C), jnp.float32),
            pltpu.VMEM((2, SLOTS, B, C), jnp.float32),
            pltpu.VMEM((2, SLOTS, A, 8, C), jnp.float32),
            pltpu.VMEM((2, SLOTS, 8, A * B), jnp.float32),
            pltpu.VMEM((SLOTS, 8, A * B), jnp.float32),
            pltpu.VMEM((7, A, B, C), jnp.float32),
            pltpu.VMEM((A, B, C), jnp.float32),
            pltpu.SemaphoreType.DMA((SLOTS, 6)),
            pltpu.SemaphoreType.DMA((SLOTS, 6)),
        ],
        compiler_params=pltpu.CompilerParams(collective_id=ident, has_side_effects=True),
    )(*level_args)


def restrict_into(src, dst, scale):
    A, B, C = src.shape
    coarse_rows = (
        lax.broadcasted_iota(jnp.int32, (B // 2, B), 1) // 2
        == lax.broadcasted_iota(jnp.int32, (B // 2, B), 0)
    ).astype(jnp.float32)
    coarse_cols = (
        lax.broadcasted_iota(jnp.int32, (C, C // 2), 0) // 2
        == lax.broadcasted_iota(jnp.int32, (C, C // 2), 1)
    ).astype(jnp.float32)
    for i in range(A // 2):
        pair = src[2 * i] + src[2 * i + 1]
        half = jnp.dot(
            coarse_rows, pair, precision=lax.Precision.HIGHEST, preferred_element_type=jnp.float32
        )
        dst[i] = scale * jnp.dot(
            half, coarse_cols, precision=lax.Precision.HIGHEST, preferred_element_type=jnp.float32
        )


def neighbour_targets(sizes):
    index = [lax.axis_index(axis) for axis in AXES]
    targets = []
    for k in range(6):
        axis = k // 2
        if k % 2 == 0:
            exists = index[axis] > 0
            other = index[axis] - 1
        else:
            exists = index[axis] < sizes[axis] - 1
            other = index[axis] + 1
        device = tuple(other if a == axis else index[a] for a in range(3))
        targets.append((exists, device))
    return targets


def level_tools(shape, level, targets, bufs, send_sem, recv_sem):
    A, B, C = shape
    fld, xh, yh, zh, zsend, coef, dbuf = bufs

    def halo(h, slot):
        if h < 2:
            return xh.at[h, slot]
        return yh.at[h - 2, slot] if h < 4 else zh.at[h - 4, slot]

    picks = lax.broadcasted_iota(jnp.int32, (8, C), 0)
    lanes = lax.broadcasted_iota(jnp.int32, (8, C), 1)
    selector = jnp.where(
        (picks == 0) & (lanes == 0), 1.0, jnp.where((picks == 1) & (lanes == C - 1), 1.0, 0.0)
    ).astype(jnp.float32)
    rows = lax.broadcasted_iota(jnp.int32, (B, C), 0)
    cols = lax.broadcasted_iota(jnp.int32, (B, C), 1)

    def zero_halos():
        for h, (exists, device) in enumerate(targets):

            @pl.when(jnp.logical_not(exists))
            def _():
                for slot in range(SLOTS):
                    buf = halo(h, slot)
                    buf[...] = jnp.zeros(buf.shape, buf.dtype)

    def exchange_start(src, slot):
        block = src[...].reshape(A * B, C)
        zsend[slot] = lax.dot_general(
            selector, block, (((1,), (1,)), ((), ())),
            precision=lax.Precision.HIGHEST, preferred_element_type=jnp.float32,
        )
        sources = (
            src.at[0], src.at[A - 1],
            src.at[:, 0:8, :], src.at[:, B - 8 : B, :],
            zsend.at[slot], zsend.at[slot],
        )
        waits = []
        for k, (exists, device) in enumerate(targets):
            copy = pltpu.make_async_remote_copy(
                src_ref=sources[k],
                dst_ref=halo(k ^ 1, slot),
                send_sem=send_sem.at[level, slot, k],
                recv_sem=recv_sem.at[level, slot, k ^ 1],
                device_id=device,
                device_id_type=MESH,
            )
            pl.when(exists)(copy.start)
            incoming = pltpu.make_async_remote_copy(
                src_ref=sources[k ^ 1],
                dst_ref=halo(k, slot),
                send_sem=send_sem.at[level, slot, k ^ 1],
                recv_sem=recv_sem.at[level, slot, k],
                device_id=device,
                device_id_type=MESH,
            )
            waits.append((exists, copy.wait_send))
            waits.append((exists, incoming.wait_recv))
        return waits

    def exchange_finish(waits):
        for exists, wait in waits:
            pl.when(exists)(wait)

    def exchange(src, slot):
        exchange_finish(exchange_start(src, slot))

    def z_columns(slot):
        return (jnp.transpose(zh[0, slot]), jnp.transpose(zh[1, slot]))

    def sides(src, i, slot, columns):
        here = src[i]
        lower_x = src[i - 1] if i > 0 else xh[0, slot]
        upper_x = src[i + 1] if i < A - 1 else xh[1, slot]
        lower_y = jnp.where(rows == 0, yh[0, slot, i, 7:8, :], pltpu.roll(here, 1, 0))
        upper_y = jnp.where(rows == B - 1, yh[1, slot, i, 0:1, :], pltpu.roll(here, B - 1, 0))
        lower_z = jnp.where(cols == 0, columns[0][i * B : (i + 1) * B, 1:2], pltpu.roll(here, 1, 1))
        upper_z = jnp.where(
            cols == C - 1, columns[1][i * B : (i + 1) * B, 0:1], pltpu.roll(here, C - 1, 1)
        )
        return here, (lower_x, upper_x, lower_y, upper_y, lower_z, upper_z)

    def build_coef(beta_ref, alpha_ref, slot, shift):
        columns = z_columns(slot)
        for i in range(A):
            here, others = sides(beta_ref, i, slot, columns)
            diagonal = shift * alpha_ref[i]
            for k in range(6):
                face = 0.5 * (here + others[k])
                coef[k, i] = face
                diagonal = diagonal + face
            coef[6, i] = diagonal

    def apply_op(src, slot, i, columns):
        here, others = sides(src, i, slot, columns)
        acc = coef[0, i] * others[0]
        for k in range(1, 6):
            acc = acc + coef[k, i] * others[k]
        return coef[6, i] * here - acc

    def apply_rows(src, b_ref, slot, i, columns):
        return b_ref[i] - apply_op(src, slot, i, columns)

    def smooth_down(b_ref, v_out, next_rhs, count, lower):
        center = (UPPER_EIG + lower) / 2.0
        half_width = (UPPER_EIG - lower) / 2.0
        sigma_ratio = center / half_width
        rho_old = 1.0 / sigma_ratio
        current = 0
        for i in range(A):
            update = b_ref[i] / coef[6, i] / center
            dbuf[i] = update
            fld[current, i] = update
        slot = 0
        for sweep in range(count - 1):
            rho_new = 1.0 / (2.0 * sigma_ratio - rho_old)
            slot = (slot + 1) % SLOTS
            src = fld.at[current]
            exchange(src, slot)
            columns = z_columns(slot)
            dst = v_out if sweep == count - 2 else fld.at[1 - current]
            for i in range(A):
                remain = apply_rows(src, b_ref, slot, i, columns)
                update = (rho_new * rho_old) * dbuf[i] + (2.0 * rho_new / half_width) * (
                    remain / coef[6, i]
                )
                dbuf[i] = update
                dst[i] = src[i] + update
            rho_old = rho_new
            current = 1 - current
        slot = (slot + 1) % SLOTS
        exchange(v_out, slot)
        columns = z_columns(slot)
        for i in range(A):
            dbuf[i] = apply_rows(v_out, b_ref, slot, i, columns)
        restrict_into(dbuf, next_rhs, 0.5)

    def smooth_up(b_ref, v_out, count, lower, first_slot, first_waits, residual_out, split):
        start = fld.at[1]
        if first_waits is None:
            exchange(start, first_slot)
        else:
            exchange_finish(first_waits)
        center = (UPPER_EIG + lower) / 2.0
        half_width = (UPPER_EIG - lower) / 2.0
        sigma_ratio = center / half_width
        rho_old = 1.0 / sigma_ratio
        columns = z_columns(first_slot)
        for i in range(A):
            remain = apply_rows(start, b_ref, first_slot, i, columns)
            update = remain / coef[6, i] / center
            dbuf[i] = update
            fld[0, i] = start[i] + update
        current = 0
        slot = first_slot
        for sweep in range(count - 1):
            rho_new = 1.0 / (2.0 * sigma_ratio - rho_old)
            slot = (slot + 1) % SLOTS
            src = fld.at[current]
            exchange(src, slot)
            columns = z_columns(slot)
            dst = v_out if sweep == count - 2 else fld.at[1 - current]
            for i in range(A):
                remain = apply_rows(src, b_ref, slot, i, columns)
                update = (rho_new * rho_old) * dbuf[i] + (2.0 * rho_new / half_width) * (
                    remain / coef[6, i]
                )
                dbuf[i] = update
                dst[i] = src[i] + update
                if split is not None and sweep == count - 2:
                    split[0][i] = src[i]
                    split[1][i] = update
            rho_old = rho_new
            current = 1 - current
        if residual_out is not None:
            slot = (slot + 1) % SLOTS
            exchange(v_out, slot)
            columns = z_columns(slot)
            for i in range(A):
                residual_out[i] = apply_op(v_out, slot, i, columns)

    def prolong_start(coarse, smoothed):
        fine_rows = (
            lax.broadcasted_iota(jnp.int32, (B, B // 2), 0) // 2
            == lax.broadcasted_iota(jnp.int32, (B, B // 2), 1)
        ).astype(jnp.float32)
        fine_cols = (
            lax.broadcasted_iota(jnp.int32, (C // 2, C), 1) // 2
            == lax.broadcasted_iota(jnp.int32, (C // 2, C), 0)
        ).astype(jnp.float32)
        for i in range(A):
            half = jnp.dot(
                fine_rows, coarse[i // 2], precision=lax.Precision.HIGHEST,
                preferred_element_type=jnp.float32,
            )
            fine = jnp.dot(
                half, fine_cols, precision=lax.Precision.HIGHEST,
                preferred_element_type=jnp.float32,
            )
            fld[1, i] = smoothed[i] + fine

    return (
        zero_halos, exchange_start, exchange_finish, build_coef, smooth_down, smooth_up,
        prolong_start, fld,
    )


def up_kernel(cfg, *refs):
    sizes, shapes, shifts = cfg
    depth = len(shapes)
    coarsest = refs[0]
    level_in = [refs[1 + 4 * l : 5 + 4 * l] for l in range(depth)]
    parts_out = refs[1 + 4 * depth]
    previous_out, update_out, operator_out = (parts_out.at[n] for n in range(3))
    scratch = refs[2 + 4 * depth :]
    results = scratch[7 * depth : 8 * depth]
    send_sem, recv_sem = scratch[8 * depth], scratch[8 * depth + 1]
    targets = neighbour_targets(sizes)
    barrier = pltpu.get_barrier_semaphore()
    total = jnp.int32(0)
    for exists, device in targets:

        @pl.when(exists)
        def _():
            pl.semaphore_signal(barrier, inc=1, device_id=device, device_id_type=MESH)

        total = total + exists.astype(jnp.int32)
    tools = [
        level_tools(shapes[l], l, targets, scratch[7 * l : 7 * l + 7], send_sem, recv_sem)
        for l in range(depth)
    ]
    for tool in tools:
        tool[0]()
    top = depth - 1
    tools[top][6](coarsest, level_in[top][0])
    pl.semaphore_wait(barrier, total)
    first_waits = tools[top][1](tools[top][7].at[1], 1)
    waits = [tools[l][1](level_in[l][2], 0) for l in range(depth)]
    for l in range(depth):
        tools[l][2](waits[l])
        tools[l][3](level_in[l][2], level_in[l][3], 0, shifts[l])
    coarse = None
    for l in range(top, -1, -1):
        if l < top:
            tools[l][6](coarse, level_in[l][0])
        v_out = results[l]
        tools[l][5](
            level_in[l][1], v_out, SWEEPS, SMOOTH_LOWER, 1,
            first_waits if l == top else None, operator_out if l == 0 else None,
            (previous_out, update_out) if l == 0 else None,
        )
        coarse = v_out


def up_chain(coarsest, smoothed, rhs_levels, betas, alphas):
    sizes = tuple(lax.axis_size(axis) for axis in AXES)
    shapes = [tuple(x.shape) for x in smoothed]
    shifts = tuple(SHIFT_BASE * 4.0**l for l in range(LEVELS))
    cfg = (sizes, tuple(shapes), shifts)
    vmem = pl.BlockSpec(memory_space=pltpu.VMEM)
    args = [coarsest]
    for l in range(LEVELS):
        args += [smoothed[l], rhs_levels[l], betas[l], alphas[l]]
    scratch = []
    for s in shapes:
        scratch += level_scratch(s)
    scratch += [pltpu.VMEM(s, jnp.float32) for s in shapes]
    scratch += [
        pltpu.SemaphoreType.DMA((LEVELS, SLOTS, 6)),
        pltpu.SemaphoreType.DMA((LEVELS, SLOTS, 6)),
    ]
    fine = jax.ShapeDtypeStruct(shapes[0], jnp.float32)
    stacked = jax.ShapeDtypeStruct((3,) + shapes[0], jnp.float32)
    parts = pl.pallas_call(
        functools.partial(up_kernel, cfg),
        out_shape=stacked,
        in_specs=[vmem] * len(args),
        out_specs=vmem,
        scratch_shapes=scratch,
        compiler_params=pltpu.CompilerParams(collective_id=48, has_side_effects=True),
    )(*args)
    return pl.pallas_call(
        finish_kernel,
        out_shape=(fine, fine),
        in_specs=[vmem, vmem],
        out_specs=(vmem, vmem),
    )(parts, rhs_levels[0])


def finish_kernel(parts_ref, rhs_ref, solution_ref, residual_ref):
    solution_ref[...] = parts_ref[0] + parts_ref[1]
    residual_ref[...] = rhs_ref[...] - parts_ref[2]


def level_scratch(shape):
    A, B, C = shape
    return [
        pltpu.VMEM((2, A, B, C), jnp.float32),
        pltpu.VMEM((2, SLOTS, B, C), jnp.float32),
        pltpu.VMEM((2, SLOTS, A, 8, C), jnp.float32),
        pltpu.VMEM((2, SLOTS, 8, A * B), jnp.float32),
        pltpu.VMEM((SLOTS, 8, A * B), jnp.float32),
        pltpu.VMEM((7, A, B, C), jnp.float32),
        pltpu.VMEM((A, B, C), jnp.float32),
    ]


def down_kernel(cfg, *refs):
    sizes, shapes, shifts = cfg
    depth = len(shapes)
    b0, beta0, alpha0 = refs[0:3]
    outs = refs[3 : 3 + 4 * depth]
    iterates = outs[0:depth]
    rhs = [b0] + list(outs[depth : 2 * depth])
    betas = [beta0] + list(outs[2 * depth : 3 * depth])
    alphas = [alpha0] + list(outs[3 * depth : 4 * depth])
    gathered = refs[3 + 4 * depth]
    scratch = refs[4 + 4 * depth :]
    send_sem, recv_sem = scratch[7 * depth], scratch[7 * depth + 1]
    row, first, dense, grouped, gsend, grecv = scratch[7 * depth + 2 :]
    targets = neighbour_targets(sizes)
    line, plane = gather_peers(sizes)
    barrier = pltpu.get_barrier_semaphore()
    for peer in line + [peer for _, peer in plane]:
        pl.semaphore_signal(barrier, inc=1, device_id=peer, device_id_type=MESH)
    total = len(line) + len(plane)
    tools = [
        level_tools(shapes[l], l, targets, scratch[7 * l : 7 * l + 7], send_sem, recv_sem)
        for l in range(depth)
    ]
    for tool in tools:
        tool[0]()
    for l in range(depth):
        restrict_into(betas[l], betas[l + 1], 0.125)
        restrict_into(alphas[l], alphas[l + 1], 0.125)
    pl.semaphore_wait(barrier, total)
    waits = [tools[l][1](betas[l], 0) for l in range(depth)]
    for l in range(depth):
        tools[l][2](waits[l])
        tools[l][3](betas[l], alphas[l], 0, shifts[l])
    for l in range(depth):
        tools[l][4](rhs[l], iterates[l], rhs[l + 1], SWEEPS, SMOOTH_LOWER)
    lanes = row.shape[1]
    packed = jnp.zeros((1, lanes), jnp.float32)
    offset = 0
    for part in (rhs[depth], betas[depth], alphas[depth]):
        pa, pb, pc = part.shape
        for x in range(pa):
            for j in range(pb):
                pick = (lax.broadcasted_iota(jnp.int32, (1, pb), 1) == j).astype(jnp.float32)
                line_values = jnp.dot(
                    pick, part[x], precision=lax.Precision.HIGHEST,
                    preferred_element_type=jnp.float32,
                )
                place = (
                    lax.broadcasted_iota(jnp.int32, (pc, lanes), 0) + offset
                    == lax.broadcasted_iota(jnp.int32, (pc, lanes), 1)
                ).astype(jnp.float32)
                packed = packed + jnp.dot(
                    line_values, place, precision=lax.Precision.HIGHEST,
                    preferred_element_type=jnp.float32,
                )
                offset += pc
    row[...] = packed
    gather_stages(
        sizes, line, plane, row, gathered, first, dense, gsend, grecv, rhs[depth].shape, grouped
    )


def down_chain(right_side, beta_coef, alpha_coef):
    sizes = tuple(lax.axis_size(axis) for axis in AXES)
    shapes = [tuple(n >> l for n in right_side.shape) for l in range(LEVELS + 1)]
    shifts = tuple(SHIFT_BASE * 4.0**l for l in range(LEVELS))
    cfg = (sizes, tuple(shapes[:LEVELS]), shifts)
    vmem = pl.BlockSpec(memory_space=pltpu.VMEM)
    out_shapes = [jax.ShapeDtypeStruct(s, jnp.float32) for s in shapes[:LEVELS]]
    out_shapes += [jax.ShapeDtypeStruct(s, jnp.float32) for s in shapes[1:]] * 3
    scratch = []
    for s in shapes[:LEVELS]:
        scratch += level_scratch(s)
    nx, ny, nz = sizes
    width = 3 * shapes[LEVELS][0] * shapes[LEVELS][1] * shapes[LEVELS][2]
    lanes = -(-width // 128) * 128
    top = max(nz, nx * ny)
    a3, b3, c3 = shapes[LEVELS]
    count = 3 * a3 * b3
    height = -(-count // 8) * 8
    out_shapes.append(jax.ShapeDtypeStruct((nx, ny, height, nz * c3), jnp.float32))
    scratch += [
        pltpu.SemaphoreType.DMA((LEVELS, SLOTS, 6)),
        pltpu.SemaphoreType.DMA((LEVELS, SLOTS, 6)),
        pltpu.VMEM((1, lanes), jnp.float32),
        pltpu.VMEM((nz, 1, lanes), jnp.float32),
        pltpu.VMEM((nz, lanes), jnp.float32),
        pltpu.VMEM((height, nz * c3), jnp.float32),
        pltpu.SemaphoreType.DMA((2, top)),
        pltpu.SemaphoreType.DMA((2, top)),
    ]
    outs = pl.pallas_call(
        functools.partial(down_kernel, cfg),
        out_shape=tuple(out_shapes),
        in_specs=[vmem] * 3,
        out_specs=tuple([vmem] * len(out_shapes)),
        scratch_shapes=scratch,
        compiler_params=pltpu.CompilerParams(collective_id=32, has_side_effects=True),
    )(right_side, beta_coef, alpha_coef)
    iterates = list(outs[0:LEVELS])
    rhs_levels = [right_side] + list(outs[LEVELS : 2 * LEVELS])
    betas = [beta_coef] + list(outs[2 * LEVELS : 3 * LEVELS])
    alphas = [alpha_coef] + list(outs[3 * LEVELS : 4 * LEVELS])
    whole = outs[4 * LEVELS][:, :, :count].reshape((nx, ny, 3, a3, b3, nz * c3))
    whole = whole.transpose(2, 0, 3, 1, 4, 5)
    whole = whole.reshape((3,) + tuple(n * s for n, s in zip(sizes, shapes[LEVELS])))
    return iterates, rhs_levels, betas, alphas, whole


def gather_peers(sizes):
    index = [lax.axis_index(axis) for axis in AXES]
    nx, ny, nz = sizes
    ix, iy, iz = index
    line = [(ix, iy, lax.rem(iz + step, nz)) for step in range(1, nz)]
    plane = []
    for dx in range(nx):
        for dy in range(ny):
            if dx or dy:
                plane.append(((dx, dy), (lax.rem(ix + dx, nx), lax.rem(iy + dy, ny), iz)))

    return line, plane


def gather_stages(sizes, line, plane, row_ref, out_ref, first, dense, send_sem, recv_sem, block, grouped):
    index = [lax.axis_index(axis) for axis in AXES]
    nx, ny, nz = sizes
    ix, iy, iz = index
    waits = []
    for step in range(1, nz):
        copy = pltpu.make_async_remote_copy(
            src_ref=row_ref,
            dst_ref=first.at[iz],
            send_sem=send_sem.at[0, step],
            recv_sem=recv_sem.at[0, iz],
            device_id=line[step - 1],
            device_id_type=MESH,
        )
        copy.start()
        origin = lax.rem(iz + nz - step, nz)
        incoming = pltpu.make_async_remote_copy(
            src_ref=row_ref,
            dst_ref=first.at[origin],
            send_sem=send_sem.at[0, step],
            recv_sem=recv_sem.at[0, origin],
            device_id=line[step - 1],
            device_id_type=MESH,
        )
        waits.append((copy, incoming))
    first[iz] = row_ref[...]
    for copy, incoming in waits:
        copy.wait_send()
        incoming.wait_recv()
    for z in range(nz):
        dense[z : z + 1, :] = first[z]
    pa, pb, pc = block
    count = 3 * pa * pb
    height, lanes = grouped.shape
    flipped = jnp.transpose(dense[...])
    regrouped = jnp.zeros((height, lanes), jnp.float32)
    for k in range(pc):
        pick = (
            lax.broadcasted_iota(jnp.int32, (height, dense.shape[1]), 0) * pc + k
            == lax.broadcasted_iota(jnp.int32, (height, dense.shape[1]), 1)
        ) & (lax.broadcasted_iota(jnp.int32, (height, dense.shape[1]), 0) < count)
        spread = (
            lax.broadcasted_iota(jnp.int32, (nz, lanes), 0) * pc + k
            == lax.broadcasted_iota(jnp.int32, (nz, lanes), 1)
        )
        chosen = jnp.dot(
            pick.astype(jnp.float32), flipped, precision=lax.Precision.HIGHEST,
            preferred_element_type=jnp.float32,
        )
        regrouped = regrouped + jnp.dot(
            chosen, spread.astype(jnp.float32), precision=lax.Precision.HIGHEST,
            preferred_element_type=jnp.float32,
        )
    grouped[...] = regrouped

    mine = ix * ny + iy
    waits = []
    for n, ((dx, dy), peer) in enumerate(plane):
        copy = pltpu.make_async_remote_copy(
            src_ref=grouped,
            dst_ref=out_ref.at[ix, iy],
            send_sem=send_sem.at[1, n],
            recv_sem=recv_sem.at[1, mine],
            device_id=peer,
            device_id_type=MESH,
        )
        copy.start()
        ox = lax.rem(ix + nx - dx, nx)
        oy = lax.rem(iy + ny - dy, ny)
        incoming = pltpu.make_async_remote_copy(
            src_ref=grouped,
            dst_ref=out_ref.at[ox, oy],
            send_sem=send_sem.at[1, n],
            recv_sem=recv_sem.at[1, ox * ny + oy],
            device_id=peer,
            device_id_type=MESH,
        )
        waits.append((copy, incoming))
    out_ref[ix, iy] = grouped[...]
    for copy, incoming in waits:
        copy.wait_send()
        incoming.wait_recv()


def gather_kernel(sizes, row_ref, out_ref, first, dense, send_sem, recv_sem):
    line, plane = gather_peers(sizes)
    barrier = pltpu.get_barrier_semaphore()
    for peer in line + [peer for _, peer in plane]:
        pl.semaphore_signal(barrier, inc=1, device_id=peer, device_id_type=MESH)
    pl.semaphore_wait(barrier, len(line) + len(plane))
    gather_stages(sizes, line, plane, row_ref, out_ref, first, dense, send_sem, recv_sem)


def gather_bottom(packed):
    sizes = tuple(lax.axis_size(axis) for axis in AXES)
    nx, ny, nz = sizes
    width = packed.size
    lanes = -(-width // 128) * 128
    row = jnp.pad(packed.reshape(1, width), ((0, 0), (0, lanes - width)))
    vmem = pl.BlockSpec(memory_space=pltpu.VMEM)
    top = max(nz, nx * ny)
    whole = pl.pallas_call(
        functools.partial(gather_kernel, sizes),
        out_shape=jax.ShapeDtypeStruct((nx, ny, nz, lanes), jnp.float32),
        in_specs=[vmem],
        out_specs=vmem,
        scratch_shapes=[
            pltpu.VMEM((nz, 1, lanes), jnp.float32),
            pltpu.VMEM((nz, lanes), jnp.float32),
            pltpu.SemaphoreType.DMA((2, top)),
            pltpu.SemaphoreType.DMA((2, top)),
        ],
        compiler_params=pltpu.CompilerParams(collective_id=64, has_side_effects=True),
    )(row)
    whole = whole[..., :width].reshape((nx, ny, nz) + packed.shape)
    whole = whole.transpose(3, 0, 4, 1, 5, 2, 6)
    return whole.reshape(
        (packed.shape[0],) + tuple(n * s for n, s in zip(sizes, packed.shape[1:]))
    )


def split_padded(padded):
    return (
        padded[:-2, 1:-1, 1:-1],
        padded[2:, 1:-1, 1:-1],
        padded[1:-1, :-2, 1:-1],
        padded[1:-1, 2:, 1:-1],
        padded[1:-1, 1:-1, :-2],
        padded[1:-1, 1:-1, 2:],
    )


def zero_pad(field):
    return split_padded(jnp.pad(field, 1))


def level_operator(beta_level, alpha_level, beta_sides, shift):
    coeffs = tuple((0.5 * (beta_level + other) for other in beta_sides))
    diagonal = shift * alpha_level
    for coeff in coeffs:
        diagonal = diagonal + coeff
    return (coeffs, diagonal)


def apply_operator(field, operator, pad_field):
    coeffs, diagonal = operator
    others = pad_field(field)
    total = coeffs[0] * others[0]
    for index in range(1, 6):
        total = total + coeffs[index] * others[index]
    return diagonal * field - total


def chebyshev(iterate, rhs_level, operator, count, lower, zero_start, pad_field):
    diagonal = operator[1]
    center = (UPPER_EIG + lower) / 2.0
    half_width = (UPPER_EIG - lower) / 2.0
    sigma_ratio = center / half_width
    rho_old = 1.0 / sigma_ratio
    if zero_start:
        remain = rhs_level
    else:
        remain = rhs_level - apply_operator(iterate, operator, pad_field)
    update = remain / diagonal / center
    iterate = iterate + update
    for sweep_index in range(count - 1):
        remain = rhs_level - apply_operator(iterate, operator, pad_field)
        rho_new = 1.0 / (2.0 * sigma_ratio - rho_old)
        update = rho_new * rho_old * update + 2.0 * rho_new / half_width * (remain / diagonal)
        iterate = iterate + update
        rho_old = rho_new
    return iterate


def restrict_mean(field):
    first, second, third = field.shape
    blocks = field.reshape(first // 2, 2, second // 2, 2, third // 2, 2)
    return jnp.sum(blocks, axis=(1, 3, 5)) * 0.125


def prolong_copy(field):
    return jnp.repeat(jnp.repeat(jnp.repeat(field, 2, axis=0), 2, axis=1), 2, axis=2)


def shards(right_side, alpha_coef, beta_coef):
    smoothed, rhs_levels, betas, alphas, packed = down_chain(right_side, beta_coef, alpha_coef)
    local_shape = rhs_levels[LEVELS].shape
    index_x = lax.axis_index("gx")
    index_y = lax.axis_index("gy")
    index_z = lax.axis_index("gz")
    whole_rhs = packed[0]
    whole_beta = packed[1]
    whole_alpha = packed[2]
    bottom_operator = level_operator(
        whole_beta, whole_alpha, zero_pad(whole_beta), SHIFT_BASE * 4.0**LEVELS
    )
    whole_correction = chebyshev(
        jnp.zeros_like(whole_rhs), whole_rhs, bottom_operator, BOTTOM, BOTTOM_LOWER, True, zero_pad
    )
    starts = (index_x * local_shape[0], index_y * local_shape[1], index_z * local_shape[2])
    correction = lax.dynamic_slice(whole_correction, starts, local_shape)
    correction, residual_field = up_chain(correction, smoothed, rhs_levels, betas, alphas)
    return (correction, residual_field)


def solution(mesh):
    in_specs = (P("gx", "gy", "gz"), P("gx", "gy", "gz"), P("gx", "gy", "gz"))
    out_specs = (P("gx", "gy", "gz"), P("gx", "gy", "gz"))
    return jax.shard_map(shards, mesh=mesh, in_specs=in_specs, out_specs=out_specs, check_vma=False)
```

```python
import functools

import jax
import jax.numpy as jnp
from jax import lax
from jax.experimental import pallas as pl
from jax.experimental.pallas import tpu as pltpu
from jax.sharding import PartitionSpec as P

MESH = pl.DeviceIdType.MESH
AXES = ("gx", "gy", "gz")
SLOTS = 3

LEVELS = 3
SWEEPS = 4
BOTTOM = 12


SHIFT_BASE = 0.01
UPPER_EIG = 2.0
SMOOTH_LOWER = 0.25
BOTTOM_LOWER = 0.02


def level_kernel(cfg, *refs):
    sizes, shift, count, lower, zero_start, residual, restrict = cfg
    n_in = 3 if zero_start else 4
    b_ref, beta_ref, alpha_ref = refs[0:3]
    v0_ref = None if zero_start else refs[3]
    n_out = 1 + (1 if residual and not restrict else 0) + (3 if restrict else 0)
    outs = refs[n_in : n_in + n_out]
    fld, xh, yh, zh, zsend, coef, dbuf, send_sem, recv_sem = refs[n_in + len(outs) :]
    A, B, C = b_ref.shape
    index = [lax.axis_index(axis) for axis in AXES]
    targets = []
    for k in range(6):
        axis = k // 2
        if k % 2 == 0:
            exists = index[axis] > 0
            other = index[axis] - 1
        else:
            exists = index[axis] < sizes[axis] - 1
            other = index[axis] + 1
        device = tuple(other if a == axis else index[a] for a in range(3))
        targets.append((exists, device))

    def halo(h, slot):
        if h < 2:
            return xh.at[h, slot]
        return yh.at[h - 2, slot] if h < 4 else zh.at[h - 4, slot]

    picks = lax.broadcasted_iota(jnp.int32, (8, C), 0)
    lanes = lax.broadcasted_iota(jnp.int32, (8, C), 1)
    selector = jnp.where(
        (picks == 0) & (lanes == 0), 1.0, jnp.where((picks == 1) & (lanes == C - 1), 1.0, 0.0)
    ).astype(jnp.float32)

    barrier = pltpu.get_barrier_semaphore()
    total = jnp.int32(0)
    for exists, device in targets:

        @pl.when(exists)
        def _():
            pl.semaphore_signal(barrier, inc=1, device_id=device, device_id_type=MESH)

        total = total + exists.astype(jnp.int32)
    for h, (exists, device) in enumerate(targets):

        @pl.when(jnp.logical_not(exists))
        def _():
            for slot in range(SLOTS):
                buf = halo(h, slot)
                buf[...] = jnp.zeros(buf.shape, buf.dtype)

    if restrict:
        coarse_rows = (
            lax.broadcasted_iota(jnp.int32, (B // 2, B), 1) // 2
            == lax.broadcasted_iota(jnp.int32, (B // 2, B), 0)
        ).astype(jnp.float32)
        coarse_cols = (
            lax.broadcasted_iota(jnp.int32, (C, C // 2), 0) // 2
            == lax.broadcasted_iota(jnp.int32, (C, C // 2), 1)
        ).astype(jnp.float32)

        def restrict_into(src, dst, scale):
            for i in range(A // 2):
                pair = src[2 * i] + src[2 * i + 1]
                half = jnp.dot(
                    coarse_rows, pair, precision=lax.Precision.HIGHEST,
                    preferred_element_type=jnp.float32,
                )
                dst[i] = scale * jnp.dot(
                    half, coarse_cols, precision=lax.Precision.HIGHEST,
                    preferred_element_type=jnp.float32,
                )

        restrict_into(beta_ref, outs[2], 0.125)
        restrict_into(alpha_ref, outs[3], 0.125)
    pl.semaphore_wait(barrier, total)

    def exchange_start(src, slot):
        block = src[...].reshape(A * B, C)
        zsend[slot] = lax.dot_general(
            selector, block, (((1,), (1,)), ((), ())),
            precision=lax.Precision.HIGHEST, preferred_element_type=jnp.float32,
        )
        sources = (
            src.at[0], src.at[A - 1],
            src.at[:, 0:8, :], src.at[:, B - 8 : B, :],
            zsend.at[slot], zsend.at[slot],
        )
        waits = []
        for k, (exists, device) in enumerate(targets):
            copy = pltpu.make_async_remote_copy(
                src_ref=sources[k],
                dst_ref=halo(k ^ 1, slot),
                send_sem=send_sem.at[slot, k],
                recv_sem=recv_sem.at[slot, k ^ 1],
                device_id=device,
                device_id_type=MESH,
            )
            pl.when(exists)(copy.start)
            incoming = pltpu.make_async_remote_copy(
                src_ref=sources[k ^ 1],
                dst_ref=halo(k, slot),
                send_sem=send_sem.at[slot, k ^ 1],
                recv_sem=recv_sem.at[slot, k],
                device_id=device,
                device_id_type=MESH,
            )
            waits.append((exists, copy.wait_send))
            waits.append((exists, incoming.wait_recv))
        return waits

    def exchange_finish(waits):
        for exists, wait in waits:
            pl.when(exists)(wait)

    def exchange(src, slot):
        exchange_finish(exchange_start(src, slot))

    rows = lax.broadcasted_iota(jnp.int32, (B, C), 0)
    cols = lax.broadcasted_iota(jnp.int32, (B, C), 1)

    def z_columns(slot):
        return (jnp.transpose(zh[0, slot]), jnp.transpose(zh[1, slot]))

    def sides(src, i, slot, columns):
        here = src[i]
        lower_x = src[i - 1] if i > 0 else xh[0, slot]
        upper_x = src[i + 1] if i < A - 1 else xh[1, slot]
        lower_y = jnp.where(rows == 0, yh[0, slot, i, 7:8, :], pltpu.roll(here, 1, 0))
        upper_y = jnp.where(rows == B - 1, yh[1, slot, i, 0:1, :], pltpu.roll(here, B - 1, 0))
        lower_z = jnp.where(cols == 0, columns[0][i * B : (i + 1) * B, 1:2], pltpu.roll(here, 1, 1))
        upper_z = jnp.where(
            cols == C - 1, columns[1][i * B : (i + 1) * B, 0:1], pltpu.roll(here, C - 1, 1)
        )
        return here, (lower_x, upper_x, lower_y, upper_y, lower_z, upper_z)

    exchanges = [0]

    def next_slot():
        slot = exchanges[0] % SLOTS
        exchanges[0] += 1
        return slot

    slot = next_slot()
    if zero_start:
        exchange(beta_ref, slot)
    else:
        first_slot = next_slot()
        first_waits = exchange_start(v0_ref, first_slot)
        exchange(beta_ref, slot)
    columns = z_columns(slot)
    for i in range(A):
        here, others = sides(beta_ref, i, slot, columns)
        diagonal = shift * alpha_ref[i]
        for k in range(6):
            face = 0.5 * (here + others[k])
            coef[k, i] = face
            diagonal = diagonal + face
        coef[6, i] = diagonal

    def apply_rows(src, slot, i, columns):
        here, others = sides(src, i, slot, columns)
        acc = coef[0, i] * others[0]
        for k in range(1, 6):
            acc = acc + coef[k, i] * others[k]
        return b_ref[i] - (coef[6, i] * here - acc)

    center = (UPPER_EIG + lower) / 2.0
    half_width = (UPPER_EIG - lower) / 2.0
    sigma_ratio = center / half_width
    rho_old = 1.0 / sigma_ratio
    current = 0
    if zero_start:
        for i in range(A):
            update = b_ref[i] / coef[6, i] / center
            dbuf[i] = update
            fld[current, i] = update
    else:
        exchange_finish(first_waits)
        columns = z_columns(first_slot)
        for i in range(A):
            remain = apply_rows(v0_ref, first_slot, i, columns)
            update = remain / coef[6, i] / center
            dbuf[i] = update
            fld[current, i] = v0_ref[i] + update
    for sweep in range(count - 1):
        rho_new = 1.0 / (2.0 * sigma_ratio - rho_old)
        slot = next_slot()
        src = fld.at[current]
        exchange(src, slot)
        last = sweep == count - 2
        dst = outs[0] if last else fld.at[1 - current]
        columns = z_columns(slot)
        for i in range(A):
            remain = apply_rows(src, slot, i, columns)
            update = (rho_new * rho_old) * dbuf[i] + (2.0 * rho_new / half_width) * (
                remain / coef[6, i]
            )
            dbuf[i] = update
            dst[i] = src[i] + update
        rho_old = rho_new
        current = 1 - current
    if residual:
        slot = next_slot()
        exchange(outs[0], slot)
        remain_ref = dbuf if restrict else outs[1]
        columns = z_columns(slot)
        for i in range(A):
            remain_ref[i] = apply_rows(outs[0], slot, i, columns)
        if restrict:
            restrict_into(dbuf, outs[1], 0.5)


KERNELS = {}


def smooth(level_args, shift, count, lower, zero_start, residual, restrict=False):
    A, B, C = level_args[0].shape
    sizes = tuple(lax.axis_size(axis) for axis in AXES)
    cfg = (sizes, shift, count, lower, zero_start, residual, restrict)
    ident = KERNELS.setdefault((A, B, C) + cfg[1:], len(KERNELS))
    vmem = pl.BlockSpec(memory_space=pltpu.VMEM)
    block = jax.ShapeDtypeStruct((A, B, C), jnp.float32)
    coarse = jax.ShapeDtypeStruct((A // 2, B // 2, C // 2), jnp.float32)
    shapes = [block] + ([block] if residual and not restrict else []) + ([coarse] * 3 if restrict else [])
    n_out = len(shapes)
    return pl.pallas_call(
        functools.partial(level_kernel, cfg),
        out_shape=tuple(shapes),
        in_specs=[vmem] * len(level_args),
        out_specs=tuple([vmem] * n_out),
        scratch_shapes=[
            pltpu.VMEM((2, A, B, C), jnp.float32),
            pltpu.VMEM((2, SLOTS, B, C), jnp.float32),
            pltpu.VMEM((2, SLOTS, A, 8, C), jnp.float32),
            pltpu.VMEM((2, SLOTS, 8, A * B), jnp.float32),
            pltpu.VMEM((SLOTS, 8, A * B), jnp.float32),
            pltpu.VMEM((7, A, B, C), jnp.float32),
            pltpu.VMEM((A, B, C), jnp.float32),
            pltpu.SemaphoreType.DMA((SLOTS, 6)),
            pltpu.SemaphoreType.DMA((SLOTS, 6)),
        ],
        compiler_params=pltpu.CompilerParams(collective_id=ident, has_side_effects=True),
    )(*level_args)


def restrict_into(src, dst, scale):
    A, B, C = src.shape
    coarse_rows = (
        lax.broadcasted_iota(jnp.int32, (B // 2, B), 1) // 2
        == lax.broadcasted_iota(jnp.int32, (B // 2, B), 0)
    ).astype(jnp.float32)
    coarse_cols = (
        lax.broadcasted_iota(jnp.int32, (C, C // 2), 0) // 2
        == lax.broadcasted_iota(jnp.int32, (C, C // 2), 1)
    ).astype(jnp.float32)
    for i in range(A // 2):
        pair = src[2 * i] + src[2 * i + 1]
        half = jnp.dot(
            coarse_rows, pair, precision=lax.Precision.HIGHEST, preferred_element_type=jnp.float32
        )
        dst[i] = scale * jnp.dot(
            half, coarse_cols, precision=lax.Precision.HIGHEST, preferred_element_type=jnp.float32
        )


def neighbour_targets(sizes):
    index = [lax.axis_index(axis) for axis in AXES]
    targets = []
    for k in range(6):
        axis = k // 2
        if k % 2 == 0:
            exists = index[axis] > 0
            other = index[axis] - 1
        else:
            exists = index[axis] < sizes[axis] - 1
            other = index[axis] + 1
        device = tuple(other if a == axis else index[a] for a in range(3))
        targets.append((exists, device))
    return targets


def level_tools(shape, level, targets, bufs, send_sem, recv_sem):
    A, B, C = shape
    fld, xh, yh, zh, zsend, coef, dbuf = bufs

    def halo(h, slot):
        if h < 2:
            return xh.at[h, slot]
        return yh.at[h - 2, slot] if h < 4 else zh.at[h - 4, slot]

    picks = lax.broadcasted_iota(jnp.int32, (8, C), 0)
    lanes = lax.broadcasted_iota(jnp.int32, (8, C), 1)
    selector = jnp.where(
        (picks == 0) & (lanes == 0), 1.0, jnp.where((picks == 1) & (lanes == C - 1), 1.0, 0.0)
    ).astype(jnp.float32)
    rows = lax.broadcasted_iota(jnp.int32, (B, C), 0)
    cols = lax.broadcasted_iota(jnp.int32, (B, C), 1)

    def zero_halos():
        for h, (exists, device) in enumerate(targets):

            @pl.when(jnp.logical_not(exists))
            def _():
                for slot in range(SLOTS):
                    buf = halo(h, slot)
                    buf[...] = jnp.zeros(buf.shape, buf.dtype)

    def exchange_start(src, slot):
        block = src[...].reshape(A * B, C)
        zsend[slot] = lax.dot_general(
            selector, block, (((1,), (1,)), ((), ())),
            precision=lax.Precision.HIGHEST, preferred_element_type=jnp.float32,
        )
        sources = (
            src.at[0], src.at[A - 1],
            src.at[:, 0:8, :], src.at[:, B - 8 : B, :],
            zsend.at[slot], zsend.at[slot],
        )
        waits = []
        for k, (exists, device) in enumerate(targets):
            copy = pltpu.make_async_remote_copy(
                src_ref=sources[k],
                dst_ref=halo(k ^ 1, slot),
                send_sem=send_sem.at[level, slot, k],
                recv_sem=recv_sem.at[level, slot, k ^ 1],
                device_id=device,
                device_id_type=MESH,
            )
            pl.when(exists)(copy.start)
            incoming = pltpu.make_async_remote_copy(
                src_ref=sources[k ^ 1],
                dst_ref=halo(k, slot),
                send_sem=send_sem.at[level, slot, k ^ 1],
                recv_sem=recv_sem.at[level, slot, k],
                device_id=device,
                device_id_type=MESH,
            )
            waits.append((exists, copy.wait_send))
            waits.append((exists, incoming.wait_recv))
        return waits

    def exchange_finish(waits):
        for exists, wait in waits:
            pl.when(exists)(wait)

    def exchange(src, slot):
        exchange_finish(exchange_start(src, slot))

    def z_columns(slot):
        return (jnp.transpose(zh[0, slot]), jnp.transpose(zh[1, slot]))

    def sides(src, i, slot, columns):
        here = src[i]
        lower_x = src[i - 1] if i > 0 else xh[0, slot]
        upper_x = src[i + 1] if i < A - 1 else xh[1, slot]
        lower_y = jnp.where(rows == 0, yh[0, slot, i, 7:8, :], pltpu.roll(here, 1, 0))
        upper_y = jnp.where(rows == B - 1, yh[1, slot, i, 0:1, :], pltpu.roll(here, B - 1, 0))
        lower_z = jnp.where(cols == 0, columns[0][i * B : (i + 1) * B, 1:2], pltpu.roll(here, 1, 1))
        upper_z = jnp.where(
            cols == C - 1, columns[1][i * B : (i + 1) * B, 0:1], pltpu.roll(here, C - 1, 1)
        )
        return here, (lower_x, upper_x, lower_y, upper_y, lower_z, upper_z)

    def build_coef(beta_ref, alpha_ref, slot, shift):
        columns = z_columns(slot)
        for i in range(A):
            here, others = sides(beta_ref, i, slot, columns)
            diagonal = shift * alpha_ref[i]
            for k in range(6):
                face = 0.5 * (here + others[k])
                coef[k, i] = face
                diagonal = diagonal + face
            coef[6, i] = diagonal

    def apply_op(src, slot, i, columns):
        here, others = sides(src, i, slot, columns)
        acc = coef[0, i] * others[0]
        for k in range(1, 6):
            acc = acc + coef[k, i] * others[k]
        return coef[6, i] * here - acc

    def apply_rows(src, b_ref, slot, i, columns):
        return b_ref[i] - apply_op(src, slot, i, columns)

    def smooth_down(b_ref, v_out, next_rhs, count, lower):
        center = (UPPER_EIG + lower) / 2.0
        half_width = (UPPER_EIG - lower) / 2.0
        sigma_ratio = center / half_width
        rho_old = 1.0 / sigma_ratio
        current = 0
        for i in range(A):
            update = b_ref[i] / coef[6, i] / center
            dbuf[i] = update
            fld[current, i] = update
        slot = 0
        for sweep in range(count - 1):
            rho_new = 1.0 / (2.0 * sigma_ratio - rho_old)
            slot = (slot + 1) % SLOTS
            src = fld.at[current]
            exchange(src, slot)
            columns = z_columns(slot)
            dst = v_out if sweep == count - 2 else fld.at[1 - current]
            for i in range(A):
                remain = apply_rows(src, b_ref, slot, i, columns)
                update = (rho_new * rho_old) * dbuf[i] + (2.0 * rho_new / half_width) * (
                    remain / coef[6, i]
                )
                dbuf[i] = update
                dst[i] = src[i] + update
            rho_old = rho_new
            current = 1 - current
        slot = (slot + 1) % SLOTS
        exchange(v_out, slot)
        columns = z_columns(slot)
        for i in range(A):
            dbuf[i] = apply_rows(v_out, b_ref, slot, i, columns)
        restrict_into(dbuf, next_rhs, 0.5)

    def smooth_up(b_ref, v_out, count, lower, first_slot, first_waits, residual_out, split):
        start = fld.at[1]
        if first_waits is None:
            exchange(start, first_slot)
        else:
            exchange_finish(first_waits)
        center = (UPPER_EIG + lower) / 2.0
        half_width = (UPPER_EIG - lower) / 2.0
        sigma_ratio = center / half_width
        rho_old = 1.0 / sigma_ratio
        columns = z_columns(first_slot)
        for i in range(A):
            remain = apply_rows(start, b_ref, first_slot, i, columns)
            update = remain / coef[6, i] / center
            dbuf[i] = update
            fld[0, i] = start[i] + update
        current = 0
        slot = first_slot
        for sweep in range(count - 1):
            rho_new = 1.0 / (2.0 * sigma_ratio - rho_old)
            slot = (slot + 1) % SLOTS
            src = fld.at[current]
            exchange(src, slot)
            columns = z_columns(slot)
            dst = v_out if sweep == count - 2 else fld.at[1 - current]
            for i in range(A):
                remain = apply_rows(src, b_ref, slot, i, columns)
                update = (rho_new * rho_old) * dbuf[i] + (2.0 * rho_new / half_width) * (
                    remain / coef[6, i]
                )
                dbuf[i] = update
                dst[i] = src[i] + update
                if split is not None and sweep == count - 2:
                    split[0][i] = src[i]
                    split[1][i] = update
            rho_old = rho_new
            current = 1 - current
        if residual_out is not None:
            slot = (slot + 1) % SLOTS
            exchange(v_out, slot)
            columns = z_columns(slot)
            for i in range(A):
                residual_out[i] = apply_op(v_out, slot, i, columns)

    def prolong_start(coarse, smoothed):
        fine_rows = (
            lax.broadcasted_iota(jnp.int32, (B, B // 2), 0) // 2
            == lax.broadcasted_iota(jnp.int32, (B, B // 2), 1)
        ).astype(jnp.float32)
        fine_cols = (
            lax.broadcasted_iota(jnp.int32, (C // 2, C), 1) // 2
            == lax.broadcasted_iota(jnp.int32, (C // 2, C), 0)
        ).astype(jnp.float32)
        for i in range(A):
            half = jnp.dot(
                fine_rows, coarse[i // 2], precision=lax.Precision.HIGHEST,
                preferred_element_type=jnp.float32,
            )
            fine = jnp.dot(
                half, fine_cols, precision=lax.Precision.HIGHEST,
                preferred_element_type=jnp.float32,
            )
            fld[1, i] = smoothed[i] + fine

    return (
        zero_halos, exchange_start, exchange_finish, build_coef, smooth_down, smooth_up,
        prolong_start, fld,
    )


def up_kernel(cfg, *refs):
    sizes, shapes, shifts = cfg
    depth = len(shapes)
    coarsest = refs[0]
    level_in = [refs[1 + 4 * l : 5 + 4 * l] for l in range(depth)]
    parts_out = refs[1 + 4 * depth]
    previous_out, update_out, operator_out = (parts_out.at[n] for n in range(3))
    scratch = refs[2 + 4 * depth :]
    results = scratch[7 * depth : 8 * depth]
    send_sem, recv_sem = scratch[8 * depth], scratch[8 * depth + 1]
    targets = neighbour_targets(sizes)
    barrier = pltpu.get_barrier_semaphore()
    total = jnp.int32(0)
    for exists, device in targets:

        @pl.when(exists)
        def _():
            pl.semaphore_signal(barrier, inc=1, device_id=device, device_id_type=MESH)

        total = total + exists.astype(jnp.int32)
    tools = [
        level_tools(shapes[l], l, targets, scratch[7 * l : 7 * l + 7], send_sem, recv_sem)
        for l in range(depth)
    ]
    for tool in tools:
        tool[0]()
    top = depth - 1
    tools[top][6](coarsest, level_in[top][0])
    pl.semaphore_wait(barrier, total)
    first_waits = tools[top][1](tools[top][7].at[1], 1)
    waits = [tools[l][1](level_in[l][2], 0) for l in range(depth)]
    for l in range(depth):
        tools[l][2](waits[l])
        tools[l][3](level_in[l][2], level_in[l][3], 0, shifts[l])
    coarse = None
    for l in range(top, -1, -1):
        if l < top:
            tools[l][6](coarse, level_in[l][0])
        v_out = results[l]
        tools[l][5](
            level_in[l][1], v_out, SWEEPS, SMOOTH_LOWER, 1,
            first_waits if l == top else None, operator_out if l == 0 else None,
            (previous_out, update_out) if l == 0 else None,
        )
        coarse = v_out


def up_chain(coarsest, smoothed, rhs_levels, betas, alphas):
    sizes = tuple(lax.axis_size(axis) for axis in AXES)
    shapes = [tuple(x.shape) for x in smoothed]
    shifts = tuple(SHIFT_BASE * 4.0**l for l in range(LEVELS))
    cfg = (sizes, tuple(shapes), shifts)
    vmem = pl.BlockSpec(memory_space=pltpu.VMEM)
    args = [coarsest]
    for l in range(LEVELS):
        args += [smoothed[l], rhs_levels[l], betas[l], alphas[l]]
    scratch = []
    for s in shapes:
        scratch += level_scratch(s)
    scratch += [pltpu.VMEM(s, jnp.float32) for s in shapes]
    scratch += [
        pltpu.SemaphoreType.DMA((LEVELS, SLOTS, 6)),
        pltpu.SemaphoreType.DMA((LEVELS, SLOTS, 6)),
    ]
    fine = jax.ShapeDtypeStruct(shapes[0], jnp.float32)
    stacked = jax.ShapeDtypeStruct((3,) + shapes[0], jnp.float32)
    parts = pl.pallas_call(
        functools.partial(up_kernel, cfg),
        out_shape=stacked,
        in_specs=[vmem] * len(args),
        out_specs=vmem,
        scratch_shapes=scratch,
        compiler_params=pltpu.CompilerParams(collective_id=48, has_side_effects=True),
    )(*args)
    return pl.pallas_call(
        finish_kernel,
        out_shape=(fine, fine),
        in_specs=[vmem, vmem],
        out_specs=(vmem, vmem),
    )(parts, rhs_levels[0])


def finish_kernel(parts_ref, rhs_ref, solution_ref, residual_ref):
    solution_ref[...] = parts_ref[0] + parts_ref[1]
    residual_ref[...] = rhs_ref[...] - parts_ref[2]


def level_scratch(shape):
    A, B, C = shape
    return [
        pltpu.VMEM((2, A, B, C), jnp.float32),
        pltpu.VMEM((2, SLOTS, B, C), jnp.float32),
        pltpu.VMEM((2, SLOTS, A, 8, C), jnp.float32),
        pltpu.VMEM((2, SLOTS, 8, A * B), jnp.float32),
        pltpu.VMEM((SLOTS, 8, A * B), jnp.float32),
        pltpu.VMEM((7, A, B, C), jnp.float32),
        pltpu.VMEM((A, B, C), jnp.float32),
    ]


def down_kernel(cfg, *refs):
    sizes, shapes, shifts = cfg
    depth = len(shapes)
    b0, beta0, alpha0 = refs[0:3]
    outs = refs[3 : 3 + 4 * depth]
    iterates = outs[0:depth]
    rhs = [b0] + list(outs[depth : 2 * depth])
    betas = [beta0] + list(outs[2 * depth : 3 * depth])
    alphas = [alpha0] + list(outs[3 * depth : 4 * depth])
    gathered = refs[3 + 4 * depth]
    scratch = refs[4 + 4 * depth :]
    send_sem, recv_sem = scratch[7 * depth], scratch[7 * depth + 1]
    row, first, dense, grouped, gsend, grecv = scratch[7 * depth + 2 :]
    targets = neighbour_targets(sizes)
    line, plane = gather_peers(sizes)
    barrier = pltpu.get_barrier_semaphore()
    for peer in line + [peer for _, peer in plane]:
        pl.semaphore_signal(barrier, inc=1, device_id=peer, device_id_type=MESH)
    total = len(line) + len(plane)
    tools = [
        level_tools(shapes[l], l, targets, scratch[7 * l : 7 * l + 7], send_sem, recv_sem)
        for l in range(depth)
    ]
    for tool in tools:
        tool[0]()
    for l in range(depth):
        restrict_into(betas[l], betas[l + 1], 0.125)
        restrict_into(alphas[l], alphas[l + 1], 0.125)
    pl.semaphore_wait(barrier, total)
    waits = [tools[l][1](betas[l], 0) for l in range(depth)]
    for l in range(depth):
        tools[l][2](waits[l])
        tools[l][3](betas[l], alphas[l], 0, shifts[l])
    for l in range(depth):
        tools[l][4](rhs[l], iterates[l], rhs[l + 1], SWEEPS, SMOOTH_LOWER)
    lanes = row.shape[1]
    packed = jnp.zeros((1, lanes), jnp.float32)
    offset = 0
    for part in (rhs[depth], betas[depth], alphas[depth]):
        pa, pb, pc = part.shape
        for x in range(pa):
            for j in range(pb):
                pick = (lax.broadcasted_iota(jnp.int32, (1, pb), 1) == j).astype(jnp.float32)
                line_values = jnp.dot(
                    pick, part[x], precision=lax.Precision.HIGHEST,
                    preferred_element_type=jnp.float32,
                )
                place = (
                    lax.broadcasted_iota(jnp.int32, (pc, lanes), 0) + offset
                    == lax.broadcasted_iota(jnp.int32, (pc, lanes), 1)
                ).astype(jnp.float32)
                packed = packed + jnp.dot(
                    line_values, place, precision=lax.Precision.HIGHEST,
                    preferred_element_type=jnp.float32,
                )
                offset += pc
    row[...] = packed
    gather_stages(
        sizes, line, plane, row, gathered, first, dense, gsend, grecv, rhs[depth].shape, grouped
    )


def down_chain(right_side, beta_coef, alpha_coef):
    sizes = tuple(lax.axis_size(axis) for axis in AXES)
    shapes = [tuple(n >> l for n in right_side.shape) for l in range(LEVELS + 1)]
    shifts = tuple(SHIFT_BASE * 4.0**l for l in range(LEVELS))
    cfg = (sizes, tuple(shapes[:LEVELS]), shifts)
    vmem = pl.BlockSpec(memory_space=pltpu.VMEM)
    out_shapes = [jax.ShapeDtypeStruct(s, jnp.float32) for s in shapes[:LEVELS]]
    out_shapes += [jax.ShapeDtypeStruct(s, jnp.float32) for s in shapes[1:]] * 3
    scratch = []
    for s in shapes[:LEVELS]:
        scratch += level_scratch(s)
    nx, ny, nz = sizes
    width = 3 * shapes[LEVELS][0] * shapes[LEVELS][1] * shapes[LEVELS][2]
    lanes = -(-width // 128) * 128
    top = max(nz, nx * ny)
    a3, b3, c3 = shapes[LEVELS]
    count = 3 * a3 * b3
    height = -(-count // 8) * 8
    out_shapes.append(jax.ShapeDtypeStruct((nx, ny, height, nz * c3), jnp.float32))
    scratch += [
        pltpu.SemaphoreType.DMA((LEVELS, SLOTS, 6)),
        pltpu.SemaphoreType.DMA((LEVELS, SLOTS, 6)),
        pltpu.VMEM((1, lanes), jnp.float32),
        pltpu.VMEM((nz, 1, lanes), jnp.float32),
        pltpu.VMEM((nz, lanes), jnp.float32),
        pltpu.VMEM((height, nz * c3), jnp.float32),
        pltpu.SemaphoreType.DMA((2, top)),
        pltpu.SemaphoreType.DMA((2, top)),
    ]
    outs = pl.pallas_call(
        functools.partial(down_kernel, cfg),
        out_shape=tuple(out_shapes),
        in_specs=[vmem] * 3,
        out_specs=tuple([vmem] * len(out_shapes)),
        scratch_shapes=scratch,
        compiler_params=pltpu.CompilerParams(collective_id=32, has_side_effects=True),
    )(right_side, beta_coef, alpha_coef)
    iterates = list(outs[0:LEVELS])
    rhs_levels = [right_side] + list(outs[LEVELS : 2 * LEVELS])
    betas = [beta_coef] + list(outs[2 * LEVELS : 3 * LEVELS])
    alphas = [alpha_coef] + list(outs[3 * LEVELS : 4 * LEVELS])
    whole = outs[4 * LEVELS][:, :, :count].reshape((nx, ny, 3, a3, b3, nz * c3))
    whole = whole.transpose(2, 0, 3, 1, 4, 5)
    whole = whole.reshape((3,) + tuple(n * s for n, s in zip(sizes, shapes[LEVELS])))
    return iterates, rhs_levels, betas, alphas, whole


def gather_peers(sizes):
    index = [lax.axis_index(axis) for axis in AXES]
    nx, ny, nz = sizes
    ix, iy, iz = index
    line = [(ix, iy, lax.rem(iz + step, nz)) for step in range(1, nz)]
    plane = []
    for dx in range(nx):
        for dy in range(ny):
            if dx or dy:
                plane.append(((dx, dy), (lax.rem(ix + dx, nx), lax.rem(iy + dy, ny), iz)))

    return line, plane


def gather_stages(sizes, line, plane, row_ref, out_ref, first, dense, send_sem, recv_sem, block, grouped):
    index = [lax.axis_index(axis) for axis in AXES]
    nx, ny, nz = sizes
    ix, iy, iz = index
    waits = []
    for step in range(1, nz):
        copy = pltpu.make_async_remote_copy(
            src_ref=row_ref,
            dst_ref=first.at[iz],
            send_sem=send_sem.at[0, step],
            recv_sem=recv_sem.at[0, iz],
            device_id=line[step - 1],
            device_id_type=MESH,
        )
        copy.start()
        origin = lax.rem(iz + nz - step, nz)
        incoming = pltpu.make_async_remote_copy(
            src_ref=row_ref,
            dst_ref=first.at[origin],
            send_sem=send_sem.at[0, step],
            recv_sem=recv_sem.at[0, origin],
            device_id=line[step - 1],
            device_id_type=MESH,
        )
        waits.append((copy, incoming))
    first[iz] = row_ref[...]
    for copy, incoming in waits:
        copy.wait_send()
        incoming.wait_recv()
    for z in range(nz):
        dense[z : z + 1, :] = first[z]
    pa, pb, pc = block
    count = 3 * pa * pb
    height, lanes = grouped.shape
    width = dense.shape[1]
    owner = (
        lax.broadcasted_iota(jnp.int32, (height, width), 1) // pc
        == lax.broadcasted_iota(jnp.int32, (height, width), 0)
    ) & (lax.broadcasted_iota(jnp.int32, (height, width), 0) < count)
    regrouped = jnp.zeros((height, lanes), jnp.float32)
    for z in range(nz):
        spread = (
            lax.broadcasted_iota(jnp.int32, (width, lanes), 0) % pc + z * pc
            == lax.broadcasted_iota(jnp.int32, (width, lanes), 1)
        )
        rows_z = jnp.where(owner, jnp.broadcast_to(dense[z : z + 1, :], (height, width)), 0.0)
        regrouped = regrouped + jnp.dot(
            rows_z, spread.astype(jnp.float32), precision=lax.Precision.HIGHEST,
            preferred_element_type=jnp.float32,
        )
    grouped[...] = regrouped

    mine = ix * ny + iy
    waits = []
    for n, ((dx, dy), peer) in enumerate(plane):
        copy = pltpu.make_async_remote_copy(
            src_ref=grouped,
            dst_ref=out_ref.at[ix, iy],
            send_sem=send_sem.at[1, n],
            recv_sem=recv_sem.at[1, mine],
            device_id=peer,
            device_id_type=MESH,
        )
        copy.start()
        ox = lax.rem(ix + nx - dx, nx)
        oy = lax.rem(iy + ny - dy, ny)
        incoming = pltpu.make_async_remote_copy(
            src_ref=grouped,
            dst_ref=out_ref.at[ox, oy],
            send_sem=send_sem.at[1, n],
            recv_sem=recv_sem.at[1, ox * ny + oy],
            device_id=peer,
            device_id_type=MESH,
        )
        waits.append((copy, incoming))
    out_ref[ix, iy] = grouped[...]
    for copy, incoming in waits:
        copy.wait_send()
        incoming.wait_recv()


def gather_kernel(sizes, row_ref, out_ref, first, dense, send_sem, recv_sem):
    line, plane = gather_peers(sizes)
    barrier = pltpu.get_barrier_semaphore()
    for peer in line + [peer for _, peer in plane]:
        pl.semaphore_signal(barrier, inc=1, device_id=peer, device_id_type=MESH)
    pl.semaphore_wait(barrier, len(line) + len(plane))
    gather_stages(sizes, line, plane, row_ref, out_ref, first, dense, send_sem, recv_sem)


def gather_bottom(packed):
    sizes = tuple(lax.axis_size(axis) for axis in AXES)
    nx, ny, nz = sizes
    width = packed.size
    lanes = -(-width // 128) * 128
    row = jnp.pad(packed.reshape(1, width), ((0, 0), (0, lanes - width)))
    vmem = pl.BlockSpec(memory_space=pltpu.VMEM)
    top = max(nz, nx * ny)
    whole = pl.pallas_call(
        functools.partial(gather_kernel, sizes),
        out_shape=jax.ShapeDtypeStruct((nx, ny, nz, lanes), jnp.float32),
        in_specs=[vmem],
        out_specs=vmem,
        scratch_shapes=[
            pltpu.VMEM((nz, 1, lanes), jnp.float32),
            pltpu.VMEM((nz, lanes), jnp.float32),
            pltpu.SemaphoreType.DMA((2, top)),
            pltpu.SemaphoreType.DMA((2, top)),
        ],
        compiler_params=pltpu.CompilerParams(collective_id=64, has_side_effects=True),
    )(row)
    whole = whole[..., :width].reshape((nx, ny, nz) + packed.shape)
    whole = whole.transpose(3, 0, 4, 1, 5, 2, 6)
    return whole.reshape(
        (packed.shape[0],) + tuple(n * s for n, s in zip(sizes, packed.shape[1:]))
    )


def split_padded(padded):
    return (
        padded[:-2, 1:-1, 1:-1],
        padded[2:, 1:-1, 1:-1],
        padded[1:-1, :-2, 1:-1],
        padded[1:-1, 2:, 1:-1],
        padded[1:-1, 1:-1, :-2],
        padded[1:-1, 1:-1, 2:],
    )


def zero_pad(field):
    return split_padded(jnp.pad(field, 1))


def level_operator(beta_level, alpha_level, beta_sides, shift):
    coeffs = tuple((0.5 * (beta_level + other) for other in beta_sides))
    diagonal = shift * alpha_level
    for coeff in coeffs:
        diagonal = diagonal + coeff
    return (coeffs, diagonal)


def apply_operator(field, operator, pad_field):
    coeffs, diagonal = operator
    others = pad_field(field)
    total = coeffs[0] * others[0]
    for index in range(1, 6):
        total = total + coeffs[index] * others[index]
    return diagonal * field - total


def chebyshev(iterate, rhs_level, operator, count, lower, zero_start, pad_field):
    diagonal = operator[1]
    center = (UPPER_EIG + lower) / 2.0
    half_width = (UPPER_EIG - lower) / 2.0
    sigma_ratio = center / half_width
    rho_old = 1.0 / sigma_ratio
    if zero_start:
        remain = rhs_level
    else:
        remain = rhs_level - apply_operator(iterate, operator, pad_field)
    update = remain / diagonal / center
    iterate = iterate + update
    for sweep_index in range(count - 1):
        remain = rhs_level - apply_operator(iterate, operator, pad_field)
        rho_new = 1.0 / (2.0 * sigma_ratio - rho_old)
        update = rho_new * rho_old * update + 2.0 * rho_new / half_width * (remain / diagonal)
        iterate = iterate + update
        rho_old = rho_new
    return iterate


def restrict_mean(field):
    first, second, third = field.shape
    blocks = field.reshape(first // 2, 2, second // 2, 2, third // 2, 2)
    return jnp.sum(blocks, axis=(1, 3, 5)) * 0.125


def prolong_copy(field):
    return jnp.repeat(jnp.repeat(jnp.repeat(field, 2, axis=0), 2, axis=1), 2, axis=2)


def shards(right_side, alpha_coef, beta_coef):
    smoothed, rhs_levels, betas, alphas, packed = down_chain(right_side, beta_coef, alpha_coef)
    local_shape = rhs_levels[LEVELS].shape
    index_x = lax.axis_index("gx")
    index_y = lax.axis_index("gy")
    index_z = lax.axis_index("gz")
    whole_rhs = packed[0]
    whole_beta = packed[1]
    whole_alpha = packed[2]
    bottom_operator = level_operator(
        whole_beta, whole_alpha, zero_pad(whole_beta), SHIFT_BASE * 4.0**LEVELS
    )
    whole_correction = chebyshev(
        jnp.zeros_like(whole_rhs), whole_rhs, bottom_operator, BOTTOM, BOTTOM_LOWER, True, zero_pad
    )
    starts = (index_x * local_shape[0], index_y * local_shape[1], index_z * local_shape[2])
    correction = lax.dynamic_slice(whole_correction, starts, local_shape)
    correction, residual_field = up_chain(correction, smoothed, rhs_levels, betas, alphas)
    return (correction, residual_field)


def solution(mesh):
    in_specs = (P("gx", "gy", "gz"), P("gx", "gy", "gz"), P("gx", "gy", "gz"))
    out_specs = (P("gx", "gy", "gz"), P("gx", "gy", "gz"))
    return jax.shard_map(shards, mesh=mesh, in_specs=in_specs, out_specs=out_specs, check_vma=False)
```
